128 devices in a mesh: chan: 8 (over x, core), row: 16 (over y, z).
Axes of the slice: x: 4, y: 4, z: 4, core: 2. Of those that a mesh axis runs over, the one named last changes fastest.
Arguments:
- generator: bfloat16 [8, 2560, 2560], P('chan', 'row'), may hold values from -0.06 to 0.06, as said below
- hamiltonian: bfloat16 [8, 2560, 2560], P('chan', 'row'), may hold values from -6 to 6, as said below
- live_states: int32 [8], P('chan'), may hold values from 1 to 2560, 11520 in all
- pp_occupation: int32 [8, 2560], P('chan'), may hold values from -1 to 1
- ph_occupation: int32 [8, 2560], P('chan'), may hold values from -1 to 1
- ph_order: int32 [8, 2560], P('chan'), may hold values from 0 to 2559, as said below
- recoupling: float32 [8, 2], replicated, may hold values from 0.4 to 1
Outputs:
- transformed: float32 [8, 2560, 2560], P('chan', 'row')
The draws below stay inside these ranges and needn't reach their ends.
Inputs may be any that keep to these rules, and one draw needn't show every extreme that they name: Each generator[c] is antisymmetric. Each hamiltonian[c] is symmetric. Each ph_order[c] is a permutation of 0 to 2559, and entry r * 160 + q * 16 + s, for 0 <= q < 10, lies in [s * 160, (s + 1) * 160).
All inputs are finite; a program needn't handle non-finite values. No bound on the sum of `live_states` on one device may be relied on, other than what follows from the above.
Results may differ from the reference program's by a relative error of at most 0.005.
Values may be sent and summed in bfloat16 or wider, within the bound.
No kernel may reach another device: no remote copies, remote signals or barrier semaphores. Data moves between devices by JAX's collectives and lax.ppermute only.
A program may use at most 128 MiB of HBM per device.

```python
import math
import jax
import jax.numpy as jnp
import numpy as np
from jax import lax

M = 2560
TERMS = 3
CHANNELS = 8
SHARDS = 16
ROW_DEV = 160
FANOUT = 10


def draw_generator(key, part):
    raw = jnp.clip(jax.random.normal(key, (CHANNELS, M, M), jnp.float32), -4.0, 4.0)
    skewed = (raw - jnp.swapaxes(raw, 1, 2)) * (0.01 / 1.4142135)
    return skewed.astype(jnp.bfloat16)


def draw_hamiltonian(key, part):
    raw = jnp.clip(jax.random.normal(key, (CHANNELS, M, M), jnp.float32), -4.0, 4.0)
    even = (raw + jnp.swapaxes(raw, 1, 2)) * (1.0 / 1.4142135)
    return even.astype(jnp.bfloat16)


def draw_ph_order(key, part):
    key_list = jax.random.split(jax.random.fold_in(key, 17), CHANNELS * SHARDS)
    shuffled = jax.vmap(lambda one_key: jax.random.permutation(one_key, ROW_DEV))(key_list)
    shuffled = shuffled.astype(jnp.int32).reshape(CHANNELS, SHARDS, SHARDS, FANOUT)
    offsets = (jnp.arange(SHARDS, dtype=jnp.int32) * ROW_DEV).reshape(1, SHARDS, 1, 1)
    placed = jnp.transpose(shuffled + offsets, (0, 2, 3, 1))
    return placed.reshape(CHANNELS, M).astype(jnp.int32)


def touch_ends(array, own_key, low, top_value):
    shape = array.shape
    index_at = [jax.random.randint(jax.random.fold_in(own_key, axis), (), 0, shape[axis]) for axis in range(len(shape))]
    array = array.at[tuple(index_at)].set(low)
    longest = shape.index(max(shape))
    index_at[longest] = (index_at[longest] + 1) % shape[longest]
    return array.at[tuple(index_at)].set(top_value)


def profile(amount, total, bound, slope):
    loads = [(1 << 20) // math.isqrt(grade ** slope) + 1 for grade in range(2, amount + 1)]
    rest, counts = total - bound - (amount - 1), [1] * (amount - 1)
    while rest > 0:
        candidates = [i for i in range(amount - 1) if counts[i] < bound]
        pool, remaining = sum([loads[i] for i in candidates]), rest
        for i in candidates:
            addition = min(bound - counts[i], max(1, remaining * loads[i] // pool), rest)
            counts[i] = counts[i] + addition
            rest = rest - addition
    return np.array([bound] + counts)


def ragged_sizes(stream_key, count, total, bound, skew):
    if count == 2:
        one = jax.random.randint(stream_key, (), max(1, total - bound), min(bound, total - 1) + 1)
        return jnp.stack([one, total - one])
    sizes = jnp.asarray(profile(count, total, bound, skew), jnp.int32)
    pairs = (count - 1) // 2
    source_of, taker = sizes[1:1 + 2 * pairs:2], sizes[2:2 + 2 * pairs:2]
    room = jnp.minimum(source_of - 1, bound - taker)
    shifted = jax.random.randint(jax.random.fold_in(stream_key, 1), (pairs,), 0, 1 << 20) % (room + 1)
    sizes = sizes.at[1:1 + 2 * pairs:2].set(source_of - shifted).at[2:2 + 2 * pairs:2].set(taker + shifted)
    return sizes[jax.random.permutation(jax.random.fold_in(stream_key, 2), count)]


def setup_inputs(seed: int = 0) -> dict:
    splits = jax.random.split(jax.random.key(seed), 8)
    return {
        "generator": draw_generator(jax.random.fold_in(splits[7], 71), 0),
        "hamiltonian": draw_hamiltonian(jax.random.fold_in(splits[7], 71), 0),
        "live_states": ragged_sizes(splits[2], CHANNELS, CHANNELS * M // 2 + M // 2, M, 2).astype(jnp.int32),
        "pp_occupation": touch_ends(jax.random.randint(splits[3], (CHANNELS, M), -1, 2), jax.random.fold_in(splits[3], 1), -1, 1).astype(jnp.int32),
        "ph_occupation": touch_ends(jax.random.randint(splits[4], (CHANNELS, M), -1, 2), jax.random.fold_in(splits[4], 1), -1, 1).astype(jnp.int32),
        "ph_order": draw_ph_order(jax.random.fold_in(splits[7], 71), 0),
        "recoupling": jnp.clip(jax.random.uniform(splits[6], (CHANNELS, 2), jnp.float32, 0.4, 1.0), 0.4, 1.0),
    }


def reference(generator, hamiltonian, live_states, pp_occupation, ph_occupation, ph_order, recoupling):
    group_count = generator.shape[0]
    state_count = generator.shape[1]
    positions = jnp.arange(state_count, dtype=jnp.int32)
    channel_ids = jnp.arange(group_count, dtype=jnp.int32)
    partner_ids = jnp.bitwise_xor(channel_ids, group_count // 2)
    alive = positions[None, :] < live_states[:, None]
    alive_square = alive[:, :, None] & alive[:, None, :]
    generator = jnp.where(alive_square, generator, jnp.zeros_like(generator))
    hamiltonian = jnp.where(alive_square, hamiltonian, jnp.zeros_like(hamiltonian))
    position_grid = jnp.broadcast_to(positions[None, :], (group_count, state_count))
    inverse = jnp.zeros((group_count, state_count), jnp.int32).at[channel_ids[:, None], ph_order].set(position_grid)
    pp_weights = jnp.where(alive, pp_occupation, 0).astype(jnp.float32)
    ph_weights = jnp.where(alive, jnp.take_along_axis(ph_occupation, inverse, axis=1), 0).astype(jnp.float32)
    own_weights = recoupling[:, 0][:, None, None]
    far_weights = recoupling[:, 1][:, None, None]
    back_weights = recoupling[partner_ids, 1][:, None, None]
    omega_wide = generator.astype(jnp.float32)
    omega_far = omega_wide[partner_ids]
    current = hamiltonian
    running = hamiltonian.astype(jnp.float32)
    for term_index in range(1, TERMS + 1):
        wide_current = current.astype(jnp.float32)
        pp_prod = jnp.matmul(wide_current * pp_weights[:, None, :], omega_wide).astype(jnp.bfloat16)
        pp_prod = lax.optimization_barrier(pp_prod).astype(jnp.float32)
        mixed = (own_weights * wide_current + far_weights * wide_current[partner_ids]).astype(jnp.bfloat16)
        recoupled = jnp.take_along_axis(mixed, ph_order[:, :, None], axis=1).astype(jnp.float32)
        weighted = recoupled * ph_weights[:, None, :]
        ph_prod = (own_weights * jnp.matmul(weighted, omega_wide) + far_weights * jnp.matmul(weighted, omega_far)).astype(jnp.bfloat16)
        returned = jnp.take_along_axis(ph_prod, inverse[:, :, None], axis=1).astype(jnp.float32)
        combined = (pp_prod + own_weights * returned + back_weights * returned[partner_ids]).astype(jnp.bfloat16)
        combined = lax.optimization_barrier(combined).astype(jnp.float32)
        increment = -(combined + jnp.swapaxes(combined, 1, 2)) / term_index
        running = running + increment
        current = increment.astype(jnp.bfloat16)
    return running
```

```python
import jax
import jax.numpy as jnp
from jax import lax
from jax.sharding import Mesh, PartitionSpec as P

TERMS = 3


def swapped(value):
    return lax.ppermute(value, "hi", [(0, 1), (1, 0)])


def on_device(
    generator, hamiltonian, live_states, pp_occupation, ph_occupation, ph_order, recoupling
):
    row_count = generator.shape[1]
    state_count = generator.shape[2]
    half = row_count // 2
    shard_count = lax.axis_size("row")
    hi = lax.axis_index("hi")
    lo = lax.axis_index("lo")
    my_shard = lax.axis_index("row")
    first = hi == 0
    r0 = recoupling[lo]
    r1 = recoupling[lo + lax.axis_size("lo")]
    positions = jnp.arange(state_count, dtype=jnp.int32)
    live_count = live_states[0]
    column_alive = positions < live_count
    row_alive = my_shard * row_count + jnp.arange(row_count, dtype=jnp.int32) < live_count
    block_alive = row_alive[:, None] & column_alive[None, :]
    own_share = jnp.where(block_alive, generator[0], jnp.zeros_like(generator[0]))
    far_share = swapped(own_share)
    full_own = lax.all_gather(own_share, "row", axis=0, tiled=True)
    full_far = lax.all_gather(far_share, "row", axis=0, tiled=True)

    pp = jnp.where(column_alive, pp_occupation[0], 0)
    ph = jnp.zeros((state_count,), jnp.int32).at[ph_order[0]].set(ph_occupation[0])
    ph = jnp.where(column_alive, ph, 0)
    mine = jnp.stack([pp, ph]).astype(jnp.float32)
    other = swapped(mine)
    d0, n0 = jnp.where(first, mine, other)
    d1, n1 = jnp.where(first, other, mine)
    a0 = d0 + r0[0] ** 3 * n0 + r1[1] ** 3 * n1
    a1 = d1 + r1[0] ** 3 * n1 + r0[1] ** 3 * n0
    p = r0[0] ** 2 * r0[1] * n0 + r1[1] ** 2 * r1[0] * n1
    q = r1[0] ** 2 * r1[1] * n1 + r0[1] ** 2 * r0[0] * n0
    zero_set = jnp.stack([a0, p, p, q])
    one_set = jnp.stack([p, q, q, a1])
    own_set = jnp.where(first, zero_set, one_set)
    far_set = jnp.where(first, one_set, zero_set)

    own_ham = jnp.where(block_alive, hamiltonian[0], jnp.zeros_like(hamiltonian[0]))
    keep = lax.dynamic_slice_in_dim(own_ham, hi * half, half, 0)
    gone = lax.dynamic_slice_in_dim(own_ham, (1 - hi) * half, half, 0)
    came = swapped(gone)
    current = jnp.concatenate([jnp.where(first, keep, came), jnp.where(first, came, keep)])
    running = jnp.zeros(current.shape, jnp.float32)

    def mix(x, s):
        x0, x1 = x[:half], x[half:]
        top = x0 * s[0] + x1 * s[1]
        low = x0 * s[2] + x1 * s[3]
        return jnp.concatenate([top, low]).astype(jnp.bfloat16)

    for term_index in range(1, TERMS + 1):
        wide = current.astype(jnp.float32)
        combined = jnp.dot(
            mix(wide, own_set), full_own, preferred_element_type=jnp.float32
        ) + jnp.dot(mix(wide, far_set), full_far, preferred_element_type=jnp.float32)
        combined = combined.astype(jnp.bfloat16)
        if term_index < TERMS:
            sent = combined.T
            got = lax.all_to_all(sent, ("row", "hi"), split_axis=0, concat_axis=0, tiled=True)
            got = got.reshape(2 * shard_count, half, 2, half)
            flipped = jnp.transpose(got, (2, 1, 0, 3)).reshape(row_count, state_count)
            increment = -(combined.astype(jnp.float32) + flipped.astype(jnp.float32)) / term_index
            running = running + increment
            current = increment.astype(jnp.bfloat16)
    running = running - combined.astype(jnp.float32) / TERMS
    leaving = lax.dynamic_slice_in_dim(running, (1 - hi) * half, half, 0).astype(jnp.bfloat16)
    staying = lax.dynamic_slice_in_dim(running, hi * half, half, 0)
    landed = swapped(leaving).astype(jnp.float32)
    blocks = combined.reshape(2, half, shard_count, row_count)
    blocks = jnp.transpose(blocks, (0, 2, 3, 1)).reshape(2 * state_count, half)
    got = lax.all_to_all(blocks, ("hi", "row"), split_axis=0, concat_axis=0, tiled=True)
    got = got.reshape(2, shard_count, row_count, half)
    flipped = jnp.transpose(got, (2, 1, 0, 3)).reshape(row_count, state_count)
    rows = jnp.concatenate(
        [jnp.where(first, staying, landed), jnp.where(first, landed, staying)]
    )
    return (own_ham.astype(jnp.float32) + rows - flipped.astype(jnp.float32) / TERMS)[None]


def solution(mesh):
    chans, rows = mesh.devices.shape
    pairs = Mesh(mesh.devices.reshape(2, chans // 2, rows), ("hi", "lo", "row"))
    chan = ("hi", "lo")
    placed = (
        P(chan, "row", None),
        P(chan, "row", None),
        P(chan),
        P(chan, None),
        P(chan, None),
        P(chan, None),
        P(),
    )
    return jax.shard_map(
        on_device, mesh=pairs, in_specs=placed, out_specs=P(chan, "row", None), check_vma=False
    )
```

```python
import functools

import jax
import jax.numpy as jnp
from jax import lax
from jax.experimental import pallas as pl
from jax.experimental.pallas import tpu as pltpu
from jax.sharding import Mesh, PartitionSpec as P

TERMS = 3
LANES = 128
STEP = 32
BF = jnp.bfloat16
F32 = jnp.float32
VMEM = pl.BlockSpec(memory_space=pltpu.VMEM)
SMEM = pl.BlockSpec(memory_space=pltpu.SMEM)


def tile_at(index):
    return pl.ds(pl.multiple_of(index * LANES, LANES), LANES)


def pack_kernel(sent_tiles, tiles, scalars, gen_ref, out_ref):
    start, live = scalars[0], scalars[1]
    for group in range(gen_ref.shape[0] // STEP):
        rows = pl.ds(group * STEP, STEP)
        first_row = start + group * STEP
        diagonal = first_row // LANES
        row_at = first_row + lax.broadcasted_iota(jnp.int32, (STEP, LANES), 0)
        for apart in range(sent_tiles):
            tile = lax.rem(diagonal + apart, tiles)
            column_at = tile * LANES + lax.broadcasted_iota(jnp.int32, (STEP, LANES), 1)
            alive = (row_at < live) & (column_at < live)
            value = gen_ref[rows, tile_at(tile)].astype(F32)
            out_ref[rows, apart * LANES : (apart + 1) * LANES] = jnp.where(
                alive, value, 0.0
            ).astype(BF)


def unpack_kernel(blocks, sent_tiles, tiles, got_ref, out_ref, held, sems):
    matrix, a = pl.program_id(0), pl.program_id(1)
    rows = got_ref.shape[2]

    def copies(which):
        return [
            pltpu.make_async_copy(
                got_ref.at[block, which],
                held.at[which, pl.ds(block * rows, rows)],
                sems.at[which, block],
            )
            for block in range(blocks)
        ]

    @pl.when((matrix == 0) & (a == 0))
    def _():
        for which in range(2):
            for copy in copies(which):
                copy.start()

    for which in range(2):

        @pl.when((matrix == which) & (a == 0))
        def _(which=which):
            for copy in copies(which):
                copy.wait()

    for apart in range(tiles):
        b = lax.rem(a + apart, tiles)
        if apart < sent_tiles:
            value = held[matrix, tile_at(a), apart * LANES : (apart + 1) * LANES]
        else:
            back = tiles - apart
            value = held[matrix, tile_at(b), back * LANES : (back + 1) * LANES]
            value = (-value).T
        out_ref[0, :, tile_at(b)] = value


def send_kernel(half, c_ref, out_ref):
    filler = jnp.zeros((LANES - half, LANES), F32)
    for tile in range(c_ref.shape[1] // LANES):
        at = slice(tile * LANES, (tile + 1) * LANES)
        for channel in range(2):
            block = c_ref[channel * half : (channel + 1) * half, at].astype(F32)
            block = jnp.concatenate([block, filler]).T
            out_ref[at, channel * LANES : (channel + 1) * LANES] = block.astype(BF)


def laid_out(pieces, half, tile):
    lane = lax.broadcasted_iota(jnp.int32, (1, LANES), 1)
    low = tile * LANES
    result = None
    for piece in range(low // half, (low + LANES - 1) // half + 1):
        shift = (piece * half - low) % LANES
        value = pieces(piece)
        if shift:
            value = pltpu.roll(value, shift, 1)
        begin = piece * half - low
        inside = lane >= begin
        result = value if result is None else jnp.where(inside, value, result)
    return result


def mix(x0, x1, weights, out_ref, half, at):
    out_ref[:half, at] = (x0 * weights[0:1] + x1 * weights[1:2]).astype(BF)
    out_ref[half:, at] = (x0 * weights[2:3] + x1 * weights[3:4]).astype(BF)


def start_kernel(half, x_ref, own_ref, far_ref, a_own, a_far):
    for tile in range(x_ref.shape[1] // LANES):
        at = slice(tile * LANES, (tile + 1) * LANES)
        x0, x1 = x_ref[:half, at].astype(F32), x_ref[half:, at].astype(F32)
        mix(x0, x1, own_ref[:, at], a_own, half, at)
        mix(x0, x1, far_ref[:, at], a_far, half, at)


def update_kernel(half, scale, c_ref, got_ref, run_ref, own_ref, far_ref, run_out, a_own, a_far):
    for tile in range(c_ref.shape[1] // LANES):
        at = slice(tile * LANES, (tile + 1) * LANES)
        xs = []
        for channel in range(2):
            lanes = slice(channel * LANES, (channel + 1) * LANES)
            flipped = laid_out(lambda s: got_ref[s, :, lanes].astype(F32), half, tile)
            rows = slice(channel * half, (channel + 1) * half)
            increment = (c_ref[rows, at].astype(F32) + flipped) * scale
            run_out[rows, at] = run_ref[rows, at] + increment
            xs.append(increment.astype(BF).astype(F32))
        mix(xs[0], xs[1], own_ref[:, at], a_own, half, at)
        mix(xs[0], xs[1], far_ref[:, at], a_far, half, at)


def end_kernel(half, scale, first_ref, ham_ref, stay_ref, land_ref, got_ref, out_ref):
    first = first_ref[0] != 0
    for tile in range(ham_ref.shape[1] // LANES):
        at = slice(tile * LANES, (tile + 1) * LANES)
        flipped = laid_out(
            lambda s: got_ref[s % 2, s // 2].astype(F32), half, tile
        )
        total = ham_ref[:, at].astype(F32) + flipped * scale
        stay, land = stay_ref[:, at], land_ref[:, at].astype(F32)
        out_ref[:half, at] = total[:half] + jnp.where(first, stay, land)
        out_ref[half:, at] = total[half:] + jnp.where(first, land, stay)


def call(kernel, out_shape, specs, name, megabytes=0):
    single = not isinstance(out_shape, (list, tuple))
    return pl.pallas_call(
        kernel,
        out_shape=out_shape,
        in_specs=specs,
        out_specs=VMEM if single else [VMEM] * len(out_shape),
        compiler_params=pltpu.CompilerParams(vmem_limit_bytes=24 << 20),
        name=name,
    )


def swapped(value):
    return lax.ppermute(value, "hi", [(0, 1), (1, 0)])


def on_device(
    generator, hamiltonian, live_states, pp_occupation, ph_occupation, ph_order, recoupling
):
    row_count = generator.shape[1]
    state_count = generator.shape[2]
    half = row_count // 2
    shard_count = lax.axis_size("row")
    tiles = state_count // LANES
    sent_tiles = tiles // 2 + 1
    hi = lax.axis_index("hi")
    lo = lax.axis_index("lo")
    my_shard = lax.axis_index("row")
    first = hi == 0
    shape = jax.ShapeDtypeStruct
    r0 = recoupling[lo]
    r1 = recoupling[lo + lax.axis_size("lo")]
    positions = jnp.arange(state_count, dtype=jnp.int32)
    live_count = live_states[0]
    column_alive = positions < live_count
    row_alive = my_shard * row_count + jnp.arange(row_count, dtype=jnp.int32) < live_count
    block_alive = row_alive[:, None] & column_alive[None, :]

    share = call(
        functools.partial(pack_kernel, sent_tiles, tiles),
        shape((row_count, sent_tiles * LANES), BF),
        [SMEM, VMEM],
        "pack",
    )(jnp.stack([my_shard * row_count, live_count]), generator[0])
    both = jnp.stack([share, swapped(share)])
    gathered = lax.all_gather(both, "row", axis=0, tiled=False)
    omegas = pl.pallas_call(
        functools.partial(unpack_kernel, shard_count, sent_tiles, tiles),
        grid=(2, tiles),
        out_shape=shape((2, state_count, state_count), BF),
        in_specs=[pl.BlockSpec(memory_space=pl.ANY)],
        out_specs=pl.BlockSpec((1, LANES, state_count), lambda m, a: (m, a, 0)),
        scratch_shapes=[
            pltpu.VMEM((2, state_count, sent_tiles * LANES), BF),
            pltpu.SemaphoreType.DMA((2, shard_count)),
        ],
        compiler_params=pltpu.CompilerParams(vmem_limit_bytes=24 << 20),
        name="unpack",
    )(gathered)

    pp = jnp.where(column_alive, pp_occupation[0], 0)
    ph = jnp.zeros((state_count,), jnp.int32).at[ph_order[0]].set(ph_occupation[0])
    ph = jnp.where(column_alive, ph, 0)
    mine = jnp.stack([pp, ph]).astype(F32)
    other = swapped(mine)
    d0, n0 = jnp.where(first, mine, other)
    d1, n1 = jnp.where(first, other, mine)
    a0 = d0 + r0[0] ** 3 * n0 + r1[1] ** 3 * n1
    a1 = d1 + r1[0] ** 3 * n1 + r0[1] ** 3 * n0
    p = r0[0] ** 2 * r0[1] * n0 + r1[1] ** 2 * r1[0] * n1
    q = r1[0] ** 2 * r1[1] * n1 + r0[1] ** 2 * r0[0] * n0
    zero_set = jnp.stack([a0, p, p, q])
    one_set = jnp.stack([p, q, q, a1])
    own_set = jnp.where(first, zero_set, one_set)
    far_set = jnp.where(first, one_set, zero_set)

    own_ham = jnp.where(block_alive, hamiltonian[0], jnp.zeros_like(hamiltonian[0]))
    keep = lax.dynamic_slice_in_dim(own_ham, hi * half, half, 0)
    gone = lax.dynamic_slice_in_dim(own_ham, (1 - hi) * half, half, 0)
    came = swapped(gone)
    current = jnp.concatenate([jnp.where(first, keep, came), jnp.where(first, came, keep)])
    running = jnp.zeros(current.shape, F32)
    mixed_shape = shape((row_count, state_count), BF)
    mixed_own, mixed_far = call(
        functools.partial(start_kernel, half), [mixed_shape] * 2, [VMEM] * 3, "start"
    )(current, own_set, far_set)

    for term_index in range(1, TERMS + 1):
        combined = jnp.dot(mixed_own, omegas[0], preferred_element_type=F32) + jnp.dot(
            mixed_far, omegas[1], preferred_element_type=F32
        )
        combined = combined.astype(BF)
        columns = call(
            functools.partial(send_kernel, half),
            shape((state_count, 2 * LANES), BF),
            [VMEM],
            "send",
        )(combined)
        if term_index < TERMS:
            got = lax.all_to_all(
                columns.reshape(2 * shard_count, half, 2 * LANES),
                ("row", "hi"),
                split_axis=0,
                concat_axis=0,
                tiled=True,
            )
            running, mixed_own, mixed_far = call(
                functools.partial(update_kernel, half, -1.0 / term_index),
                [shape((row_count, state_count), F32), mixed_shape, mixed_shape],
                [VMEM] * 5,
                "update",
            )(combined, got, running, own_set, far_set)
    running = running - combined.astype(F32) / TERMS
    leaving = lax.dynamic_slice_in_dim(running, (1 - hi) * half, half, 0).astype(BF)
    staying = lax.dynamic_slice_in_dim(running, hi * half, half, 0)
    landed = swapped(leaving)
    blocks = columns.reshape(shard_count, row_count, 2, LANES)
    blocks = jnp.transpose(blocks, (2, 0, 1, 3)).reshape(2 * shard_count, row_count, LANES)
    got = lax.all_to_all(blocks, ("hi", "row"), split_axis=0, concat_axis=0, tiled=True)
    result = call(
        functools.partial(end_kernel, half, -1.0 / TERMS),
        shape((row_count, state_count), F32),
        [SMEM] + [VMEM] * 4,
        "finish",
    )(
        first.astype(jnp.int32)[None],
        own_ham,
        staying,
        landed,
        got.reshape(2, shard_count, row_count, LANES),
    )
    return result[None]


def solution(mesh):
    chans, rows = mesh.devices.shape
    pairs = Mesh(mesh.devices.reshape(2, chans // 2, rows), ("hi", "lo", "row"))
    chan = ("hi", "lo")
    placed = (
        P(chan, "row", None),
        P(chan, "row", None),
        P(chan),
        P(chan, None),
        P(chan, None),
        P(chan, None),
        P(),
    )
    return jax.shard_map(
        on_device, mesh=pairs, in_specs=placed, out_specs=P(chan, "row", None), check_vma=False
    )
```

```python
import functools

import jax
import jax.numpy as jnp
from jax import lax
from jax.experimental import pallas as pl
from jax.experimental.pallas import tpu as pltpu
from jax.sharding import Mesh, PartitionSpec as P

TERMS = 3
LANES = 128
STEP = 32
BF = jnp.bfloat16
F32 = jnp.float32
VMEM = pl.BlockSpec(memory_space=pltpu.VMEM)
SMEM = pl.BlockSpec(memory_space=pltpu.SMEM)
HBM = pl.BlockSpec(memory_space=pltpu.HBM)


def tile_at(index):
    return pl.ds(pl.multiple_of(index * LANES, LANES), LANES)


def pack_kernel(sent_tiles, tiles, scalars, gen_ref, out_ref):
    start, live = scalars[0], scalars[1]
    for group in range(gen_ref.shape[0] // STEP):
        rows = pl.ds(group * STEP, STEP)
        first_row = start + group * STEP
        diagonal = first_row // LANES
        row_at = first_row + lax.broadcasted_iota(jnp.int32, (STEP, LANES), 0)
        for apart in range(sent_tiles):
            tile = lax.rem(diagonal + apart, tiles)
            column_at = tile * LANES + lax.broadcasted_iota(jnp.int32, (STEP, LANES), 1)
            alive = (row_at < live) & (column_at < live)
            value = gen_ref[rows, tile_at(tile)].astype(F32)
            out_ref[rows, apart * LANES : (apart + 1) * LANES] = jnp.where(
                alive, value, 0.0
            ).astype(BF)


def shifted(value, shift):
    shift = shift % LANES
    return pltpu.roll(value, shift, 1) if shift else value


def lane_index():
    return lax.broadcasted_iota(jnp.int32, (1, LANES), 1)


def laid_out(pieces, half, tile):
    low = tile * LANES
    result = None
    for piece in range(low // half, (low + LANES - 1) // half + 1):
        begin = piece * half - low
        value = pieces(piece, begin)
        result = value if result is None else jnp.where(lane_index() >= begin, value, result)
    return result


def mix(x0, x1, own_ref, far_ref, mixed, half, tile, tiles):
    at = slice(tile * LANES, (tile + 1) * LANES)
    places = [at]
    if (tile + tiles + 1) * LANES <= mixed.shape[2]:
        places.append(slice((tile + tiles) * LANES, (tile + tiles + 1) * LANES))
    for which, weights in enumerate((own_ref, far_ref)):
        top = (x0 * weights[0:1, at] + x1 * weights[1:2, at]).astype(BF)
        low = (x0 * weights[2:3, at] + x1 * weights[3:4, at]).astype(BF)
        for place in places:
            mixed[which, :half, place] = top
            mixed[which, half:, place] = low


def product(got_ref, mixed, total, held, sems, tiles):
    pairs = tiles // 2
    blocks = got_ref.shape[0]
    per_chunk = blocks // 2

    def step(index, carry):
        which = index // pairs
        pair = lax.rem(index, pairs)

        @pl.when(lax.rem(index, pairs // 2) == 0)
        def _():
            chunk = lax.rem(index // (pairs // 2), 2)

            @pl.loop(0, per_chunk)
            def _(k):
                block_copy(got_ref, held, sems, which, chunk * per_chunk + k).wait()

        even = pl.multiple_of(pair * 2 * LANES, 2 * LANES)
        odd = pl.multiple_of(even + LANES, LANES)

        def rows(start, low, high):
            return held[which, pl.ds(start, LANES), low * LANES : high * LANES]

        def left(apart, count):
            at = pl.multiple_of(even + apart * LANES, LANES)
            return mixed[which, :, pl.ds(at, count * LANES)]

        def add(apart, count, value):
            at = pl.multiple_of(even + apart * LANES, LANES)
            total[:, pl.ds(at, count * LANES)] += value

        def straight(a, w):
            return jnp.dot(a, w, preferred_element_type=F32)

        def turned(a, w):
            return lax.dot_general(a, w, (((1,), (1,)), ((), ())), preferred_element_type=F32)

        span = pairs
        both = jnp.concatenate([rows(even, 1, span + 1), rows(odd, 0, span)], 0)
        add(1, span, straight(left(0, 2), both))
        both = jnp.concatenate([rows(even, 2, span), rows(odd, 1, span - 1)], 0)
        add(0, 2, -turned(left(2, span - 2), both))
        add(0, 1, straight(left(0, 1), rows(even, 0, 1)) - turned(left(1, 1), rows(even, 1, 2)))
        add(1, 1, -turned(left(span, 1), rows(odd, span - 1, span)))
        add(span + 1, 1, straight(left(1, 1), rows(odd, span, span + 1)))
        return carry

    lax.fori_loop(0, 2 * pairs, step, 0)


def block_copy(got_ref, held, sems, which, block):
    rows = got_ref.shape[2]
    at = pl.multiple_of(block * rows, rows)
    return pltpu.make_async_copy(
        got_ref.at[block, which], held.at[which, pl.ds(at, rows)], sems.at[which, block]
    )


def begin(got_ref, held, sems):
    for which in range(2):

        @pl.loop(0, got_ref.shape[0])
        def _(block):
            block_copy(got_ref, held, sems, which, block).start()


def folded(total, tile, tiles):
    at = slice(tile * LANES, (tile + 1) * LANES)
    value = total[:, at]
    if (tile + tiles + 1) * LANES <= total.shape[1]:
        value = value + total[:, (tile + tiles) * LANES : (tile + tiles + 1) * LANES]
    return value.astype(BF)


def pack_columns(c_ref, columns, half):
    count = c_ref.shape[1] // half
    rest = c_ref.shape[0] - LANES
    for tile in range(c_ref.shape[1] // LANES):
        block = c_ref[:LANES, tile * LANES : (tile + 1) * LANES].astype(F32).T.astype(BF)
        step = 16
        for k in range(LANES // step):
            row = tile * LANES + k * step
            columns[row // half, row % half : row % half + step, :] = block[k * step : (k + 1) * step]
    for piece in range(count):
        tile, off = divmod(piece * half, LANES)
        tail = slice(LANES, LANES + rest)
        value = shifted(c_ref[tail, tile * LANES : (tile + 1) * LANES].astype(F32), -off)
        if off + half > LANES:
            more = c_ref[tail, (tile + 1) * LANES : (tile + 2) * LANES].astype(F32)
            value = jnp.where(lane_index() < LANES - off, value, shifted(more, -off))
        columns[piece, half : half + rest, :] = value.astype(BF)


def flipped_tiles(got_ref, turned, half, tile):
    rest = 2 * half - LANES
    group = LANES // rest
    kept = half - rest

    def near(s, begin):
        return shifted(got_ref[s, :half, :].astype(F32), begin)

    def far(s, begin):
        front = shifted(got_ref[s, :half, :].astype(F32), begin - half)
        back = turned[s // group, :half, :]
        back = shifted(back, begin + kept - rest * (s % group))
        return jnp.where(lane_index() >= begin + kept, back, front)

    def far_safe(s, begin):
        return far(s, begin)

    return laid_out(near, half, tile), laid_out(far_safe, half, tile)


def turn_rest(got_ref, turned, half):
    rest = 2 * half - LANES
    group = LANES // rest
    for k in range(got_ref.shape[0] // group):
        block = jnp.concatenate(
            [got_ref[k * group + m, half : half + rest, :].astype(F32) for m in range(group)], 0
        )
        turned[k] = block.T


def finish_products(c_out, total, tiles):
    for tile in range(tiles):
        c_out[:, tile * LANES : (tile + 1) * LANES] = folded(total, tile, tiles)


def first_kernel(
    half, tiles, x_ref, own_ref, far_ref, got_ref, c_out, columns, mixed, total, held, sems
):
    begin(got_ref, held, sems)
    for tile in range(tiles):
        at = slice(tile * LANES, (tile + 1) * LANES)
        x0, x1 = x_ref[:half, at].astype(F32), x_ref[half:, at].astype(F32)
        mix(x0, x1, own_ref, far_ref, mixed, half, tile, tiles)
    total[...] = jnp.zeros_like(total)
    product(got_ref, mixed, total, held, sems, tiles)
    finish_products(c_out, total, tiles)
    pack_columns(c_out, columns, half)


def update(half, tiles, scale, c_ref, back_ref, own_ref, far_ref, mixed, turned, keep):
    turn_rest(back_ref, turned, half)
    for tile in range(tiles):
        at = slice(tile * LANES, (tile + 1) * LANES)
        xs = []
        for channel, flipped in enumerate(flipped_tiles(back_ref, turned, half, tile)):
            rows = slice(channel * half, (channel + 1) * half)
            increment = (c_ref[rows, at].astype(F32) + flipped) * scale
            keep(rows, at, increment)
            xs.append(increment.astype(BF).astype(F32))
        mix(xs[0], xs[1], own_ref, far_ref, mixed, half, tile, tiles)


def middle_kernel(
    half, tiles, scale, c_ref, back_ref, own_ref, far_ref, got_ref, c_out, run_out, columns,
    mixed, total, held, sems, turned,
):
    begin(got_ref, held, sems)

    def keep(rows, at, increment):
        run_out[rows, at] = increment

    update(half, tiles, scale, c_ref, back_ref, own_ref, far_ref, mixed, turned, keep)
    total[...] = jnp.zeros_like(total)
    product(got_ref, mixed, total, held, sems, tiles)
    finish_products(c_out, total, tiles)
    pack_columns(c_out, columns, half)


def last_kernel(
    half, tiles, scale, last_scale, first_ref, c_ref, back_ref, run_ref, own_ref, far_ref, got_ref,
    leave, stay, columns, mixed, total, held, sems, turned, run,
):
    begin(got_ref, held, sems)

    def keep(rows, at, increment):
        run[rows, at] = run_ref[rows, at] + increment

    update(half, tiles, scale, c_ref, back_ref, own_ref, far_ref, mixed, turned, keep)
    total[...] = jnp.zeros_like(total)
    product(got_ref, mixed, total, held, sems, tiles)
    first = first_ref[0] != 0
    filler = jnp.zeros((LANES - half, LANES), F32)
    for tile in range(tiles):
        at = slice(tile * LANES, (tile + 1) * LANES)
        value = folded(total, tile, tiles).astype(F32)
        for channel in range(2):
            block = jnp.concatenate([value[channel * half : (channel + 1) * half], filler])
            columns[channel, at, :] = block.T.astype(BF)
        both = run[:, at] + value * last_scale
        leave[:, at] = jnp.where(first, both[half:], both[:half]).astype(BF)
        stay[:, at] = jnp.where(first, both[:half], both[half:])


def end_kernel(half, scale, first_ref, ham_ref, stay_ref, land_ref, got_ref, out_ref):
    first = first_ref[0] != 0

    def piece(s, begin):
        return shifted(got_ref[s % 2, s // 2].astype(F32), begin)

    for tile in range(ham_ref.shape[1] // LANES):
        at = slice(tile * LANES, (tile + 1) * LANES)
        total = ham_ref[:, at].astype(F32) + laid_out(piece, half, tile) * scale
        stay, land = stay_ref[:, at], land_ref[:, at].astype(F32)
        out_ref[:half, at] = total[:half] + jnp.where(first, stay, land)
        out_ref[half:, at] = total[half:] + jnp.where(first, land, stay)


def call(kernel, out_shape, specs, name, scratch=(), cost=None):
    single = not isinstance(out_shape, (list, tuple))
    return pl.pallas_call(
        kernel,
        out_shape=out_shape,
        in_specs=specs,
        out_specs=VMEM if single else [VMEM] * len(out_shape),
        scratch_shapes=scratch,
        compiler_params=pltpu.CompilerParams(vmem_limit_bytes=(40 if scratch else 16) << 20),
        cost_estimate=cost,
        name=name,
    )


def swapped(value):
    return lax.ppermute(value, "hi", [(0, 1), (1, 0)])


def on_device(
    generator, hamiltonian, live_states, pp_occupation, ph_occupation, ph_order, recoupling
):
    row_count = generator.shape[1]
    state_count = generator.shape[2]
    half = row_count // 2
    shard_count = lax.axis_size("row")
    tiles = state_count // LANES
    sent_tiles = tiles // 2 + 1
    hi = lax.axis_index("hi")
    lo = lax.axis_index("lo")
    my_shard = lax.axis_index("row")
    first = hi == 0
    shape = jax.ShapeDtypeStruct
    r0 = recoupling[lo]
    r1 = recoupling[lo + lax.axis_size("lo")]
    positions = jnp.arange(state_count, dtype=jnp.int32)
    live_count = live_states[0]
    column_alive = positions < live_count
    row_alive = my_shard * row_count + jnp.arange(row_count, dtype=jnp.int32) < live_count
    block_alive = row_alive[:, None] & column_alive[None, :]

    share = call(
        functools.partial(pack_kernel, sent_tiles, tiles),
        shape((row_count, sent_tiles * LANES), BF),
        [SMEM, VMEM],
        "pack",
    )(jnp.stack([my_shard * row_count, live_count]), generator[0])
    both = jnp.stack([share, swapped(share)])
    gathered = lax.all_gather(both, "row", axis=0, tiled=False)
    pp = jnp.where(column_alive, pp_occupation[0], 0)
    ph = jnp.zeros((state_count,), jnp.int32).at[ph_order[0]].set(ph_occupation[0])
    ph = jnp.where(column_alive, ph, 0)
    mine = jnp.stack([pp, ph]).astype(F32)
    other = swapped(mine)
    d0, n0 = jnp.where(first, mine, other)
    d1, n1 = jnp.where(first, other, mine)
    a0 = d0 + r0[0] ** 3 * n0 + r1[1] ** 3 * n1
    a1 = d1 + r1[0] ** 3 * n1 + r0[1] ** 3 * n0
    p = r0[0] ** 2 * r0[1] * n0 + r1[1] ** 2 * r1[0] * n1
    q = r1[0] ** 2 * r1[1] * n1 + r0[1] ** 2 * r0[0] * n0
    zero_set = jnp.stack([a0, p, p, q])
    one_set = jnp.stack([p, q, q, a1])
    own_set = jnp.where(first, zero_set, one_set)
    far_set = jnp.where(first, one_set, zero_set)

    own_ham = jnp.where(block_alive, hamiltonian[0], jnp.zeros_like(hamiltonian[0]))
    keep = lax.dynamic_slice_in_dim(own_ham, hi * half, half, 0)
    gone = lax.dynamic_slice_in_dim(own_ham, (1 - hi) * half, half, 0)
    came = swapped(gone)
    current = jnp.concatenate([jnp.where(first, keep, came), jnp.where(first, came, keep)])

    wide = (tiles + sent_tiles - 1) * LANES
    rest = row_count - LANES
    destinations = 2 * shard_count
    scratch = [
        pltpu.VMEM((2, row_count, wide), BF),
        pltpu.VMEM((row_count, wide), F32),
        pltpu.VMEM((2, state_count, sent_tiles * LANES), BF),
        pltpu.SemaphoreType.DMA((2, shard_count)),
    ]
    more = [pltpu.VMEM((destinations * rest // LANES, LANES, LANES), F32)]
    c_shape = shape((row_count, state_count), BF)
    run_shape = shape((row_count, state_count), F32)
    sent_shape = shape((destinations, half + rest, LANES), BF)
    cost = pl.CostEstimate(
        flops=4 * row_count * state_count * state_count,
        bytes_accessed=gathered.size * 2,
        transcendentals=0,
    )

    def exchanged(columns):
        return lax.all_to_all(columns, ("row", "hi"), split_axis=0, concat_axis=0, tiled=True)

    combined, columns = call(
        functools.partial(first_kernel, half, tiles),
        [c_shape, sent_shape],
        [VMEM] * 3 + [HBM],
        "first",
        scratch,
        cost,
    )(current, own_set, far_set, gathered)
    back = exchanged(columns)
    combined, running, columns = call(
        functools.partial(middle_kernel, half, tiles, -1.0),
        [c_shape, run_shape, sent_shape],
        [VMEM] * 4 + [HBM],
        "middle",
        scratch + more,
        cost,
    )(combined, back, own_set, far_set, gathered)
    back = exchanged(columns)
    which = first.astype(jnp.int32)[None]
    leaving, staying, blocks = call(
        functools.partial(last_kernel, half, tiles, -0.5, -1.0 / TERMS),
        [
            shape((half, state_count), BF),
            shape((half, state_count), F32),
            shape((2, state_count, LANES), BF),
        ],
        [SMEM] + [VMEM] * 5 + [HBM],
        "last",
        scratch + more + [pltpu.VMEM((row_count, state_count), F32)],
        cost,
    )(which, combined, back, running, own_set, far_set, gathered)
    landed = swapped(leaving)
    got = lax.all_to_all(
        blocks.reshape(destinations, row_count, LANES),
        ("hi", "row"),
        split_axis=0,
        concat_axis=0,
        tiled=True,
    )
    result = call(
        functools.partial(end_kernel, half, -1.0 / TERMS),
        shape((row_count, state_count), F32),
        [SMEM] + [VMEM] * 4,
        "finish",
    )(which, own_ham, staying, landed, got.reshape(2, shard_count, row_count, LANES))
    return result[None]


def solution(mesh):
    chans, rows = mesh.devices.shape
    pairs = Mesh(mesh.devices.reshape(2, chans // 2, rows), ("hi", "lo", "row"))
    chan = ("hi", "lo")
    placed = (
        P(chan, "row", None),
        P(chan, "row", None),
        P(chan),
        P(chan, None),
        P(chan, None),
        P(chan, None),
        P(),
    )
    return jax.shard_map(
        on_device, mesh=pairs, in_specs=placed, out_specs=P(chan, "row", None), check_vma=False
    )
```

```python
import functools

import jax
import jax.numpy as jnp
from jax import lax
from jax.experimental import pallas as pl
from jax.experimental.pallas import tpu as pltpu
from jax.sharding import Mesh, PartitionSpec as P

TERMS = 3
LANES = 128
STEP = 32
BF = jnp.bfloat16
F32 = jnp.float32
VMEM = pl.BlockSpec(memory_space=pltpu.VMEM)
SMEM = pl.BlockSpec(memory_space=pltpu.SMEM)
HBM = pl.BlockSpec(memory_space=pltpu.HBM)


def tile_at(index):
    return pl.ds(pl.multiple_of(index * LANES, LANES), LANES)


def pack_kernel(sent_tiles, tiles, scalars, gen_ref, out_ref):
    start, live = scalars[0], scalars[1]
    for group in range(gen_ref.shape[0] // STEP):
        rows = pl.ds(group * STEP, STEP)
        first_row = start + group * STEP
        diagonal = first_row // LANES
        row_at = first_row + lax.broadcasted_iota(jnp.int32, (STEP, LANES), 0)
        for apart in range(sent_tiles):
            tile = lax.rem(diagonal + apart, tiles)
            column_at = tile * LANES + lax.broadcasted_iota(jnp.int32, (STEP, LANES), 1)
            alive = (row_at < live) & (column_at < live)
            value = gen_ref[rows, tile_at(tile)].astype(F32)
            out_ref[rows, apart * LANES : (apart + 1) * LANES] = jnp.where(
                alive, value, 0.0
            ).astype(BF)


def shifted(value, shift):
    shift = shift % LANES
    return pltpu.roll(value, shift, 1) if shift else value


def lane_index():
    return lax.broadcasted_iota(jnp.int32, (1, LANES), 1)


def laid_out(pieces, half, tile):
    low = tile * LANES
    result = None
    for piece in range(low // half, (low + LANES - 1) // half + 1):
        begin = piece * half - low
        value = pieces(piece, begin)
        result = value if result is None else jnp.where(lane_index() >= begin, value, result)
    return result


def mix(x0, x1, own_ref, far_ref, mixed, half, tile, tiles):
    at = slice(tile * LANES, (tile + 1) * LANES)
    places = [at]
    if (tile + tiles + 1) * LANES <= mixed.shape[2]:
        places.append(slice((tile + tiles) * LANES, (tile + tiles + 1) * LANES))
    for which, weights in enumerate((own_ref, far_ref)):
        top = (x0 * weights[0:1, at] + x1 * weights[1:2, at]).astype(BF)
        low = (x0 * weights[2:3, at] + x1 * weights[3:4, at]).astype(BF)
        for place in places:
            mixed[which, :half, place] = top
            mixed[which, half:, place] = low


def product(got_ref, mixed, total, held, sems, tiles):
    pairs = tiles // 2
    per_chunk = got_ref.shape[0] // 2

    def step(pair, carry):
        @pl.when(lax.rem(pair, pairs // 2) == 0)
        def _():
            chunk = pair // (pairs // 2)
            for which in range(2):

                @pl.loop(0, per_chunk)
                def _(k):
                    block_copy(got_ref, held, sems, which, chunk * per_chunk + k).wait()

        even = pl.multiple_of(pair * 2 * LANES, 2 * LANES)
        odd = pl.multiple_of(even + LANES, LANES)

        def rows(which, start, low, high):
            return held[which, pl.ds(start, LANES), low * LANES : high * LANES]

        def left(apart, count):
            at = pl.ds(pl.multiple_of(even + apart * LANES, LANES), count * LANES)
            return jnp.concatenate([mixed[0, :, at], mixed[1, :, at]], 1)

        def add(apart, count, value):
            at = pl.multiple_of(even + apart * LANES, LANES)
            total[:, pl.ds(at, count * LANES)] += value

        def straight(a, parts):
            w = jnp.concatenate(parts, 0)
            return jnp.dot(a, w, preferred_element_type=F32)

        def turned(a, parts):
            w = jnp.concatenate(parts, 1)
            return lax.dot_general(a, w, (((1,), (1,)), ((), ())), preferred_element_type=F32)

        def two(start, low, high):
            return [rows(w, start, low, high) for w in range(2)]

        span = pairs
        parts = []
        for w in range(2):
            parts += [rows(w, even, 1, span + 1), rows(w, odd, 0, span)]
        add(1, span, straight(left(0, 2), parts))
        parts = [
            jnp.concatenate([rows(w, even, 2, span), rows(w, odd, 1, span - 1)], 0)
            for w in range(2)
        ]
        add(0, 2, -turned(left(2, span - 2), parts))
        near = straight(left(0, 1), two(even, 0, 1))
        add(0, 1, near - turned(left(1, 1), two(even, 1, 2)))
        add(1, 1, -turned(left(span, 1), two(odd, span - 1, span)))
        add(span + 1, 1, straight(left(1, 1), two(odd, span, span + 1)))
        return carry

    lax.fori_loop(0, pairs, step, 0)


def block_copy(got_ref, held, sems, which, block):
    rows = got_ref.shape[2]
    at = pl.multiple_of(block * rows, rows)
    return pltpu.make_async_copy(
        got_ref.at[block, which], held.at[which, pl.ds(at, rows)], sems.at[which, block]
    )


def begin(got_ref, held, sems):
    for which in range(2):

        @pl.loop(0, got_ref.shape[0])
        def _(block):
            block_copy(got_ref, held, sems, which, block).start()


def folded(total, tile, tiles):
    at = slice(tile * LANES, (tile + 1) * LANES)
    value = total[:, at]
    if (tile + tiles + 1) * LANES <= total.shape[1]:
        value = value + total[:, (tile + tiles) * LANES : (tile + tiles + 1) * LANES]
    return value.astype(BF)


def pack_columns(c_ref, columns, half):
    count = c_ref.shape[1] // half
    rest = c_ref.shape[0] - LANES
    for tile in range(c_ref.shape[1] // LANES):
        block = c_ref[:LANES, tile * LANES : (tile + 1) * LANES].astype(F32).T.astype(BF)
        step = 16
        for k in range(LANES // step):
            row = tile * LANES + k * step
            columns[row // half, row % half : row % half + step, :] = block[k * step : (k + 1) * step]
    for piece in range(count):
        tile, off = divmod(piece * half, LANES)
        tail = slice(LANES, LANES + rest)
        value = shifted(c_ref[tail, tile * LANES : (tile + 1) * LANES].astype(F32), -off)
        if off + half > LANES:
            more = c_ref[tail, (tile + 1) * LANES : (tile + 2) * LANES].astype(F32)
            value = jnp.where(lane_index() < LANES - off, value, shifted(more, -off))
        columns[piece, half : half + rest, :] = value.astype(BF)


def flipped_tiles(got_ref, turned, half, tile):
    rest = 2 * half - LANES
    group = LANES // rest
    kept = half - rest

    def near(s, begin):
        return shifted(got_ref[s, :half, :].astype(F32), begin)

    def far(s, begin):
        front = shifted(got_ref[s, :half, :].astype(F32), begin - half)
        back = turned[s // group, :half, :]
        back = shifted(back, begin + kept - rest * (s % group))
        return jnp.where(lane_index() >= begin + kept, back, front)

    return laid_out(near, half, tile), laid_out(far, half, tile)


def turn_rest(got_ref, turned, half):
    rest = 2 * half - LANES
    group = LANES // rest
    for k in range(got_ref.shape[0] // group):
        block = jnp.concatenate(
            [got_ref[k * group + m, half : half + rest, :].astype(F32) for m in range(group)], 0
        )
        turned[k] = block.T


def finish_products(c_out, total, tiles):
    for tile in range(tiles):
        c_out[:, tile * LANES : (tile + 1) * LANES] = folded(total, tile, tiles)


def first_kernel(
    half, tiles, x_ref, own_ref, far_ref, got_ref, c_out, columns, mixed, total, held, sems
):
    begin(got_ref, held, sems)
    for tile in range(tiles):
        at = slice(tile * LANES, (tile + 1) * LANES)
        x0, x1 = x_ref[:half, at].astype(F32), x_ref[half:, at].astype(F32)
        mix(x0, x1, own_ref, far_ref, mixed, half, tile, tiles)
    total[...] = jnp.zeros_like(total)
    product(got_ref, mixed, total, held, sems, tiles)
    finish_products(c_out, total, tiles)
    pack_columns(c_out, columns, half)


def update(half, tiles, scale, c_ref, back_ref, own_ref, far_ref, mixed, turned, keep):
    turn_rest(back_ref, turned, half)
    for tile in range(tiles):
        at = slice(tile * LANES, (tile + 1) * LANES)
        xs = []
        for channel, flipped in enumerate(flipped_tiles(back_ref, turned, half, tile)):
            rows = slice(channel * half, (channel + 1) * half)
            increment = (c_ref[rows, at].astype(F32) + flipped) * scale
            keep(rows, at, increment)
            xs.append(increment.astype(BF).astype(F32))
        mix(xs[0], xs[1], own_ref, far_ref, mixed, half, tile, tiles)


def middle_kernel(
    half, tiles, scale, c_ref, back_ref, own_ref, far_ref, got_ref, c_out, run_out, columns,
    mixed, total, held, sems, turned,
):
    begin(got_ref, held, sems)

    def keep(rows, at, increment):
        run_out[rows, at] = increment

    update(half, tiles, scale, c_ref, back_ref, own_ref, far_ref, mixed, turned, keep)
    total[...] = jnp.zeros_like(total)
    product(got_ref, mixed, total, held, sems, tiles)
    finish_products(c_out, total, tiles)
    pack_columns(c_out, columns, half)


def last_kernel(
    half, tiles, scale, last_scale, first_ref, c_ref, back_ref, run_ref, own_ref, far_ref, got_ref,
    leave, stay, columns, mixed, total, held, sems, turned, run, turned_all,
):
    begin(got_ref, held, sems)

    def keep(rows, at, increment):
        run[rows, at] = run_ref[rows, at] + increment

    update(half, tiles, scale, c_ref, back_ref, own_ref, far_ref, mixed, turned, keep)
    total[...] = jnp.zeros_like(total)
    product(got_ref, mixed, total, held, sems, tiles)
    first = first_ref[0] != 0
    filler = jnp.zeros((LANES - half, LANES), F32)
    for tile in range(tiles):
        at = slice(tile * LANES, (tile + 1) * LANES)
        value = folded(total, tile, tiles).astype(F32)
        for channel in range(2):
            block = jnp.concatenate([value[channel * half : (channel + 1) * half], filler])
            turned_all[channel, at, :] = block.T
        both = run[:, at] + value * last_scale
        leave[:, at] = jnp.where(first, both[half:], both[:half]).astype(BF)
        stay[:, at] = jnp.where(first, both[:half], both[half:])
    tall, spare = 2 * half, LANES - half
    high = columns.shape[2]
    for channel in range(2):
        for row in range(columns.shape[1]):
            base = turned_all[channel, row * tall : row * tall + high]
            tail = turned_all[channel, row * tall + high : (row + 1) * tall]
            side = jnp.concatenate([shifted(tail, half), shifted(tail, half - spare)])
            side = jnp.concatenate([side, jnp.zeros((high - side.shape[0], LANES), F32)])
            columns[channel, row] = jnp.where(lane_index() < half, base, side).astype(BF)


def end_kernel(half, scale, first_ref, ham_ref, stay_ref, land_ref, got_ref, out_ref):
    first = first_ref[0] != 0

    spare = LANES - half
    left_over = 2 * half - got_ref.shape[2]

    def piece(s, begin):
        block = got_ref[s % 2, s // 2].astype(F32)
        front = shifted(block[:left_over], begin - half)
        back = shifted(block[left_over : 2 * left_over], begin - half + spare)
        tail = jnp.where(lane_index() >= begin + spare, back, front)
        return jnp.concatenate([shifted(block, begin), tail])

    for tile in range(ham_ref.shape[1] // LANES):
        at = slice(tile * LANES, (tile + 1) * LANES)
        total = ham_ref[:, at].astype(F32) + laid_out(piece, half, tile) * scale
        stay, land = stay_ref[:, at], land_ref[:, at].astype(F32)
        out_ref[:half, at] = total[:half] + jnp.where(first, stay, land)
        out_ref[half:, at] = total[half:] + jnp.where(first, land, stay)


def call(kernel, out_shape, specs, name, scratch=(), cost=None):
    single = not isinstance(out_shape, (list, tuple))
    return pl.pallas_call(
        kernel,
        out_shape=out_shape,
        in_specs=specs,
        out_specs=VMEM if single else [VMEM] * len(out_shape),
        scratch_shapes=scratch,
        compiler_params=pltpu.CompilerParams(vmem_limit_bytes=(40 if scratch else 16) << 20),
        cost_estimate=cost,
        name=name,
    )


def swapped(value):
    return lax.ppermute(value, "hi", [(0, 1), (1, 0)])


def on_device(
    generator, hamiltonian, live_states, pp_occupation, ph_occupation, ph_order, recoupling
):
    row_count = generator.shape[1]
    state_count = generator.shape[2]
    half = row_count // 2
    shard_count = lax.axis_size("row")
    tiles = state_count // LANES
    sent_tiles = tiles // 2 + 1
    hi = lax.axis_index("hi")
    lo = lax.axis_index("lo")
    my_shard = lax.axis_index("row")
    first = hi == 0
    shape = jax.ShapeDtypeStruct
    r0 = recoupling[lo]
    r1 = recoupling[lo + lax.axis_size("lo")]
    positions = jnp.arange(state_count, dtype=jnp.int32)
    live_count = live_states[0]
    column_alive = positions < live_count
    row_alive = my_shard * row_count + jnp.arange(row_count, dtype=jnp.int32) < live_count
    block_alive = row_alive[:, None] & column_alive[None, :]

    share = call(
        functools.partial(pack_kernel, sent_tiles, tiles),
        shape((row_count, sent_tiles * LANES), BF),
        [SMEM, VMEM],
        "pack",
    )(jnp.stack([my_shard * row_count, live_count]), generator[0])
    both = jnp.stack([share, swapped(share)])
    gathered = lax.all_gather(both, "row", axis=0, tiled=False)
    pp = jnp.where(column_alive, pp_occupation[0], 0)
    ph = jnp.zeros((state_count,), jnp.int32).at[ph_order[0]].set(ph_occupation[0])
    ph = jnp.where(column_alive, ph, 0)
    mine = jnp.stack([pp, ph]).astype(F32)
    other = swapped(mine)
    d0, n0 = jnp.where(first, mine, other)
    d1, n1 = jnp.where(first, other, mine)
    a0 = d0 + r0[0] ** 3 * n0 + r1[1] ** 3 * n1
    a1 = d1 + r1[0] ** 3 * n1 + r0[1] ** 3 * n0
    p = r0[0] ** 2 * r0[1] * n0 + r1[1] ** 2 * r1[0] * n1
    q = r1[0] ** 2 * r1[1] * n1 + r0[1] ** 2 * r0[0] * n0
    zero_set = jnp.stack([a0, p, p, q])
    one_set = jnp.stack([p, q, q, a1])
    own_set = jnp.where(first, zero_set, one_set)
    far_set = jnp.where(first, one_set, zero_set)

    own_ham = jnp.where(block_alive, hamiltonian[0], jnp.zeros_like(hamiltonian[0]))
    keep = lax.dynamic_slice_in_dim(own_ham, hi * half, half, 0)
    gone = lax.dynamic_slice_in_dim(own_ham, (1 - hi) * half, half, 0)
    came = swapped(gone)
    current = jnp.concatenate([jnp.where(first, keep, came), jnp.where(first, came, keep)])

    wide = (tiles + sent_tiles - 1) * LANES
    rest = row_count - LANES
    destinations = 2 * shard_count
    scratch = [
        pltpu.VMEM((2, row_count, wide), BF),
        pltpu.VMEM((row_count, wide), F32),
        pltpu.VMEM((2, state_count, sent_tiles * LANES), BF),
        pltpu.SemaphoreType.DMA((2, shard_count)),
    ]
    more = [pltpu.VMEM((destinations * rest // LANES, LANES, LANES), F32)]
    c_shape = shape((row_count, state_count), BF)
    run_shape = shape((row_count, state_count), F32)
    sent_shape = shape((destinations, half + rest, LANES), BF)
    cost = pl.CostEstimate(
        flops=4 * row_count * state_count * state_count,
        bytes_accessed=gathered.size * 2,
        transcendentals=0,
    )

    def exchanged(columns):
        return lax.all_to_all(columns, ("row", "hi"), split_axis=0, concat_axis=0, tiled=True)

    combined, columns = call(
        functools.partial(first_kernel, half, tiles),
        [c_shape, sent_shape],
        [VMEM] * 3 + [HBM],
        "first",
        scratch,
        cost,
    )(current, own_set, far_set, gathered)
    back = exchanged(columns)
    combined, running, columns = call(
        functools.partial(middle_kernel, half, tiles, -1.0),
        [c_shape, run_shape, sent_shape],
        [VMEM] * 4 + [HBM],
        "middle",
        scratch + more,
        cost,
    )(combined, back, own_set, far_set, gathered)
    back = exchanged(columns)
    which = first.astype(jnp.int32)[None]
    leaving, staying, blocks = call(
        functools.partial(last_kernel, half, tiles, -0.5, -1.0 / TERMS),
        [
            shape((half, state_count), BF),
            shape((half, state_count), F32),
            shape((2, shard_count, half + rest, LANES), BF),
        ],
        [SMEM] + [VMEM] * 5 + [HBM],
        "last",
        scratch
        + more
        + [pltpu.VMEM((row_count, state_count), F32), pltpu.VMEM((2, state_count, LANES), F32)],
        cost,
    )(which, combined, back, running, own_set, far_set, gathered)
    landed = swapped(leaving)
    got = lax.all_to_all(
        blocks.reshape(destinations, half + rest, LANES),
        ("hi", "row"),
        split_axis=0,
        concat_axis=0,
        tiled=True,
    )
    result = call(
        functools.partial(end_kernel, half, -1.0 / TERMS),
        shape((row_count, state_count), F32),
        [SMEM] + [VMEM] * 4,
        "finish",
    )(which, own_ham, staying, landed, got.reshape(2, shard_count, half + rest, LANES))
    return result[None]


def solution(mesh):
    chans, rows = mesh.devices.shape
    pairs = Mesh(mesh.devices.reshape(2, chans // 2, rows), ("hi", "lo", "row"))
    chan = ("hi", "lo")
    placed = (
        P(chan, "row", None),
        P(chan, "row", None),
        P(chan),
        P(chan, None),
        P(chan, None),
        P(chan, None),
        P(),
    )
    return jax.shard_map(
        on_device, mesh=pairs, in_specs=placed, out_specs=P(chan, "row", None), check_vma=False
    )
```

```python
import functools

import jax
import jax.numpy as jnp
from jax import lax
from jax.experimental import pallas as pl
from jax.experimental.pallas import tpu as pltpu
from jax.sharding import Mesh, PartitionSpec as P

TERMS = 3
LANES = 128
STEP = 32
BF = jnp.bfloat16
F32 = jnp.float32
VMEM = pl.BlockSpec(memory_space=pltpu.VMEM)
SMEM = pl.BlockSpec(memory_space=pltpu.SMEM)
HBM = pl.BlockSpec(memory_space=pltpu.HBM)


def tile_at(index):
    return pl.ds(pl.multiple_of(index * LANES, LANES), LANES)


def pack_kernel(sent_tiles, tiles, scalars, gen_ref, out_ref):
    start, live = scalars[0], scalars[1]
    for group in range(gen_ref.shape[0] // STEP):
        rows = pl.ds(group * STEP, STEP)
        first_row = start + group * STEP
        diagonal = first_row // LANES
        row_at = first_row + lax.broadcasted_iota(jnp.int32, (STEP, LANES), 0)
        for apart in range(sent_tiles):
            tile = lax.rem(diagonal + apart, tiles)
            column_at = tile * LANES + lax.broadcasted_iota(jnp.int32, (STEP, LANES), 1)
            alive = (row_at < live) & (column_at < live)
            value = gen_ref[rows, tile_at(tile)].astype(F32)
            out_ref[rows, apart * LANES : (apart + 1) * LANES] = jnp.where(
                alive, value, 0.0
            ).astype(BF)


def shifted(value, shift):
    shift = shift % LANES
    return pltpu.roll(value, shift, 1) if shift else value


def lane_index():
    return lax.broadcasted_iota(jnp.int32, (1, LANES), 1)


def laid_out(pieces, half, tile):
    low = tile * LANES
    result = None
    for piece in range(low // half, (low + LANES - 1) // half + 1):
        begin = piece * half - low
        value = pieces(piece, begin)
        result = value if result is None else jnp.where(lane_index() >= begin, value, result)
    return result


def mix(x0, x1, own_ref, far_ref, mixed, half, tile, tiles):
    at = slice(tile * LANES, (tile + 1) * LANES)
    places = [at]
    if (tile + tiles + 1) * LANES <= mixed.shape[2]:
        places.append(slice((tile + tiles) * LANES, (tile + tiles + 1) * LANES))
    for which, weights in enumerate((own_ref, far_ref)):
        top = (x0 * weights[0:1, at] + x1 * weights[1:2, at]).astype(BF)
        low = (x0 * weights[2:3, at] + x1 * weights[3:4, at]).astype(BF)
        for place in places:
            mixed[which, :half, place] = top
            mixed[which, half:, place] = low


def product(got_ref, mixed, total, held, sems, tiles):
    pairs = tiles // 2

    def step(pair, carry):
        rows_of = got_ref.shape[2]

        def blocks_before(p):
            return (p * 2 * LANES + rows_of - 1) // rows_of

        @pl.loop(blocks_before(pair), blocks_before(pair + 1))
        def _(block):
            for which in range(2):
                block_copy(got_ref, held, sems, which, block).wait()

        even = pl.multiple_of(pair * 2 * LANES, 2 * LANES)
        odd = pl.multiple_of(even + LANES, LANES)

        def rows(which, start, low, high):
            return held[which, pl.ds(start, LANES), low * LANES : high * LANES]

        def left(apart, count):
            at = pl.ds(pl.multiple_of(even + apart * LANES, LANES), count * LANES)
            return jnp.concatenate([mixed[0, :, at], mixed[1, :, at]], 1)

        def add(apart, count, value):
            at = pl.multiple_of(even + apart * LANES, LANES)
            total[:, pl.ds(at, count * LANES)] += value

        def straight(a, parts):
            w = jnp.concatenate(parts, 0)
            return jnp.dot(a, w, preferred_element_type=F32)

        def turned(a, parts):
            w = jnp.concatenate(parts, 1)
            return lax.dot_general(a, w, (((1,), (1,)), ((), ())), preferred_element_type=F32)

        def two(start, low, high):
            return [rows(w, start, low, high) for w in range(2)]

        span = pairs
        parts = []
        for w in range(2):
            parts += [rows(w, even, 1, span + 1), rows(w, odd, 0, span)]
        add(1, span, straight(left(0, 2), parts))
        parts = [
            jnp.concatenate([rows(w, even, 2, span), rows(w, odd, 1, span - 1)], 0)
            for w in range(2)
        ]
        add(0, 2, -turned(left(2, span - 2), parts))
        near = straight(left(0, 1), two(even, 0, 1))
        add(0, 1, near - turned(left(1, 1), two(even, 1, 2)))
        add(1, 1, -turned(left(span, 1), two(odd, span - 1, span)))
        add(span + 1, 1, straight(left(1, 1), two(odd, span, span + 1)))
        return carry

    lax.fori_loop(0, pairs, step, 0)


def block_copy(got_ref, held, sems, which, block):
    rows = got_ref.shape[2]
    at = pl.multiple_of(block * rows, rows)
    return pltpu.make_async_copy(
        got_ref.at[block, which], held.at[which, pl.ds(at, rows)], sems.at[which, block]
    )


def begin(got_ref, held, sems):
    @pl.loop(0, got_ref.shape[0])
    def _(block):
        for which in range(2):
            block_copy(got_ref, held, sems, which, block).start()


def folded(total, tile, tiles):
    at = slice(tile * LANES, (tile + 1) * LANES)
    value = total[:, at]
    if (tile + tiles + 1) * LANES <= total.shape[1]:
        value = value + total[:, (tile + tiles) * LANES : (tile + tiles + 1) * LANES]
    return value.astype(BF)


def pack_columns(c_ref, columns, half):
    count = c_ref.shape[1] // half
    rest = c_ref.shape[0] - LANES
    for tile in range(c_ref.shape[1] // LANES):
        block = c_ref[:LANES, tile * LANES : (tile + 1) * LANES].astype(F32).T.astype(BF)
        step = 16
        for k in range(LANES // step):
            row = tile * LANES + k * step
            columns[row // half, row % half : row % half + step, :] = block[k * step : (k + 1) * step]
    for piece in range(count):
        tile, off = divmod(piece * half, LANES)
        tail = slice(LANES, LANES + rest)
        value = shifted(c_ref[tail, tile * LANES : (tile + 1) * LANES].astype(F32), -off)
        if off + half > LANES:
            more = c_ref[tail, (tile + 1) * LANES : (tile + 2) * LANES].astype(F32)
            value = jnp.where(lane_index() < LANES - off, value, shifted(more, -off))
        columns[piece, half : half + rest, :] = value.astype(BF)


def flipped_tiles(got_ref, turned, half, tile):
    rest = 2 * half - LANES
    group = LANES // rest
    kept = half - rest

    def near(s, begin):
        return shifted(got_ref[s, :half, :].astype(F32), begin)

    def far(s, begin):
        front = shifted(got_ref[s, :half, :].astype(F32), begin - half)
        back = turned[s // group, :half, :]
        back = shifted(back, begin + kept - rest * (s % group))
        return jnp.where(lane_index() >= begin + kept, back, front)

    return laid_out(near, half, tile), laid_out(far, half, tile)


def turn_rest(got_ref, turned, half):
    rest = 2 * half - LANES
    group = LANES // rest
    for k in range(got_ref.shape[0] // group):
        block = jnp.concatenate(
            [got_ref[k * group + m, half : half + rest, :].astype(F32) for m in range(group)], 0
        )
        turned[k] = block.T


def finish_products(c_out, total, tiles):
    for tile in range(tiles):
        c_out[:, tile * LANES : (tile + 1) * LANES] = folded(total, tile, tiles)


def first_kernel(
    half, tiles, x_ref, own_ref, far_ref, got_ref, c_out, columns, mixed, total, held, sems
):
    begin(got_ref, held, sems)
    for tile in range(tiles):
        at = slice(tile * LANES, (tile + 1) * LANES)
        x0, x1 = x_ref[:half, at].astype(F32), x_ref[half:, at].astype(F32)
        mix(x0, x1, own_ref, far_ref, mixed, half, tile, tiles)
    total[...] = jnp.zeros_like(total)
    product(got_ref, mixed, total, held, sems, tiles)
    finish_products(c_out, total, tiles)
    pack_columns(c_out, columns, half)


def update(half, tiles, scale, c_ref, back_ref, own_ref, far_ref, mixed, turned, keep):
    turn_rest(back_ref, turned, half)
    for tile in range(tiles):
        at = slice(tile * LANES, (tile + 1) * LANES)
        xs = []
        for channel, flipped in enumerate(flipped_tiles(back_ref, turned, half, tile)):
            rows = slice(channel * half, (channel + 1) * half)
            increment = (c_ref[rows, at].astype(F32) + flipped) * scale
            keep(rows, at, increment)
            xs.append(increment.astype(BF).astype(F32))
        mix(xs[0], xs[1], own_ref, far_ref, mixed, half, tile, tiles)


def middle_kernel(
    half, tiles, scale, c_ref, back_ref, own_ref, far_ref, got_ref, c_out, run_out, columns,
    mixed, total, held, sems, turned,
):
    begin(got_ref, held, sems)

    def keep(rows, at, increment):
        run_out[rows, at] = increment

    update(half, tiles, scale, c_ref, back_ref, own_ref, far_ref, mixed, turned, keep)
    total[...] = jnp.zeros_like(total)
    product(got_ref, mixed, total, held, sems, tiles)
    finish_products(c_out, total, tiles)
    pack_columns(c_out, columns, half)


def last_kernel(
    half, tiles, scale, last_scale, first_ref, c_ref, back_ref, run_ref, own_ref, far_ref, got_ref,
    leave, stay, columns, mixed, total, held, sems, turned, run, turned_all,
):
    begin(got_ref, held, sems)

    def keep(rows, at, increment):
        run[rows, at] = run_ref[rows, at] + increment

    update(half, tiles, scale, c_ref, back_ref, own_ref, far_ref, mixed, turned, keep)
    total[...] = jnp.zeros_like(total)
    product(got_ref, mixed, total, held, sems, tiles)
    first = first_ref[0] != 0
    filler = jnp.zeros((LANES - half, LANES), F32)
    for tile in range(tiles):
        at = slice(tile * LANES, (tile + 1) * LANES)
        value = folded(total, tile, tiles).astype(F32)
        for channel in range(2):
            block = jnp.concatenate([value[channel * half : (channel + 1) * half], filler])
            turned_all[channel, at, :] = block.T
        both = run[:, at] + value * last_scale
        leave[:, at] = jnp.where(first, both[half:], both[:half]).astype(BF)
        stay[:, at] = jnp.where(first, both[:half], both[half:])
    tall, spare = 2 * half, LANES - half
    high = columns.shape[2]
    for channel in range(2):
        for row in range(columns.shape[1]):
            base = turned_all[channel, row * tall : row * tall + high]
            tail = turned_all[channel, row * tall + high : (row + 1) * tall]
            side = jnp.concatenate([shifted(tail, half), shifted(tail, half - spare)])
            side = jnp.concatenate([side, jnp.zeros((high - side.shape[0], LANES), F32)])
            columns[channel, row] = jnp.where(lane_index() < half, base, side).astype(BF)


def end_kernel(half, scale, first_ref, ham_ref, stay_ref, land_ref, got_ref, out_ref):
    first = first_ref[0] != 0

    spare = LANES - half
    left_over = 2 * half - got_ref.shape[2]

    def piece(s, begin):
        block = got_ref[s % 2, s // 2].astype(F32)
        front = shifted(block[:left_over], begin - half)
        back = shifted(block[left_over : 2 * left_over], begin - half + spare)
        tail = jnp.where(lane_index() >= begin + spare, back, front)
        return jnp.concatenate([shifted(block, begin), tail])

    for tile in range(ham_ref.shape[1] // LANES):
        at = slice(tile * LANES, (tile + 1) * LANES)
        total = ham_ref[:, at].astype(F32) + laid_out(piece, half, tile) * scale
        stay, land = stay_ref[:, at], land_ref[:, at].astype(F32)
        out_ref[:half, at] = total[:half] + jnp.where(first, stay, land)
        out_ref[half:, at] = total[half:] + jnp.where(first, land, stay)


def call(kernel, out_shape, specs, name, scratch=(), cost=None):
    single = not isinstance(out_shape, (list, tuple))
    return pl.pallas_call(
        kernel,
        out_shape=out_shape,
        in_specs=specs,
        out_specs=VMEM if single else [VMEM] * len(out_shape),
        scratch_shapes=scratch,
        compiler_params=pltpu.CompilerParams(vmem_limit_bytes=(40 if scratch else 16) << 20),
        cost_estimate=cost,
        name=name,
    )


def swapped(value):
    return lax.ppermute(value, "hi", [(0, 1), (1, 0)])


def on_device(
    generator, hamiltonian, live_states, pp_occupation, ph_occupation, ph_order, recoupling
):
    row_count = generator.shape[1]
    state_count = generator.shape[2]
    half = row_count // 2
    shard_count = lax.axis_size("row")
    tiles = state_count // LANES
    sent_tiles = tiles // 2 + 1
    hi = lax.axis_index("hi")
    lo = lax.axis_index("lo")
    my_shard = lax.axis_index("row")
    first = hi == 0
    shape = jax.ShapeDtypeStruct
    r0 = recoupling[lo]
    r1 = recoupling[lo + lax.axis_size("lo")]
    positions = jnp.arange(state_count, dtype=jnp.int32)
    live_count = live_states[0]
    column_alive = positions < live_count
    row_alive = my_shard * row_count + jnp.arange(row_count, dtype=jnp.int32) < live_count
    block_alive = row_alive[:, None] & column_alive[None, :]

    share = call(
        functools.partial(pack_kernel, sent_tiles, tiles),
        shape((row_count, sent_tiles * LANES), BF),
        [SMEM, VMEM],
        "pack",
    )(jnp.stack([my_shard * row_count, live_count]), generator[0])
    both = jnp.stack([share, swapped(share)])
    gathered = lax.all_gather(both, "row", axis=0, tiled=False)
    pp = jnp.where(column_alive, pp_occupation[0], 0)
    ph = jnp.zeros((state_count,), jnp.int32).at[ph_order[0]].set(ph_occupation[0])
    ph = jnp.where(column_alive, ph, 0)
    mine = jnp.stack([pp, ph]).astype(F32)
    other = swapped(mine)
    d0, n0 = jnp.where(first, mine, other)
    d1, n1 = jnp.where(first, other, mine)
    a0 = d0 + r0[0] ** 3 * n0 + r1[1] ** 3 * n1
    a1 = d1 + r1[0] ** 3 * n1 + r0[1] ** 3 * n0
    p = r0[0] ** 2 * r0[1] * n0 + r1[1] ** 2 * r1[0] * n1
    q = r1[0] ** 2 * r1[1] * n1 + r0[1] ** 2 * r0[0] * n0
    zero_set = jnp.stack([a0, p, p, q])
    one_set = jnp.stack([p, q, q, a1])
    own_set = jnp.where(first, zero_set, one_set)
    far_set = jnp.where(first, one_set, zero_set)

    own_ham = jnp.where(block_alive, hamiltonian[0], jnp.zeros_like(hamiltonian[0]))
    keep = lax.dynamic_slice_in_dim(own_ham, hi * half, half, 0)
    gone = lax.dynamic_slice_in_dim(own_ham, (1 - hi) * half, half, 0)
    came = swapped(gone)
    current = jnp.concatenate([jnp.where(first, keep, came), jnp.where(first, came, keep)])

    wide = (tiles + sent_tiles - 1) * LANES
    rest = row_count - LANES
    destinations = 2 * shard_count
    scratch = [
        pltpu.VMEM((2, row_count, wide), BF),
        pltpu.VMEM((row_count, wide), F32),
        pltpu.VMEM((2, state_count, sent_tiles * LANES), BF),
        pltpu.SemaphoreType.DMA((2, shard_count)),
    ]
    more = [pltpu.VMEM((destinations * rest // LANES, LANES, LANES), F32)]
    c_shape = shape((row_count, state_count), BF)
    run_shape = shape((row_count, state_count), F32)
    sent_shape = shape((destinations, half + rest, LANES), BF)
    cost = pl.CostEstimate(
        flops=4 * row_count * state_count * state_count,
        bytes_accessed=gathered.size * 2,
        transcendentals=0,
    )

    def exchanged(columns):
        return lax.all_to_all(columns, ("row", "hi"), split_axis=0, concat_axis=0, tiled=True)

    combined, columns = call(
        functools.partial(first_kernel, half, tiles),
        [c_shape, sent_shape],
        [VMEM] * 3 + [HBM],
        "first",
        scratch,
        cost,
    )(current, own_set, far_set, gathered)
    back = exchanged(columns)
    combined, running, columns = call(
        functools.partial(middle_kernel, half, tiles, -1.0),
        [c_shape, run_shape, sent_shape],
        [VMEM] * 4 + [HBM],
        "middle",
        scratch + more,
        cost,
    )(combined, back, own_set, far_set, gathered)
    back = exchanged(columns)
    which = first.astype(jnp.int32)[None]
    leaving, staying, blocks = call(
        functools.partial(last_kernel, half, tiles, -0.5, -1.0 / TERMS),
        [
            shape((half, state_count), BF),
            shape((half, state_count), F32),
            shape((2, shard_count, half + rest, LANES), BF),
        ],
        [SMEM] + [VMEM] * 5 + [HBM],
        "last",
        scratch
        + more
        + [pltpu.VMEM((row_count, state_count), F32), pltpu.VMEM((2, state_count, LANES), F32)],
        cost,
    )(which, combined, back, running, own_set, far_set, gathered)
    landed = swapped(leaving)
    got = lax.all_to_all(
        blocks.reshape(destinations, half + rest, LANES),
        ("hi", "row"),
        split_axis=0,
        concat_axis=0,
        tiled=True,
    )
    result = call(
        functools.partial(end_kernel, half, -1.0 / TERMS),
        shape((row_count, state_count), F32),
        [SMEM] + [VMEM] * 4,
        "finish",
    )(which, own_ham, staying, landed, got.reshape(2, shard_count, half + rest, LANES))
    return result[None]


def solution(mesh):
    chans, rows = mesh.devices.shape
    pairs = Mesh(mesh.devices.reshape(2, chans // 2, rows), ("hi", "lo", "row"))
    chan = ("hi", "lo")
    placed = (
        P(chan, "row", None),
        P(chan, "row", None),
        P(chan),
        P(chan, None),
        P(chan, None),
        P(chan, None),
        P(),
    )
    return jax.shard_map(
        on_device, mesh=pairs, in_specs=placed, out_specs=P(chan, "row", None), check_vma=False
    )
```

```python
import functools
import math

import jax
import jax.numpy as jnp
from jax import lax
from jax.experimental import pallas as pl
from jax.experimental.pallas import tpu as pltpu
from jax.sharding import Mesh, PartitionSpec as P

TERMS = 3
ROW = ("y", "z")
LANES = 128
STEP = 32
BF = jnp.bfloat16
F32 = jnp.float32
VMEM = pl.BlockSpec(memory_space=pltpu.VMEM)
SMEM = pl.BlockSpec(memory_space=pltpu.SMEM)
HBM = pl.BlockSpec(memory_space=pltpu.HBM)


def tile_at(index):
    return pl.ds(pl.multiple_of(index * LANES, LANES), LANES)


def pack_kernel(sent_tiles, tiles, scalars, gen_ref, out_ref):
    start, live = scalars[0], scalars[1]
    for group in range(gen_ref.shape[0] // STEP):
        rows = pl.ds(group * STEP, STEP)
        first_row = start + group * STEP
        diagonal = first_row // LANES
        row_at = first_row + lax.broadcasted_iota(jnp.int32, (STEP, LANES), 0)
        for apart in range(sent_tiles):
            tile = lax.rem(diagonal + apart, tiles)
            column_at = tile * LANES + lax.broadcasted_iota(jnp.int32, (STEP, LANES), 1)
            alive = (row_at < live) & (column_at < live)
            value = gen_ref[rows, tile_at(tile)].astype(F32)
            out_ref[rows, apart * LANES : (apart + 1) * LANES] = jnp.where(
                alive, value, 0.0
            ).astype(BF)


def shifted(value, shift):
    shift = shift % LANES
    return pltpu.roll(value, shift, 1) if shift else value


def lane_index():
    return lax.broadcasted_iota(jnp.int32, (1, LANES), 1)


def laid_out(pieces, half, tile):
    low = tile * LANES
    result = None
    for piece in range(low // half, (low + LANES - 1) // half + 1):
        begin = piece * half - low
        value = pieces(piece, begin)
        result = value if result is None else jnp.where(lane_index() >= begin, value, result)
    return result


def mix(x0, x1, own_ref, far_ref, mixed, half, tile, tiles):
    at = slice(tile * LANES, (tile + 1) * LANES)
    places = [at]
    if (tile + tiles + 1) * LANES <= mixed.shape[2]:
        places.append(slice((tile + tiles) * LANES, (tile + tiles + 1) * LANES))
    for which, weights in enumerate((own_ref, far_ref)):
        top = (x0 * weights[0:1, at] + x1 * weights[1:2, at]).astype(BF)
        low = (x0 * weights[2:3, at] + x1 * weights[3:4, at]).astype(BF)
        for place in places:
            mixed[which, :half, place] = top
            mixed[which, half:, place] = low


def product(got, mixed, total, held, sems, tiles):
    pairs = tiles // 2

    def step(pair, carry):
        rows_of = got[0].shape[1]

        def blocks_before(p):
            return (p * 2 * LANES + rows_of - 1) // rows_of

        @pl.loop(blocks_before(pair), blocks_before(pair + 1))
        def _(block):
            for which in range(2):
                block_copy(got, held, sems, which, block).wait()

        even = pl.multiple_of(pair * 2 * LANES, 2 * LANES)
        odd = pl.multiple_of(even + LANES, LANES)

        def rows(which, start, low, high):
            return held[which, pl.ds(start, LANES), low * LANES : high * LANES]

        def left(apart, count):
            at = pl.ds(pl.multiple_of(even + apart * LANES, LANES), count * LANES)
            return jnp.concatenate([mixed[0, :, at], mixed[1, :, at]], 1)

        def add(apart, count, value):
            at = pl.multiple_of(even + apart * LANES, LANES)
            total[:, pl.ds(at, count * LANES)] += value

        def straight(a, parts):
            w = jnp.concatenate(parts, 0)
            return jnp.dot(a, w, preferred_element_type=F32)

        def turned(a, parts):
            w = jnp.concatenate(parts, 1)
            return lax.dot_general(a, w, (((1,), (1,)), ((), ())), preferred_element_type=F32)

        def two(start, low, high):
            return [rows(w, start, low, high) for w in range(2)]

        span = pairs
        parts = []
        for w in range(2):
            parts += [rows(w, even, 1, span + 1), rows(w, odd, 0, span)]
        add(1, span, straight(left(0, 2), parts))
        parts = [
            jnp.concatenate([rows(w, even, 2, span), rows(w, odd, 1, span - 1)], 0)
            for w in range(2)
        ]
        add(0, 2, -turned(left(2, span - 2), parts))
        near = straight(left(0, 1), two(even, 0, 1))
        add(0, 1, near - turned(left(1, 1), two(even, 1, 2)))
        add(1, 1, -turned(left(span, 1), two(odd, span - 1, span)))
        add(span + 1, 1, straight(left(1, 1), two(odd, span, span + 1)))
        return carry

    lax.fori_loop(0, pairs, step, 0)


NEAR = (0, -1)
REST = (1, 2)
APART = (0, -1, 1, 2)


def collect_kernel(place, *refs):
    *got, out, sems = refs
    half = got[0].shape[0] // 2
    y, z, side = place[0], place[1], place[2]
    copies = []
    buffer = 0
    for part in range(2):
        for near in (NEAR, REST):
            for second in APART:
                for piece, first in enumerate(near):
                    dy, dz = (first, second) if part == 0 else (second, first)
                    row = lax.rem(y + dy + side, side)
                    column = lax.rem(z + dz + side, side)
                    copies.append(
                        pltpu.make_async_copy(
                            got[buffer].at[piece * half : (piece + 1) * half],
                            out.at[row * side + column, part * half : (part + 1) * half],
                            sems.at[len(copies)],
                        )
                    )
                buffer += 1
    for copy in copies:
        copy.start()
    for copy in copies:
        copy.wait()


def block_copy(got, held, sems, which, block):
    rows = got[which].shape[1]
    at = pl.multiple_of(block * rows, rows)
    return pltpu.make_async_copy(
        got[which].at[block], held.at[which, pl.ds(at, rows)], sems.at[which, block]
    )


def begin(got, held, sems):
    @pl.loop(0, got[0].shape[0])
    def _(block):
        for which in range(2):
            block_copy(got, held, sems, which, block).start()


def folded(total, tile, tiles):
    at = slice(tile * LANES, (tile + 1) * LANES)
    value = total[:, at]
    if (tile + tiles + 1) * LANES <= total.shape[1]:
        value = value + total[:, (tile + tiles) * LANES : (tile + tiles + 1) * LANES]
    return value.astype(BF)


def pack_columns(c_ref, columns, half):
    count = c_ref.shape[1] // half
    rest = c_ref.shape[0] - LANES
    for tile in range(c_ref.shape[1] // LANES):
        block = c_ref[:LANES, tile * LANES : (tile + 1) * LANES].astype(F32).T.astype(BF)
        step = 16
        for k in range(LANES // step):
            row = tile * LANES + k * step
            columns[row // half, row % half : row % half + step, :] = block[k * step : (k + 1) * step]
    for piece in range(count):
        tile, off = divmod(piece * half, LANES)
        tail = slice(LANES, LANES + rest)
        value = shifted(c_ref[tail, tile * LANES : (tile + 1) * LANES].astype(F32), -off)
        if off + half > LANES:
            more = c_ref[tail, (tile + 1) * LANES : (tile + 2) * LANES].astype(F32)
            value = jnp.where(lane_index() < LANES - off, value, shifted(more, -off))
        columns[piece, half : half + rest, :] = value.astype(BF)


def flipped_tiles(got_ref, turned, half, tile):
    rest = 2 * half - LANES
    group = LANES // rest
    kept = half - rest

    def near(s, begin):
        return shifted(got_ref[s, :half, :].astype(F32), begin)

    def far(s, begin):
        front = shifted(got_ref[s, :half, :].astype(F32), begin - half)
        back = turned[s // group, :half, :]
        back = shifted(back, begin + kept - rest * (s % group))
        return jnp.where(lane_index() >= begin + kept, back, front)

    return laid_out(near, half, tile), laid_out(far, half, tile)


def turn_rest(got_ref, turned, half):
    rest = 2 * half - LANES
    group = LANES // rest
    for k in range(got_ref.shape[0] // group):
        block = jnp.concatenate(
            [got_ref[k * group + m, half : half + rest, :].astype(F32) for m in range(group)], 0
        )
        turned[k] = block.T


def finish_products(c_out, total, tiles):
    for tile in range(tiles):
        c_out[:, tile * LANES : (tile + 1) * LANES] = folded(total, tile, tiles)


def first_kernel(half, tiles, place, x_ref, own_ref, far_ref, *refs):
    *got, c_out, columns, mixed, total, held, sems = refs
    begin(got, held, sems)
    for tile in range(tiles):
        at = slice(tile * LANES, (tile + 1) * LANES)
        x0, x1 = x_ref[:half, at].astype(F32), x_ref[half:, at].astype(F32)
        mix(x0, x1, own_ref, far_ref, mixed, half, tile, tiles)
    total[...] = jnp.zeros_like(total)
    product(got, mixed, total, held, sems, tiles)
    finish_products(c_out, total, tiles)
    pack_columns(c_out, columns, half)


def update(half, tiles, scale, c_ref, back_ref, own_ref, far_ref, mixed, turned, keep):
    turn_rest(back_ref, turned, half)
    for tile in range(tiles):
        at = slice(tile * LANES, (tile + 1) * LANES)
        xs = []
        for channel, flipped in enumerate(flipped_tiles(back_ref, turned, half, tile)):
            rows = slice(channel * half, (channel + 1) * half)
            increment = (c_ref[rows, at].astype(F32) + flipped) * scale
            keep(rows, at, increment)
            xs.append(increment.astype(BF).astype(F32))
        mix(xs[0], xs[1], own_ref, far_ref, mixed, half, tile, tiles)


def middle_kernel(half, tiles, scale, place, c_ref, back_ref, own_ref, far_ref, *refs):
    *got, c_out, run_out, columns, mixed, total, held, sems, turned = refs
    begin(got, held, sems)

    def keep(rows, at, increment):
        run_out[rows, at] = increment

    update(half, tiles, scale, c_ref, back_ref, own_ref, far_ref, mixed, turned, keep)
    total[...] = jnp.zeros_like(total)
    product(got, mixed, total, held, sems, tiles)
    finish_products(c_out, total, tiles)
    pack_columns(c_out, columns, half)


def last_kernel(
    half, tiles, scale, last_scale, place, c_ref, back_ref, run_ref, own_ref, far_ref, *refs
):
    *got, leave, stay, columns, mixed, total, held, sems, turned, run, turned_all = refs
    begin(got, held, sems)

    def keep(rows, at, increment):
        run[rows, at] = run_ref[rows, at] + increment

    update(half, tiles, scale, c_ref, back_ref, own_ref, far_ref, mixed, turned, keep)
    total[...] = jnp.zeros_like(total)
    product(got, mixed, total, held, sems, tiles)
    first = place[3] != 0
    filler = jnp.zeros((LANES - half, LANES), F32)
    for tile in range(tiles):
        at = slice(tile * LANES, (tile + 1) * LANES)
        value = folded(total, tile, tiles).astype(F32)
        for channel in range(2):
            block = jnp.concatenate([value[channel * half : (channel + 1) * half], filler])
            turned_all[channel, at, :] = block.T
        both = run[:, at] + value * last_scale
        leave[:, at] = jnp.where(first, both[half:], both[:half]).astype(BF)
        stay[:, at] = jnp.where(first, both[:half], both[half:])
    tall, spare = 2 * half, LANES - half
    high = columns.shape[2]
    for channel in range(2):
        for row in range(columns.shape[1]):
            base = turned_all[channel, row * tall : row * tall + high]
            tail = turned_all[channel, row * tall + high : (row + 1) * tall]
            side = jnp.concatenate([shifted(tail, half), shifted(tail, half - spare)])
            side = jnp.concatenate([side, jnp.zeros((high - side.shape[0], LANES), F32)])
            columns[channel, row] = jnp.where(lane_index() < half, base, side).astype(BF)


def end_kernel(half, scale, first_ref, ham_ref, stay_ref, land_ref, got_ref, out_ref):
    first = first_ref[0] != 0

    spare = LANES - half
    left_over = 2 * half - got_ref.shape[2]

    def piece(s, begin):
        block = got_ref[s % 2, s // 2].astype(F32)
        front = shifted(block[:left_over], begin - half)
        back = shifted(block[left_over : 2 * left_over], begin - half + spare)
        tail = jnp.where(lane_index() >= begin + spare, back, front)
        return jnp.concatenate([shifted(block, begin), tail])

    for tile in range(ham_ref.shape[1] // LANES):
        at = slice(tile * LANES, (tile + 1) * LANES)
        total = ham_ref[:, at].astype(F32) + laid_out(piece, half, tile) * scale
        stay, land = stay_ref[:, at], land_ref[:, at].astype(F32)
        out_ref[:half, at] = total[:half] + jnp.where(first, stay, land)
        out_ref[half:, at] = total[half:] + jnp.where(first, land, stay)


def call(kernel, out_shape, specs, name, scratch=(), cost=None, megabytes=16):
    single = not isinstance(out_shape, (list, tuple))
    return pl.pallas_call(
        kernel,
        out_shape=out_shape,
        in_specs=specs,
        out_specs=VMEM if single else [VMEM] * len(out_shape),
        scratch_shapes=scratch,
        compiler_params=pltpu.CompilerParams(vmem_limit_bytes=megabytes << 20),
        cost_estimate=cost,
        name=name,
    )


def passed(value, axis, apart):
    size = lax.axis_size(axis)
    return lax.ppermute(value, axis, [(i, (i + apart) % size) for i in range(size)])


def both_ways(value, one, other):
    by_one = {0: value, -1: passed(value, one, 1), 1: passed(value, one, -1)}
    by_one[2] = passed(value, one, 2)
    near = jnp.concatenate([by_one[k] for k in NEAR])
    rest = jnp.concatenate([by_one[k] for k in REST])
    near_up, near_down = passed(near, other, 1), passed(near, other, -1)
    rest_up, rest_down = passed(rest, other, 1), passed(rest, other, -1)
    return [
        near, near_up, near_down, passed(near_up, other, 1),
        rest, rest_up, rest_down, passed(rest_down, other, -1),
    ]


def swapped(value):
    return lax.ppermute(value, "hi", [(0, 1), (1, 0)])


def on_device(
    generator, hamiltonian, live_states, pp_occupation, ph_occupation, ph_order, recoupling
):
    row_count = generator.shape[1]
    state_count = generator.shape[2]
    half = row_count // 2
    shard_count = (lax.axis_size("y") * lax.axis_size("z"))
    tiles = state_count // LANES
    sent_tiles = tiles // 2 + 1
    hi = lax.axis_index("hi")
    lo = lax.axis_index("lo")
    my_shard = lax.axis_index(ROW)
    first = hi == 0
    shape = jax.ShapeDtypeStruct
    r0 = recoupling[lo]
    r1 = recoupling[lo + lax.axis_size("lo")]
    positions = jnp.arange(state_count, dtype=jnp.int32)
    live_count = live_states[0]
    column_alive = positions < live_count
    row_alive = my_shard * row_count + jnp.arange(row_count, dtype=jnp.int32) < live_count
    block_alive = row_alive[:, None] & column_alive[None, :]

    share = call(
        functools.partial(pack_kernel, sent_tiles, tiles),
        shape((row_count, sent_tiles * LANES), BF),
        [SMEM, VMEM],
        "pack",
    )(jnp.stack([my_shard * row_count, live_count]), generator[0])
    far_share = swapped(share)
    gathered = lax.all_gather(share, ROW, axis=0, tiled=False)
    pieces = both_ways(far_share[:half], "y", "z") + both_ways(far_share[half:], "z", "y")
    place = jnp.stack(
        [lax.axis_index("y"), lax.axis_index("z"), lax.axis_size("y"), first.astype(jnp.int32)]
    ).astype(jnp.int32)
    collected = pl.pallas_call(
        collect_kernel,
        out_shape=shape(gathered.shape, BF),
        in_specs=[SMEM] + [pl.BlockSpec(memory_space=pl.ANY)] * len(pieces),
        out_specs=HBM,
        scratch_shapes=[pltpu.SemaphoreType.DMA((2 * len(pieces),))],
        compiler_params=pltpu.CompilerParams(vmem_limit_bytes=50 << 20),
        name="collect",
    )(place, *pieces)
    gathered = [gathered, collected]

    pp = jnp.where(column_alive, pp_occupation[0], 0)
    ph = jnp.zeros((state_count,), jnp.int32).at[ph_order[0]].set(ph_occupation[0])
    ph = jnp.where(column_alive, ph, 0)
    mine = jnp.stack([pp, ph]).astype(F32)
    other = swapped(mine)
    d0, n0 = jnp.where(first, mine, other)
    d1, n1 = jnp.where(first, other, mine)
    a0 = d0 + r0[0] ** 3 * n0 + r1[1] ** 3 * n1
    a1 = d1 + r1[0] ** 3 * n1 + r0[1] ** 3 * n0
    p = r0[0] ** 2 * r0[1] * n0 + r1[1] ** 2 * r1[0] * n1
    q = r1[0] ** 2 * r1[1] * n1 + r0[1] ** 2 * r0[0] * n0
    zero_set = jnp.stack([a0, p, p, q])
    one_set = jnp.stack([p, q, q, a1])
    own_set = jnp.where(first, zero_set, one_set)
    far_set = jnp.where(first, one_set, zero_set)

    own_ham = jnp.where(block_alive, hamiltonian[0], jnp.zeros_like(hamiltonian[0]))
    keep = lax.dynamic_slice_in_dim(own_ham, hi * half, half, 0)
    gone = lax.dynamic_slice_in_dim(own_ham, (1 - hi) * half, half, 0)
    came = swapped(gone)
    current = jnp.concatenate([jnp.where(first, keep, came), jnp.where(first, came, keep)])

    wide = (tiles + sent_tiles - 1) * LANES
    rest = row_count - LANES
    destinations = 2 * shard_count
    scratch = [
        pltpu.VMEM((2, row_count, wide), BF),
        pltpu.VMEM((row_count, wide), F32),
        pltpu.VMEM((2, state_count, sent_tiles * LANES), BF),
        pltpu.SemaphoreType.DMA((2, shard_count)),
    ]
    more = [pltpu.VMEM((destinations * rest // LANES, LANES, LANES), F32)]
    c_shape = shape((row_count, state_count), BF)
    run_shape = shape((row_count, state_count), F32)
    sent_shape = shape((destinations, half + rest, LANES), BF)
    cost = pl.CostEstimate(
        flops=4 * row_count * state_count * state_count,
        bytes_accessed=4 * state_count * sent_tiles * LANES,
        transcendentals=0,
    )

    def exchanged(columns):
        return lax.all_to_all(columns, ("y", "z", "hi"), split_axis=0, concat_axis=0, tiled=True)

    combined, columns = call(
        functools.partial(first_kernel, half, tiles),
        [c_shape, sent_shape],
        [SMEM] + [VMEM] * 3 + [HBM] * len(gathered),
        "first",
        scratch,
        cost,
        52,
    )(place, current, own_set, far_set, *gathered)
    back = exchanged(columns)
    combined, running, columns = call(
        functools.partial(middle_kernel, half, tiles, -1.0),
        [c_shape, run_shape, sent_shape],
        [SMEM] + [VMEM] * 4 + [HBM] * len(gathered),
        "middle",
        scratch + more,
        cost,
        52,
    )(place, combined, back, own_set, far_set, *gathered)
    back = exchanged(columns)
    which = first.astype(jnp.int32)[None]
    leaving, staying, blocks = call(
        functools.partial(last_kernel, half, tiles, -0.5, -1.0 / TERMS),
        [
            shape((half, state_count), BF),
            shape((half, state_count), F32),
            shape((2, shard_count, half + rest, LANES), BF),
        ],
        [SMEM] + [VMEM] * 5 + [HBM] * len(gathered),
        "last",
        scratch
        + more
        + [pltpu.VMEM((row_count, state_count), F32), pltpu.VMEM((2, state_count, LANES), F32)],
        cost,
        52,
    )(place, combined, back, running, own_set, far_set, *gathered)
    landed = swapped(leaving)
    got = lax.all_to_all(
        blocks.reshape(destinations, half + rest, LANES),
        ("hi", "y", "z"),
        split_axis=0,
        concat_axis=0,
        tiled=True,
    )
    result = call(
        functools.partial(end_kernel, half, -1.0 / TERMS),
        shape((row_count, state_count), F32),
        [SMEM] + [VMEM] * 4,
        "finish",
    )(which, own_ham, staying, landed, got.reshape(2, shard_count, half + rest, LANES))
    return result[None]


def solution(mesh):
    chans, rows = mesh.devices.shape
    side = math.isqrt(rows)
    pairs = Mesh(
        mesh.devices.reshape(2, chans // 2, side, rows // side), ("hi", "lo", "y", "z")
    )
    chan = ("hi", "lo")
    placed = (
        P(chan, ROW, None),
        P(chan, ROW, None),
        P(chan),
        P(chan, None),
        P(chan, None),
        P(chan, None),
        P(),
    )
    return jax.shard_map(
        on_device, mesh=pairs, in_specs=placed, out_specs=P(chan, ROW, None), check_vma=False
    )
```

```python
import functools
import math

import jax
import jax.numpy as jnp
from jax import lax
from jax.experimental import pallas as pl
from jax.experimental.pallas import tpu as pltpu
from jax.sharding import Mesh, PartitionSpec as P

TERMS = 3
ROW = ("y", "z")
LANES = 128
STEP = 32
BF = jnp.bfloat16
F32 = jnp.float32
VMEM = pl.BlockSpec(memory_space=pltpu.VMEM)
SMEM = pl.BlockSpec(memory_space=pltpu.SMEM)
HBM = pl.BlockSpec(memory_space=pltpu.HBM)


def tile_at(index):
    return pl.ds(pl.multiple_of(index * LANES, LANES), LANES)


def pack_kernel(sent_tiles, tiles, scalars, gen_ref, out_ref):
    start, live = scalars[0], scalars[1]
    for group in range(gen_ref.shape[0] // STEP):
        rows = pl.ds(group * STEP, STEP)
        first_row = start + group * STEP
        diagonal = first_row // LANES
        row_at = first_row + lax.broadcasted_iota(jnp.int32, (STEP, LANES), 0)
        for apart in range(sent_tiles):
            tile = lax.rem(diagonal + apart, tiles)
            column_at = tile * LANES + lax.broadcasted_iota(jnp.int32, (STEP, LANES), 1)
            alive = (row_at < live) & (column_at < live)
            value = gen_ref[rows, tile_at(tile)].astype(F32)
            out_ref[rows, apart * LANES : (apart + 1) * LANES] = jnp.where(
                alive, value, 0.0
            ).astype(BF)


def shifted(value, shift):
    shift = shift % LANES
    return pltpu.roll(value, shift, 1) if shift else value


def lane_index():
    return lax.broadcasted_iota(jnp.int32, (1, LANES), 1)


def laid_out(pieces, half, tile):
    low = tile * LANES
    result = None
    for piece in range(low // half, (low + LANES - 1) // half + 1):
        begin = piece * half - low
        value = pieces(piece, begin)
        result = value if result is None else jnp.where(lane_index() >= begin, value, result)
    return result


def mix(x0, x1, own_ref, far_ref, mixed, half, tile, tiles):
    at = slice(tile * LANES, (tile + 1) * LANES)
    places = [at]
    if (tile + tiles + 1) * LANES <= mixed.shape[2]:
        places.append(slice((tile + tiles) * LANES, (tile + tiles + 1) * LANES))
    for which, weights in enumerate((own_ref, far_ref)):
        top = (x0 * weights[0:1, at] + x1 * weights[1:2, at]).astype(BF)
        low = (x0 * weights[2:3, at] + x1 * weights[3:4, at]).astype(BF)
        for place in places:
            mixed[which, :half, place] = top
            mixed[which, half:, place] = low


def product(got, mixed, total, held, sems, tiles):
    pairs = tiles // 2

    def step(pair, carry):
        rows_of = got[0].shape[1]

        def blocks_before(p):
            return (p * 2 * LANES + rows_of - 1) // rows_of

        @pl.loop(blocks_before(pair), blocks_before(pair + 1))
        def _(block):
            for which in range(2):
                block_copy(got, held, sems, which, block).wait()

        even = pl.multiple_of(pair * 2 * LANES, 2 * LANES)
        odd = pl.multiple_of(even + LANES, LANES)

        def rows(which, start, low, high):
            return held[which, pl.ds(start, LANES), low * LANES : high * LANES]

        def left(apart, count):
            at = pl.ds(pl.multiple_of(even + apart * LANES, LANES), count * LANES)
            return jnp.concatenate([mixed[0, :, at], mixed[1, :, at]], 1)

        def add(apart, count, value):
            at = pl.multiple_of(even + apart * LANES, LANES)
            total[:, pl.ds(at, count * LANES)] += value

        def straight(a, parts):
            w = jnp.concatenate(parts, 0)
            return jnp.dot(a, w, preferred_element_type=F32)

        def turned(a, parts):
            w = jnp.concatenate(parts, 1)
            return lax.dot_general(a, w, (((1,), (1,)), ((), ())), preferred_element_type=F32)

        def two(start, low, high):
            return [rows(w, start, low, high) for w in range(2)]

        span = pairs
        parts = []
        for w in range(2):
            parts += [rows(w, even, 1, span + 1), rows(w, odd, 0, span)]
        add(1, span, straight(left(0, 2), parts))
        parts = [
            jnp.concatenate([rows(w, even, 2, span), rows(w, odd, 1, span - 1)], 0)
            for w in range(2)
        ]
        add(0, 2, -turned(left(2, span - 2), parts))
        near = straight(left(0, 1), two(even, 0, 1))
        add(0, 1, near - turned(left(1, 1), two(even, 1, 2)))
        add(1, 1, -turned(left(span, 1), two(odd, span - 1, span)))
        add(span + 1, 1, straight(left(1, 1), two(odd, span, span + 1)))
        return carry

    lax.fori_loop(0, pairs, step, 0)


NEAR = (0, -1)
REST = (1, 2)
APART = (0, -1, 1, 2)


def collect_kernel(place, *refs):
    *got, out, sems = refs
    half = got[0].shape[0] // 2
    y, z, side = place[0], place[1], place[2]
    copies = []
    buffer = 0
    for part in range(2):
        for near in (NEAR, REST):
            for second in APART:
                for piece, first in enumerate(near):
                    dy, dz = (first, second) if part == 0 else (second, first)
                    row = lax.rem(y + dy + side, side)
                    column = lax.rem(z + dz + side, side)
                    copies.append(
                        pltpu.make_async_copy(
                            got[buffer].at[piece * half : (piece + 1) * half],
                            out.at[row * side + column, part * half : (part + 1) * half],
                            sems.at[len(copies)],
                        )
                    )
                buffer += 1
    for copy in copies:
        copy.start()
    for copy in copies:
        copy.wait()


def block_copy(got, held, sems, which, block):
    rows = got[which].shape[1]
    at = pl.multiple_of(block * rows, rows)
    return pltpu.make_async_copy(
        got[which].at[block], held.at[which, pl.ds(at, rows)], sems.at[which, block]
    )


def begin(got, held, sems):
    @pl.loop(0, got[0].shape[0])
    def _(block):
        for which in range(2):
            block_copy(got, held, sems, which, block).start()


def folded(total, tile, tiles):
    at = slice(tile * LANES, (tile + 1) * LANES)
    value = total[:, at]
    if (tile + tiles + 1) * LANES <= total.shape[1]:
        value = value + total[:, (tile + tiles) * LANES : (tile + tiles + 1) * LANES]
    return value.astype(BF)


def pack_columns(c_ref, columns, half):
    count = c_ref.shape[1] // half
    rest = c_ref.shape[0] - LANES
    for tile in range(c_ref.shape[1] // LANES):
        block = c_ref[:LANES, tile * LANES : (tile + 1) * LANES].astype(F32).T.astype(BF)
        step = 16
        for k in range(LANES // step):
            row = tile * LANES + k * step
            columns[row // half, row % half : row % half + step, :] = block[k * step : (k + 1) * step]
    for piece in range(count):
        tile, off = divmod(piece * half, LANES)
        tail = slice(LANES, LANES + rest)
        value = shifted(c_ref[tail, tile * LANES : (tile + 1) * LANES].astype(F32), -off)
        if off + half > LANES:
            more = c_ref[tail, (tile + 1) * LANES : (tile + 2) * LANES].astype(F32)
            value = jnp.where(lane_index() < LANES - off, value, shifted(more, -off))
        columns[piece, half : half + rest, :] = value.astype(BF)


def flipped_tiles(got_ref, turned, half, tile):
    rest = 2 * half - LANES
    group = LANES // rest
    kept = half - rest

    def near(s, begin):
        return shifted(got_ref[s, :half, :].astype(F32), begin)

    def far(s, begin):
        front = shifted(got_ref[s, :half, :].astype(F32), begin - half)
        back = turned[s // group, :half, :]
        back = shifted(back, begin + kept - rest * (s % group))
        return jnp.where(lane_index() >= begin + kept, back, front)

    return laid_out(near, half, tile), laid_out(far, half, tile)


def turn_rest(got_ref, turned, half):
    rest = 2 * half - LANES
    group = LANES // rest
    for k in range(got_ref.shape[0] // group):
        block = jnp.concatenate(
            [got_ref[k * group + m, half : half + rest, :].astype(F32) for m in range(group)], 0
        )
        turned[k] = block.T


def finish_products(c_out, total, tiles):
    for tile in range(tiles):
        c_out[:, tile * LANES : (tile + 1) * LANES] = folded(total, tile, tiles)


def first_kernel(half, tiles, place, x_ref, own_ref, far_ref, *refs):
    *got, c_out, columns, mixed, total, held, sems = refs
    begin(got, held, sems)
    for tile in range(tiles):
        at = slice(tile * LANES, (tile + 1) * LANES)
        x0, x1 = x_ref[:half, at].astype(F32), x_ref[half:, at].astype(F32)
        mix(x0, x1, own_ref, far_ref, mixed, half, tile, tiles)
    total[...] = jnp.zeros_like(total)
    product(got, mixed, total, held, sems, tiles)
    finish_products(c_out, total, tiles)
    pack_columns(c_out, columns, half)


def update(half, tiles, scale, c_ref, back_ref, own_ref, far_ref, mixed, turned, keep):
    turn_rest(back_ref, turned, half)
    for tile in range(tiles):
        at = slice(tile * LANES, (tile + 1) * LANES)
        xs = []
        for channel, flipped in enumerate(flipped_tiles(back_ref, turned, half, tile)):
            rows = slice(channel * half, (channel + 1) * half)
            increment = (c_ref[rows, at].astype(F32) + flipped) * scale
            keep(rows, at, increment)
            xs.append(increment.astype(BF).astype(F32))
        mix(xs[0], xs[1], own_ref, far_ref, mixed, half, tile, tiles)


def middle_kernel(half, tiles, scale, place, c_ref, back_ref, own_ref, far_ref, *refs):
    *got, c_out, run_out, columns, mixed, total, held, sems, turned = refs
    begin(got, held, sems)

    def keep(rows, at, increment):
        run_out[rows, at] = increment

    update(half, tiles, scale, c_ref, back_ref, own_ref, far_ref, mixed, turned, keep)
    total[...] = jnp.zeros_like(total)
    product(got, mixed, total, held, sems, tiles)
    finish_products(c_out, total, tiles)
    pack_columns(c_out, columns, half)


def last_kernel(
    half, tiles, scale, last_scale, place, c_ref, back_ref, run_ref, own_ref, far_ref, *refs
):
    *got, leave, stay, columns, mixed, total, held, sems, turned, run, turned_all = refs
    begin(got, held, sems)

    def keep(rows, at, increment):
        run[rows, at] = run_ref[rows, at] + increment

    update(half, tiles, scale, c_ref, back_ref, own_ref, far_ref, mixed, turned, keep)
    total[...] = jnp.zeros_like(total)
    product(got, mixed, total, held, sems, tiles)
    first = place[3] != 0
    filler = jnp.zeros((LANES - half, LANES), F32)
    for tile in range(tiles):
        at = slice(tile * LANES, (tile + 1) * LANES)
        value = folded(total, tile, tiles).astype(F32)
        for channel in range(2):
            block = jnp.concatenate([value[channel * half : (channel + 1) * half], filler])
            turned_all[channel, at, :] = block.T
        both = run[:, at] + value * last_scale
        leave[:, at] = jnp.where(first, both[half:], both[:half]).astype(BF)
        stay[:, at] = jnp.where(first, both[:half], both[half:])
    tall, spare = 2 * half, LANES - half
    high = columns.shape[2]
    for channel in range(2):
        for row in range(columns.shape[1]):
            base = turned_all[channel, row * tall : row * tall + high]
            tail = turned_all[channel, row * tall + high : (row + 1) * tall]
            side = jnp.concatenate([shifted(tail, half), shifted(tail, half - spare)])
            side = jnp.concatenate([side, jnp.zeros((high - side.shape[0], LANES), F32)])
            columns[channel, row] = jnp.where(lane_index() < half, base, side).astype(BF)


def end_kernel(half, scale, first_ref, ham_ref, stay_ref, land_ref, got_ref, out_ref):
    first = first_ref[0] != 0

    spare = LANES - half
    left_over = 2 * half - got_ref.shape[2]

    def piece(s, begin):
        block = got_ref[s % 2, s // 2].astype(F32)
        front = shifted(block[:left_over], begin - half)
        back = shifted(block[left_over : 2 * left_over], begin - half + spare)
        tail = jnp.where(lane_index() >= begin + spare, back, front)
        return jnp.concatenate([shifted(block, begin), tail])

    for tile in range(ham_ref.shape[1] // LANES):
        at = slice(tile * LANES, (tile + 1) * LANES)
        total = ham_ref[:, at].astype(F32) + laid_out(piece, half, tile) * scale
        stay, land = stay_ref[:, at], land_ref[:, at].astype(F32)
        out_ref[:half, at] = total[:half] + jnp.where(first, stay, land)
        out_ref[half:, at] = total[half:] + jnp.where(first, land, stay)


def call(kernel, out_shape, specs, name, scratch=(), cost=None, megabytes=16):
    single = not isinstance(out_shape, (list, tuple))
    return pl.pallas_call(
        kernel,
        out_shape=out_shape,
        in_specs=specs,
        out_specs=VMEM if single else [VMEM] * len(out_shape),
        scratch_shapes=scratch,
        compiler_params=pltpu.CompilerParams(vmem_limit_bytes=megabytes << 20),
        cost_estimate=cost,
        name=name,
    )


def passed(value, axis, apart):
    size = lax.axis_size(axis)
    return lax.ppermute(value, axis, [(i, (i + apart) % size) for i in range(size)])


def both_ways(value, one, other):
    by_one = {0: value, -1: passed(value, one, 1), 1: passed(value, one, -1)}
    by_one[2] = passed(value, one, 2)
    near = jnp.concatenate([by_one[k] for k in NEAR])
    rest = jnp.concatenate([by_one[k] for k in REST])
    near_up, near_down = passed(near, other, 1), passed(near, other, -1)
    rest_up, rest_down = passed(rest, other, 1), passed(rest, other, -1)
    return [
        near, near_up, near_down, passed(near_up, other, 1),
        rest, rest_up, rest_down, passed(rest_down, other, -1),
    ]


def swapped(value):
    return lax.ppermute(value, "hi", [(0, 1), (1, 0)])


def on_device(
    generator, hamiltonian, live_states, pp_occupation, ph_occupation, ph_order, recoupling
):
    row_count = generator.shape[1]
    state_count = generator.shape[2]
    half = row_count // 2
    shard_count = (lax.axis_size("y") * lax.axis_size("z"))
    tiles = state_count // LANES
    sent_tiles = tiles // 2 + 1
    hi = lax.axis_index("hi")
    lo = lax.axis_index("lo")
    my_shard = lax.axis_index(ROW)
    first = hi == 0
    shape = jax.ShapeDtypeStruct
    r0 = recoupling[lo]
    r1 = recoupling[lo + lax.axis_size("lo")]
    positions = jnp.arange(state_count, dtype=jnp.int32)
    share = call(
        functools.partial(pack_kernel, sent_tiles, tiles),
        shape((row_count, sent_tiles * LANES), BF),
        [SMEM, VMEM],
        "pack",
    )(jnp.stack([my_shard * row_count, live_states[0]]), generator[0])
    far_share = swapped(share)
    gathered = lax.all_gather(share, ROW, axis=0, tiled=False)
    pieces = both_ways(far_share[:half], "y", "z") + both_ways(far_share[half:], "z", "y")
    ph_order, ph_occupation, pp_occupation, hamiltonian, live_states, _, _ = (
        lax.optimization_barrier(
            (
                ph_order, ph_occupation, pp_occupation, hamiltonian, live_states,
                pieces[4], pieces[12],
            )
        )
    )
    live_count = live_states[0]
    column_alive = positions < live_count
    row_alive = my_shard * row_count + jnp.arange(row_count, dtype=jnp.int32) < live_count
    block_alive = row_alive[:, None] & column_alive[None, :]
    place = jnp.stack(
        [lax.axis_index("y"), lax.axis_index("z"), lax.axis_size("y"), first.astype(jnp.int32)]
    ).astype(jnp.int32)
    collected = pl.pallas_call(
        collect_kernel,
        out_shape=shape(gathered.shape, BF),
        in_specs=[SMEM] + [pl.BlockSpec(memory_space=pl.ANY)] * len(pieces),
        out_specs=HBM,
        scratch_shapes=[pltpu.SemaphoreType.DMA((2 * len(pieces),))],
        compiler_params=pltpu.CompilerParams(vmem_limit_bytes=40 << 20),
        name="collect",
    )(place, *pieces)
    gathered = [gathered, collected]

    pp = jnp.where(column_alive, pp_occupation[0], 0)
    ph = jnp.zeros((state_count,), jnp.int32).at[ph_order[0]].set(ph_occupation[0])
    ph = jnp.where(column_alive, ph, 0)
    mine = jnp.stack([pp, ph]).astype(F32)
    other = swapped(mine)
    d0, n0 = jnp.where(first, mine, other)
    d1, n1 = jnp.where(first, other, mine)
    a0 = d0 + r0[0] ** 3 * n0 + r1[1] ** 3 * n1
    a1 = d1 + r1[0] ** 3 * n1 + r0[1] ** 3 * n0
    p = r0[0] ** 2 * r0[1] * n0 + r1[1] ** 2 * r1[0] * n1
    q = r1[0] ** 2 * r1[1] * n1 + r0[1] ** 2 * r0[0] * n0
    zero_set = jnp.stack([a0, p, p, q])
    one_set = jnp.stack([p, q, q, a1])
    own_set = jnp.where(first, zero_set, one_set)
    far_set = jnp.where(first, one_set, zero_set)

    own_ham = jnp.where(block_alive, hamiltonian[0], jnp.zeros_like(hamiltonian[0]))
    keep = lax.dynamic_slice_in_dim(own_ham, hi * half, half, 0)
    gone = lax.dynamic_slice_in_dim(own_ham, (1 - hi) * half, half, 0)
    came = swapped(gone)
    current = jnp.concatenate([jnp.where(first, keep, came), jnp.where(first, came, keep)])

    wide = (tiles + sent_tiles - 1) * LANES
    rest = row_count - LANES
    destinations = 2 * shard_count
    scratch = [
        pltpu.VMEM((2, row_count, wide), BF),
        pltpu.VMEM((row_count, wide), F32),
        pltpu.VMEM((2, state_count, sent_tiles * LANES), BF),
        pltpu.SemaphoreType.DMA((2, shard_count)),
    ]
    more = [pltpu.VMEM((destinations * rest // LANES, LANES, LANES), F32)]
    c_shape = shape((row_count, state_count), BF)
    run_shape = shape((row_count, state_count), F32)
    sent_shape = shape((destinations, half + rest, LANES), BF)
    cost = pl.CostEstimate(
        flops=4 * row_count * state_count * state_count,
        bytes_accessed=4 * state_count * sent_tiles * LANES,
        transcendentals=0,
    )

    def exchanged(columns):
        return lax.all_to_all(columns, ("y", "z", "hi"), split_axis=0, concat_axis=0, tiled=True)

    combined, columns = call(
        functools.partial(first_kernel, half, tiles),
        [c_shape, sent_shape],
        [SMEM] + [VMEM] * 3 + [HBM] * len(gathered),
        "first",
        scratch,
        cost,
        52,
    )(place, current, own_set, far_set, *gathered)
    back = exchanged(columns)
    combined, running, columns = call(
        functools.partial(middle_kernel, half, tiles, -1.0),
        [c_shape, run_shape, sent_shape],
        [SMEM] + [VMEM] * 4 + [HBM] * len(gathered),
        "middle",
        scratch + more,
        cost,
        52,
    )(place, combined, back, own_set, far_set, *gathered)
    back = exchanged(columns)
    which = first.astype(jnp.int32)[None]
    leaving, staying, blocks = call(
        functools.partial(last_kernel, half, tiles, -0.5, -1.0 / TERMS),
        [
            shape((half, state_count), BF),
            shape((half, state_count), F32),
            shape((2, shard_count, half + rest, LANES), BF),
        ],
        [SMEM] + [VMEM] * 5 + [HBM] * len(gathered),
        "last",
        scratch
        + more
        + [pltpu.VMEM((row_count, state_count), F32), pltpu.VMEM((2, state_count, LANES), F32)],
        cost,
        52,
    )(place, combined, back, running, own_set, far_set, *gathered)
    landed = swapped(leaving)
    got = lax.all_to_all(
        blocks.reshape(destinations, half + rest, LANES),
        ("hi", "y", "z"),
        split_axis=0,
        concat_axis=0,
        tiled=True,
    )
    result = call(
        functools.partial(end_kernel, half, -1.0 / TERMS),
        shape((row_count, state_count), F32),
        [SMEM] + [VMEM] * 4,
        "finish",
    )(which, own_ham, staying, landed, got.reshape(2, shard_count, half + rest, LANES))
    return result[None]


def solution(mesh):
    chans, rows = mesh.devices.shape
    side = math.isqrt(rows)
    pairs = Mesh(
        mesh.devices.reshape(2, chans // 2, side, rows // side), ("hi", "lo", "y", "z")
    )
    chan = ("hi", "lo")
    placed = (
        P(chan, ROW, None),
        P(chan, ROW, None),
        P(chan),
        P(chan, None),
        P(chan, None),
        P(chan, None),
        P(),
    )
    return jax.shard_map(
        on_device, mesh=pairs, in_specs=placed, out_specs=P(chan, ROW, None), check_vma=False
    )
```

```python
import functools
import math

import jax
import jax.numpy as jnp
from jax import lax
from jax.experimental import pallas as pl
from jax.experimental.pallas import tpu as pltpu
from jax.sharding import Mesh, PartitionSpec as P

TERMS = 3
ROW = ("y", "z")
LANES = 128
STEP = 32
BF = jnp.bfloat16
F32 = jnp.float32
VMEM = pl.BlockSpec(memory_space=pltpu.VMEM)
SMEM = pl.BlockSpec(memory_space=pltpu.SMEM)
HBM = pl.BlockSpec(memory_space=pltpu.HBM)


def tile_at(index):
    return pl.ds(pl.multiple_of(index * LANES, LANES), LANES)


def pack_kernel(sent_tiles, tiles, scalars, gen_ref, out_ref):
    start, live = scalars[0], scalars[1]
    for group in range(gen_ref.shape[0] // STEP):
        rows = pl.ds(group * STEP, STEP)
        first_row = start + group * STEP
        diagonal = first_row // LANES
        row_at = first_row + lax.broadcasted_iota(jnp.int32, (STEP, LANES), 0)
        for apart in range(sent_tiles):
            tile = lax.rem(diagonal + apart, tiles)
            column_at = tile * LANES + lax.broadcasted_iota(jnp.int32, (STEP, LANES), 1)
            alive = (row_at < live) & (column_at < live)
            value = gen_ref[rows, tile_at(tile)].astype(F32)
            out_ref[rows, apart * LANES : (apart + 1) * LANES] = jnp.where(
                alive, value, 0.0
            ).astype(BF)


def shifted(value, shift):
    shift = shift % LANES
    return pltpu.roll(value, shift, 1) if shift else value


def lane_index():
    return lax.broadcasted_iota(jnp.int32, (1, LANES), 1)


def laid_out(pieces, half, tile):
    low = tile * LANES
    result = None
    for piece in range(low // half, (low + LANES - 1) // half + 1):
        begin = piece * half - low
        value = pieces(piece, begin)
        result = value if result is None else jnp.where(lane_index() >= begin, value, result)
    return result


def mix(x0, x1, own_ref, far_ref, mixed, half, tile, tiles):
    at = slice(tile * LANES, (tile + 1) * LANES)
    places = [at]
    if (tile + tiles + 1) * LANES <= mixed.shape[2]:
        places.append(slice((tile + tiles) * LANES, (tile + tiles + 1) * LANES))
    for which, weights in enumerate((own_ref, far_ref)):
        top = (x0 * weights[0:1, at] + x1 * weights[1:2, at]).astype(BF)
        low = (x0 * weights[2:3, at] + x1 * weights[3:4, at]).astype(BF)
        for place in places:
            mixed[which, :half, place] = top
            mixed[which, half:, place] = low


def product(got, mixed, total, held, sems, tiles):
    pairs = tiles // 2

    def step(pair, carry):
        rows_of = got[0].shape[1]

        def blocks_before(p):
            return (p * 2 * LANES + rows_of - 1) // rows_of

        @pl.loop(blocks_before(pair), blocks_before(pair + 1))
        def _(block):
            own_copy(got, held, sems, block).wait()
            for part in range(2):
                far_copy(got, held, sems, 0, part, block, 0).wait()

        even = pl.multiple_of(pair * 2 * LANES, 2 * LANES)
        odd = pl.multiple_of(even + LANES, LANES)

        def rows(which, start, low, high):
            return held[which, pl.ds(start, LANES), low * LANES : high * LANES]

        def left(apart, count):
            at = pl.ds(pl.multiple_of(even + apart * LANES, LANES), count * LANES)
            return jnp.concatenate([mixed[0, :, at], mixed[1, :, at]], 1)

        def add(apart, count, value):
            at = pl.multiple_of(even + apart * LANES, LANES)
            total[:, pl.ds(at, count * LANES)] += value

        def straight(a, parts):
            w = jnp.concatenate(parts, 0)
            return jnp.dot(a, w, preferred_element_type=F32)

        def turned(a, parts):
            w = jnp.concatenate(parts, 1)
            return lax.dot_general(a, w, (((1,), (1,)), ((), ())), preferred_element_type=F32)

        def two(start, low, high):
            return [rows(w, start, low, high) for w in range(2)]

        span = pairs
        parts = []
        for w in range(2):
            parts += [rows(w, even, 1, span + 1), rows(w, odd, 0, span)]
        add(1, span, straight(left(0, 2), parts))
        parts = [
            jnp.concatenate([rows(w, even, 2, span), rows(w, odd, 1, span - 1)], 0)
            for w in range(2)
        ]
        add(0, 2, -turned(left(2, span - 2), parts))
        near = straight(left(0, 1), two(even, 0, 1))
        add(0, 1, near - turned(left(1, 1), two(even, 1, 2)))
        add(1, 1, -turned(left(span, 1), two(odd, span - 1, span)))
        add(span + 1, 1, straight(left(1, 1), two(odd, span, span + 1)))
        return carry

    lax.fori_loop(0, pairs, step, 0)


NEAR = (0, -1)
REST = (1, 2)
APART = (0, -1, 1, 2)


def own_copy(got, held, sems, block):
    rows = got[0].shape[1]
    at = pl.multiple_of(block * rows, rows)
    return pltpu.make_async_copy(
        got[0].at[block], held.at[0, pl.ds(at, rows)], sems.at[0, block]
    )


def far_copy(got, held, sems, buffer, part, block, piece):
    half = got[1].shape[0] // 2
    at = pl.multiple_of((2 * block + part) * half, half)
    return pltpu.make_async_copy(
        got[1 + buffer].at[piece * half : (piece + 1) * half],
        held.at[1, pl.ds(at, half)],
        sems.at[1 + part, block],
    )


def begin(got, place, held, sems):
    y, z, side = place[0], place[1], place[2]
    buffer = 0
    for part in range(2):
        for near in (NEAR, REST):
            for second in APART:
                for piece, first in enumerate(near):
                    dy, dz = (first, second) if part == 0 else (second, first)
                    row = lax.rem(y + dy + side, side)
                    column = lax.rem(z + dz + side, side)
                    far_copy(got, held, sems, buffer, part, row * side + column, piece).start()
                buffer += 1

    @pl.loop(0, got[0].shape[0])
    def _(block):
        own_copy(got, held, sems, block).start()


def folded(total, tile, tiles):
    at = slice(tile * LANES, (tile + 1) * LANES)
    value = total[:, at]
    if (tile + tiles + 1) * LANES <= total.shape[1]:
        value = value + total[:, (tile + tiles) * LANES : (tile + tiles + 1) * LANES]
    return value.astype(BF)


def pack_columns(c_ref, columns, half):
    count = c_ref.shape[1] // half
    rest = c_ref.shape[0] - LANES
    for tile in range(c_ref.shape[1] // LANES):
        block = c_ref[:LANES, tile * LANES : (tile + 1) * LANES].astype(F32).T.astype(BF)
        step = 16
        for k in range(LANES // step):
            row = tile * LANES + k * step
            columns[row // half, row % half : row % half + step, :] = block[k * step : (k + 1) * step]
    for piece in range(count):
        tile, off = divmod(piece * half, LANES)
        tail = slice(LANES, LANES + rest)
        value = shifted(c_ref[tail, tile * LANES : (tile + 1) * LANES].astype(F32), -off)
        if off + half > LANES:
            more = c_ref[tail, (tile + 1) * LANES : (tile + 2) * LANES].astype(F32)
            value = jnp.where(lane_index() < LANES - off, value, shifted(more, -off))
        columns[piece, half : half + rest, :] = value.astype(BF)


def flipped_tiles(got_ref, turned, half, tile):
    rest = 2 * half - LANES
    group = LANES // rest
    kept = half - rest

    def near(s, begin):
        return shifted(got_ref[s, :half, :].astype(F32), begin)

    def far(s, begin):
        front = shifted(got_ref[s, :half, :].astype(F32), begin - half)
        back = turned[s // group, :half, :]
        back = shifted(back, begin + kept - rest * (s % group))
        return jnp.where(lane_index() >= begin + kept, back, front)

    return laid_out(near, half, tile), laid_out(far, half, tile)


def turn_rest(got_ref, turned, half):
    rest = 2 * half - LANES
    group = LANES // rest
    for k in range(got_ref.shape[0] // group):
        block = jnp.concatenate(
            [got_ref[k * group + m, half : half + rest, :].astype(F32) for m in range(group)], 0
        )
        turned[k] = block.T


def finish_products(c_out, total, tiles):
    for tile in range(tiles):
        c_out[:, tile * LANES : (tile + 1) * LANES] = folded(total, tile, tiles)


def first_kernel(half, tiles, place, x_ref, own_ref, far_ref, *refs):
    *got, c_out, columns, mixed, total, held, sems = refs
    begin(got, place, held, sems)
    for tile in range(tiles):
        at = slice(tile * LANES, (tile + 1) * LANES)
        x0, x1 = x_ref[:half, at].astype(F32), x_ref[half:, at].astype(F32)
        mix(x0, x1, own_ref, far_ref, mixed, half, tile, tiles)
    total[...] = jnp.zeros_like(total)
    product(got, mixed, total, held, sems, tiles)
    finish_products(c_out, total, tiles)
    pack_columns(c_out, columns, half)


def update(half, tiles, scale, c_ref, back_ref, own_ref, far_ref, mixed, turned, keep):
    turn_rest(back_ref, turned, half)
    for tile in range(tiles):
        at = slice(tile * LANES, (tile + 1) * LANES)
        xs = []
        for channel, flipped in enumerate(flipped_tiles(back_ref, turned, half, tile)):
            rows = slice(channel * half, (channel + 1) * half)
            increment = (c_ref[rows, at].astype(F32) + flipped) * scale
            keep(rows, at, increment)
            xs.append(increment.astype(BF).astype(F32))
        mix(xs[0], xs[1], own_ref, far_ref, mixed, half, tile, tiles)


def middle_kernel(half, tiles, scale, place, c_ref, back_ref, own_ref, far_ref, *refs):
    *got, c_out, run_out, columns, mixed, total, held, sems, turned = refs
    begin(got, place, held, sems)

    def keep(rows, at, increment):
        run_out[rows, at] = increment

    update(half, tiles, scale, c_ref, back_ref, own_ref, far_ref, mixed, turned, keep)
    total[...] = jnp.zeros_like(total)
    product(got, mixed, total, held, sems, tiles)
    finish_products(c_out, total, tiles)
    pack_columns(c_out, columns, half)


def last_kernel(
    half, tiles, scale, last_scale, place, c_ref, back_ref, run_ref, own_ref, far_ref, *refs
):
    *got, leave, stay, columns, mixed, total, held, sems, turned, run, turned_all = refs
    begin(got, place, held, sems)

    def keep(rows, at, increment):
        run[rows, at] = run_ref[rows, at] + increment

    update(half, tiles, scale, c_ref, back_ref, own_ref, far_ref, mixed, turned, keep)
    total[...] = jnp.zeros_like(total)
    product(got, mixed, total, held, sems, tiles)
    first = place[3] != 0
    filler = jnp.zeros((LANES - half, LANES), F32)
    for tile in range(tiles):
        at = slice(tile * LANES, (tile + 1) * LANES)
        value = folded(total, tile, tiles).astype(F32)
        for channel in range(2):
            block = jnp.concatenate([value[channel * half : (channel + 1) * half], filler])
            turned_all[channel, at, :] = block.T
        both = run[:, at] + value * last_scale
        leave[:, at] = jnp.where(first, both[half:], both[:half]).astype(BF)
        stay[:, at] = jnp.where(first, both[:half], both[half:])
    tall, spare = 2 * half, LANES - half
    high = columns.shape[2]
    for channel in range(2):
        for row in range(columns.shape[1]):
            base = turned_all[channel, row * tall : row * tall + high]
            tail = turned_all[channel, row * tall + high : (row + 1) * tall]
            side = jnp.concatenate([shifted(tail, half), shifted(tail, half - spare)])
            side = jnp.concatenate([side, jnp.zeros((high - side.shape[0], LANES), F32)])
            columns[channel, row] = jnp.where(lane_index() < half, base, side).astype(BF)


def end_kernel(half, scale, first_ref, ham_ref, stay_ref, land_ref, got_ref, out_ref):
    first = first_ref[0] != 0

    spare = LANES - half
    left_over = 2 * half - got_ref.shape[2]

    def piece(s, begin):
        block = got_ref[s % 2, s // 2].astype(F32)
        front = shifted(block[:left_over], begin - half)
        back = shifted(block[left_over : 2 * left_over], begin - half + spare)
        tail = jnp.where(lane_index() >= begin + spare, back, front)
        return jnp.concatenate([shifted(block, begin), tail])

    for tile in range(ham_ref.shape[1] // LANES):
        at = slice(tile * LANES, (tile + 1) * LANES)
        total = ham_ref[:, at].astype(F32) + laid_out(piece, half, tile) * scale
        stay, land = stay_ref[:, at], land_ref[:, at].astype(F32)
        out_ref[:half, at] = total[:half] + jnp.where(first, stay, land)
        out_ref[half:, at] = total[half:] + jnp.where(first, land, stay)


def call(kernel, out_shape, specs, name, scratch=(), cost=None, megabytes=16):
    single = not isinstance(out_shape, (list, tuple))
    return pl.pallas_call(
        kernel,
        out_shape=out_shape,
        in_specs=specs,
        out_specs=VMEM if single else [VMEM] * len(out_shape),
        scratch_shapes=scratch,
        compiler_params=pltpu.CompilerParams(vmem_limit_bytes=megabytes << 20),
        cost_estimate=cost,
        name=name,
    )


def passed(value, axis, apart):
    size = lax.axis_size(axis)
    return lax.ppermute(value, axis, [(i, (i + apart) % size) for i in range(size)])


def both_ways(value, one, other):
    by_one = {0: value, -1: passed(value, one, 1), 1: passed(value, one, -1)}
    by_one[2] = passed(value, one, 2)
    near = jnp.concatenate([by_one[k] for k in NEAR])
    rest = jnp.concatenate([by_one[k] for k in REST])
    near_up, near_down = passed(near, other, 1), passed(near, other, -1)
    rest_up, rest_down = passed(rest, other, 1), passed(rest, other, -1)
    return [
        near, near_up, near_down, passed(near_up, other, 1),
        rest, rest_up, rest_down, passed(rest_down, other, -1),
    ]


def swapped(value):
    return lax.ppermute(value, "hi", [(0, 1), (1, 0)])


def on_device(
    generator, hamiltonian, live_states, pp_occupation, ph_occupation, ph_order, recoupling
):
    row_count = generator.shape[1]
    state_count = generator.shape[2]
    half = row_count // 2
    shard_count = (lax.axis_size("y") * lax.axis_size("z"))
    tiles = state_count // LANES
    sent_tiles = tiles // 2 + 1
    hi = lax.axis_index("hi")
    lo = lax.axis_index("lo")
    my_shard = lax.axis_index(ROW)
    first = hi == 0
    shape = jax.ShapeDtypeStruct
    r0 = recoupling[lo]
    r1 = recoupling[lo + lax.axis_size("lo")]
    positions = jnp.arange(state_count, dtype=jnp.int32)
    share = call(
        functools.partial(pack_kernel, sent_tiles, tiles),
        shape((row_count, sent_tiles * LANES), BF),
        [SMEM, VMEM],
        "pack",
    )(jnp.stack([my_shard * row_count, live_states[0]]), generator[0])
    far_share = swapped(share)
    gathered = lax.all_gather(share, ROW, axis=0, tiled=False)
    pieces = both_ways(far_share[:half], "y", "z") + both_ways(far_share[half:], "z", "y")
    ph_order, ph_occupation, pp_occupation, hamiltonian, live_states, _, _ = (
        lax.optimization_barrier(
            (
                ph_order, ph_occupation, pp_occupation, hamiltonian, live_states,
                pieces[4], pieces[12],
            )
        )
    )
    live_count = live_states[0]
    column_alive = positions < live_count
    row_alive = my_shard * row_count + jnp.arange(row_count, dtype=jnp.int32) < live_count
    block_alive = row_alive[:, None] & column_alive[None, :]
    place = jnp.stack(
        [lax.axis_index("y"), lax.axis_index("z"), lax.axis_size("y"), first.astype(jnp.int32)]
    ).astype(jnp.int32)
    gathered = [gathered] + pieces

    pp = jnp.where(column_alive, pp_occupation[0], 0)
    ph = jnp.zeros((state_count,), jnp.int32).at[ph_order[0]].set(ph_occupation[0])
    ph = jnp.where(column_alive, ph, 0)
    mine = jnp.stack([pp, ph]).astype(F32)
    other = swapped(mine)
    d0, n0 = jnp.where(first, mine, other)
    d1, n1 = jnp.where(first, other, mine)
    a0 = d0 + r0[0] ** 3 * n0 + r1[1] ** 3 * n1
    a1 = d1 + r1[0] ** 3 * n1 + r0[1] ** 3 * n0
    p = r0[0] ** 2 * r0[1] * n0 + r1[1] ** 2 * r1[0] * n1
    q = r1[0] ** 2 * r1[1] * n1 + r0[1] ** 2 * r0[0] * n0
    zero_set = jnp.stack([a0, p, p, q])
    one_set = jnp.stack([p, q, q, a1])
    own_set = jnp.where(first, zero_set, one_set)
    far_set = jnp.where(first, one_set, zero_set)

    own_ham = jnp.where(block_alive, hamiltonian[0], jnp.zeros_like(hamiltonian[0]))
    keep = lax.dynamic_slice_in_dim(own_ham, hi * half, half, 0)
    gone = lax.dynamic_slice_in_dim(own_ham, (1 - hi) * half, half, 0)
    came = swapped(gone)
    current = jnp.concatenate([jnp.where(first, keep, came), jnp.where(first, came, keep)])

    wide = (tiles + sent_tiles - 1) * LANES
    rest = row_count - LANES
    destinations = 2 * shard_count
    scratch = [
        pltpu.VMEM((2, row_count, wide), BF),
        pltpu.VMEM((row_count, wide), F32),
        pltpu.VMEM((2, state_count, sent_tiles * LANES), BF),
        pltpu.SemaphoreType.DMA((3, shard_count)),
    ]
    more = [pltpu.VMEM((destinations * rest // LANES, LANES, LANES), F32)]
    c_shape = shape((row_count, state_count), BF)
    run_shape = shape((row_count, state_count), F32)
    sent_shape = shape((destinations, half + rest, LANES), BF)
    cost = pl.CostEstimate(
        flops=4 * row_count * state_count * state_count,
        bytes_accessed=4 * state_count * sent_tiles * LANES,
        transcendentals=0,
    )

    def exchanged(columns):
        return lax.all_to_all(columns, ("y", "z", "hi"), split_axis=0, concat_axis=0, tiled=True)

    combined, columns = call(
        functools.partial(first_kernel, half, tiles),
        [c_shape, sent_shape],
        [SMEM] + [VMEM] * 3 + [HBM] * len(gathered),
        "first",
        scratch,
        cost,
        58,
    )(place, current, own_set, far_set, *gathered)
    back = exchanged(columns)
    combined, running, columns = call(
        functools.partial(middle_kernel, half, tiles, -1.0),
        [c_shape, run_shape, sent_shape],
        [SMEM] + [VMEM] * 4 + [HBM] * len(gathered),
        "middle",
        scratch + more,
        cost,
        40,
    )(place, combined, back, own_set, far_set, *gathered)
    back = exchanged(columns)
    which = first.astype(jnp.int32)[None]
    leaving, staying, blocks = call(
        functools.partial(last_kernel, half, tiles, -0.5, -1.0 / TERMS),
        [
            shape((half, state_count), BF),
            shape((half, state_count), F32),
            shape((2, shard_count, half + rest, LANES), BF),
        ],
        [SMEM] + [VMEM] * 5 + [HBM] * len(gathered),
        "last",
        scratch
        + more
        + [pltpu.VMEM((row_count, state_count), F32), pltpu.VMEM((2, state_count, LANES), F32)],
        cost,
        40,
    )(place, combined, back, running, own_set, far_set, *gathered)
    landed = swapped(leaving)
    got = lax.all_to_all(
        blocks.reshape(destinations, half + rest, LANES),
        ("hi", "y", "z"),
        split_axis=0,
        concat_axis=0,
        tiled=True,
    )
    result = call(
        functools.partial(end_kernel, half, -1.0 / TERMS),
        shape((row_count, state_count), F32),
        [SMEM] + [VMEM] * 4,
        "finish",
    )(which, own_ham, staying, landed, got.reshape(2, shard_count, half + rest, LANES))
    return result[None]


def solution(mesh):
    chans, rows = mesh.devices.shape
    side = math.isqrt(rows)
    pairs = Mesh(
        mesh.devices.reshape(2, chans // 2, side, rows // side), ("hi", "lo", "y", "z")
    )
    chan = ("hi", "lo")
    placed = (
        P(chan, ROW, None),
        P(chan, ROW, None),
        P(chan),
        P(chan, None),
        P(chan, None),
        P(chan, None),
        P(),
    )
    return jax.shard_map(
        on_device, mesh=pairs, in_specs=placed, out_specs=P(chan, ROW, None), check_vma=False
    )
```

```python
import functools
import math

import jax
import jax.numpy as jnp
from jax import lax
from jax.experimental import pallas as pl
from jax.experimental.pallas import tpu as pltpu
from jax.sharding import Mesh, PartitionSpec as P

TERMS = 3
ROW = ("y", "z")
LANES = 128
STEP = 32
BF = jnp.bfloat16
F32 = jnp.float32
VMEM = pl.BlockSpec(memory_space=pltpu.VMEM)
SMEM = pl.BlockSpec(memory_space=pltpu.SMEM)
HBM = pl.BlockSpec(memory_space=pltpu.HBM)


def tile_at(index):
    return pl.ds(pl.multiple_of(index * LANES, LANES), LANES)


def pack_kernel(sent_tiles, tiles, scalars, gen_ref, out_ref):
    start, live = scalars[0], scalars[1]
    for group in range(gen_ref.shape[0] // STEP):
        rows = pl.ds(group * STEP, STEP)
        first_row = start + group * STEP
        diagonal = first_row // LANES
        row_at = first_row + lax.broadcasted_iota(jnp.int32, (STEP, LANES), 0)
        for apart in range(sent_tiles):
            tile = lax.rem(diagonal + apart, tiles)
            column_at = tile * LANES + lax.broadcasted_iota(jnp.int32, (STEP, LANES), 1)
            alive = (row_at < live) & (column_at < live)
            value = gen_ref[rows, tile_at(tile)].astype(F32)
            out_ref[rows, apart * LANES : (apart + 1) * LANES] = jnp.where(
                alive, value, 0.0
            ).astype(BF)


def shifted(value, shift):
    shift = shift % LANES
    return pltpu.roll(value, shift, 1) if shift else value


def lane_index():
    return lax.broadcasted_iota(jnp.int32, (1, LANES), 1)


def laid_out(pieces, half, tile):
    low = tile * LANES
    result = None
    for piece in range(low // half, (low + LANES - 1) // half + 1):
        begin = piece * half - low
        value = pieces(piece, begin)
        result = value if result is None else jnp.where(lane_index() >= begin, value, result)
    return result


def mix(x0, x1, own_ref, far_ref, mixed, half, tile, tiles):
    at = slice(tile * LANES, (tile + 1) * LANES)
    places = [at]
    if (tile + tiles + 1) * LANES <= mixed.shape[2]:
        places.append(slice((tile + tiles) * LANES, (tile + tiles + 1) * LANES))
    for which, weights in enumerate((own_ref, far_ref)):
        top = (x0 * weights[0:1, at] + x1 * weights[1:2, at]).astype(BF)
        low = (x0 * weights[2:3, at] + x1 * weights[3:4, at]).astype(BF)
        for place in places:
            mixed[which, :half, place] = top
            mixed[which, half:, place] = low


def product(got, mixed, total, held, sems, tiles):
    pairs = tiles // 2

    def step(pair, carry):
        rows_of = got[0].shape[1]

        def blocks_before(p):
            return (p * 2 * LANES + rows_of - 1) // rows_of

        @pl.loop(blocks_before(pair), blocks_before(pair + 1))
        def _(block):
            for which in range(2):
                block_copy(got, held, sems, which, block).wait()

        even = pl.multiple_of(pair * 2 * LANES, 2 * LANES)
        odd = pl.multiple_of(even + LANES, LANES)

        def rows(which, start, low, high):
            return held[which, pl.ds(start, LANES), low * LANES : high * LANES]

        def left(apart, count):
            at = pl.ds(pl.multiple_of(even + apart * LANES, LANES), count * LANES)
            return jnp.concatenate([mixed[0, :, at], mixed[1, :, at]], 1)

        def add(apart, count, value):
            at = pl.multiple_of(even + apart * LANES, LANES)
            total[:, pl.ds(at, count * LANES)] += value

        def straight(a, parts):
            w = jnp.concatenate(parts, 0)
            return jnp.dot(a, w, preferred_element_type=F32)

        def turned(a, parts):
            w = jnp.concatenate(parts, 1)
            return lax.dot_general(a, w, (((1,), (1,)), ((), ())), preferred_element_type=F32)

        def two(start, low, high):
            return [rows(w, start, low, high) for w in range(2)]

        span = pairs
        parts = []
        for w in range(2):
            parts += [rows(w, even, 1, span + 1), rows(w, odd, 0, span)]
        add(1, span, straight(left(0, 2), parts))
        parts = [
            jnp.concatenate([rows(w, even, 2, span), rows(w, odd, 1, span - 1)], 0)
            for w in range(2)
        ]
        add(0, 2, -turned(left(2, span - 2), parts))
        near = straight(left(0, 1), two(even, 0, 1))
        add(0, 1, near - turned(left(1, 1), two(even, 1, 2)))
        add(1, 1, -turned(left(span, 1), two(odd, span - 1, span)))
        add(span + 1, 1, straight(left(1, 1), two(odd, span, span + 1)))
        return carry

    lax.fori_loop(0, pairs, step, 0)


NEAR = (0, -1)
REST = (1, 2)
APART = (0, -1, 1, 2)


def collect_kernel(late, place, *refs):
    *got, out, sems = refs
    got = got[1:] if late else got
    half = got[0].shape[0] // 2
    y, z, side = place[0], place[1], place[2]
    copies = []
    buffer = 0
    for part in range(2):
        for near in (NEAR, REST):
            for second in APART[3:] if late else APART[:3]:
                for piece, first in enumerate(near):
                    dy, dz = (first, second) if part == 0 else (second, first)
                    row = lax.rem(y + dy + side, side)
                    column = lax.rem(z + dz + side, side)
                    copies.append(
                        pltpu.make_async_copy(
                            got[buffer].at[piece * half : (piece + 1) * half],
                            out.at[row * side + column, part * half : (part + 1) * half],
                            sems.at[len(copies)],
                        )
                    )
                buffer += 1
    for copy in copies:
        copy.start()
    for copy in copies:
        copy.wait()


def block_copy(got, held, sems, which, block):
    rows = got[which].shape[1]
    at = pl.multiple_of(block * rows, rows)
    return pltpu.make_async_copy(
        got[which].at[block], held.at[which, pl.ds(at, rows)], sems.at[which, block]
    )


def begin(got, held, sems):
    @pl.loop(0, got[0].shape[0])
    def _(block):
        for which in range(2):
            block_copy(got, held, sems, which, block).start()


def folded(total, tile, tiles):
    at = slice(tile * LANES, (tile + 1) * LANES)
    value = total[:, at]
    if (tile + tiles + 1) * LANES <= total.shape[1]:
        value = value + total[:, (tile + tiles) * LANES : (tile + tiles + 1) * LANES]
    return value.astype(BF)


def pack_columns(c_ref, columns, half):
    count = c_ref.shape[1] // half
    rest = c_ref.shape[0] - LANES
    for tile in range(c_ref.shape[1] // LANES):
        block = c_ref[:LANES, tile * LANES : (tile + 1) * LANES].astype(F32).T.astype(BF)
        step = 16
        for k in range(LANES // step):
            row = tile * LANES + k * step
            columns[row // half, row % half : row % half + step, :] = block[k * step : (k + 1) * step]
    for piece in range(count):
        tile, off = divmod(piece * half, LANES)
        tail = slice(LANES, LANES + rest)
        value = shifted(c_ref[tail, tile * LANES : (tile + 1) * LANES].astype(F32), -off)
        if off + half > LANES:
            more = c_ref[tail, (tile + 1) * LANES : (tile + 2) * LANES].astype(F32)
            value = jnp.where(lane_index() < LANES - off, value, shifted(more, -off))
        columns[piece, half : half + rest, :] = value.astype(BF)


def flipped_tiles(got_ref, turned, half, tile):
    rest = 2 * half - LANES
    group = LANES // rest
    kept = half - rest

    def near(s, begin):
        return shifted(got_ref[s, :half, :].astype(F32), begin)

    def far(s, begin):
        front = shifted(got_ref[s, :half, :].astype(F32), begin - half)
        back = turned[s // group, :half, :]
        back = shifted(back, begin + kept - rest * (s % group))
        return jnp.where(lane_index() >= begin + kept, back, front)

    return laid_out(near, half, tile), laid_out(far, half, tile)


def turn_rest(got_ref, turned, half):
    rest = 2 * half - LANES
    group = LANES // rest
    for k in range(got_ref.shape[0] // group):
        block = jnp.concatenate(
            [got_ref[k * group + m, half : half + rest, :].astype(F32) for m in range(group)], 0
        )
        turned[k] = block.T


def finish_products(c_out, total, tiles):
    for tile in range(tiles):
        c_out[:, tile * LANES : (tile + 1) * LANES] = folded(total, tile, tiles)


def first_kernel(half, tiles, place, x_ref, own_ref, far_ref, *refs):
    *got, c_out, columns, mixed, total, held, sems = refs
    begin(got, held, sems)
    for tile in range(tiles):
        at = slice(tile * LANES, (tile + 1) * LANES)
        x0, x1 = x_ref[:half, at].astype(F32), x_ref[half:, at].astype(F32)
        mix(x0, x1, own_ref, far_ref, mixed, half, tile, tiles)
    total[...] = jnp.zeros_like(total)
    product(got, mixed, total, held, sems, tiles)
    finish_products(c_out, total, tiles)
    pack_columns(c_out, columns, half)


def update(half, tiles, scale, c_ref, back_ref, own_ref, far_ref, mixed, turned, keep):
    turn_rest(back_ref, turned, half)
    for tile in range(tiles):
        at = slice(tile * LANES, (tile + 1) * LANES)
        xs = []
        for channel, flipped in enumerate(flipped_tiles(back_ref, turned, half, tile)):
            rows = slice(channel * half, (channel + 1) * half)
            increment = (c_ref[rows, at].astype(F32) + flipped) * scale
            keep(rows, at, increment)
            xs.append(increment.astype(BF).astype(F32))
        mix(xs[0], xs[1], own_ref, far_ref, mixed, half, tile, tiles)


def middle_kernel(half, tiles, scale, place, c_ref, back_ref, own_ref, far_ref, *refs):
    *got, c_out, run_out, columns, mixed, total, held, sems, turned = refs
    begin(got, held, sems)

    def keep(rows, at, increment):
        run_out[rows, at] = increment

    update(half, tiles, scale, c_ref, back_ref, own_ref, far_ref, mixed, turned, keep)
    total[...] = jnp.zeros_like(total)
    product(got, mixed, total, held, sems, tiles)
    finish_products(c_out, total, tiles)
    pack_columns(c_out, columns, half)


def last_kernel(
    half, tiles, scale, last_scale, place, c_ref, back_ref, run_ref, own_ref, far_ref, *refs
):
    *got, leave, stay, columns, mixed, total, held, sems, turned, run, turned_all = refs
    begin(got, held, sems)

    def keep(rows, at, increment):
        run[rows, at] = run_ref[rows, at] + increment

    update(half, tiles, scale, c_ref, back_ref, own_ref, far_ref, mixed, turned, keep)
    total[...] = jnp.zeros_like(total)
    product(got, mixed, total, held, sems, tiles)
    first = place[3] != 0
    filler = jnp.zeros((LANES - half, LANES), F32)
    for tile in range(tiles):
        at = slice(tile * LANES, (tile + 1) * LANES)
        value = folded(total, tile, tiles).astype(F32)
        for channel in range(2):
            block = jnp.concatenate([value[channel * half : (channel + 1) * half], filler])
            turned_all[channel, at, :] = block.T
        both = run[:, at] + value * last_scale
        leave[:, at] = jnp.where(first, both[half:], both[:half]).astype(BF)
        stay[:, at] = jnp.where(first, both[:half], both[half:])
    tall, spare = 2 * half, LANES - half
    high = columns.shape[2]
    for channel in range(2):
        for row in range(columns.shape[1]):
            base = turned_all[channel, row * tall : row * tall + high]
            tail = turned_all[channel, row * tall + high : (row + 1) * tall]
            side = jnp.concatenate([shifted(tail, half), shifted(tail, half - spare)])
            side = jnp.concatenate([side, jnp.zeros((high - side.shape[0], LANES), F32)])
            columns[channel, row] = jnp.where(lane_index() < half, base, side).astype(BF)


def end_kernel(half, scale, first_ref, ham_ref, stay_ref, land_ref, got_ref, out_ref):
    first = first_ref[0] != 0

    spare = LANES - half
    left_over = 2 * half - got_ref.shape[2]

    def piece(s, begin):
        block = got_ref[s % 2, s // 2].astype(F32)
        front = shifted(block[:left_over], begin - half)
        back = shifted(block[left_over : 2 * left_over], begin - half + spare)
        tail = jnp.where(lane_index() >= begin + spare, back, front)
        return jnp.concatenate([shifted(block, begin), tail])

    for tile in range(ham_ref.shape[1] // LANES):
        at = slice(tile * LANES, (tile + 1) * LANES)
        total = ham_ref[:, at].astype(F32) + laid_out(piece, half, tile) * scale
        stay, land = stay_ref[:, at], land_ref[:, at].astype(F32)
        out_ref[:half, at] = total[:half] + jnp.where(first, stay, land)
        out_ref[half:, at] = total[half:] + jnp.where(first, land, stay)


def call(kernel, out_shape, specs, name, scratch=(), cost=None, megabytes=16):
    single = not isinstance(out_shape, (list, tuple))
    return pl.pallas_call(
        kernel,
        out_shape=out_shape,
        in_specs=specs,
        out_specs=VMEM if single else [VMEM] * len(out_shape),
        scratch_shapes=scratch,
        compiler_params=pltpu.CompilerParams(vmem_limit_bytes=megabytes << 20),
        cost_estimate=cost,
        name=name,
    )


def passed(value, axis, apart):
    size = lax.axis_size(axis)
    return lax.ppermute(value, axis, [(i, (i + apart) % size) for i in range(size)])


def both_ways(value, one, other):
    by_one = {0: value, -1: passed(value, one, 1), 1: passed(value, one, -1)}
    by_one[2] = passed(value, one, 2)
    near = jnp.concatenate([by_one[k] for k in NEAR])
    rest = jnp.concatenate([by_one[k] for k in REST])
    near_up, near_down = passed(near, other, 1), passed(near, other, -1)
    rest_up, rest_down = passed(rest, other, 1), passed(rest, other, -1)
    return [
        near, near_up, near_down, passed(near_up, other, 1),
        rest, rest_up, rest_down, passed(rest_down, other, -1),
    ]


def swapped(value):
    return lax.ppermute(value, "hi", [(0, 1), (1, 0)])


def on_device(
    generator, hamiltonian, live_states, pp_occupation, ph_occupation, ph_order, recoupling
):
    row_count = generator.shape[1]
    state_count = generator.shape[2]
    half = row_count // 2
    shard_count = (lax.axis_size("y") * lax.axis_size("z"))
    tiles = state_count // LANES
    sent_tiles = tiles // 2 + 1
    hi = lax.axis_index("hi")
    lo = lax.axis_index("lo")
    my_shard = lax.axis_index(ROW)
    first = hi == 0
    shape = jax.ShapeDtypeStruct
    r0 = recoupling[lo]
    r1 = recoupling[lo + lax.axis_size("lo")]
    positions = jnp.arange(state_count, dtype=jnp.int32)
    share = call(
        functools.partial(pack_kernel, sent_tiles, tiles),
        shape((row_count, sent_tiles * LANES), BF),
        [SMEM, VMEM],
        "pack",
    )(jnp.stack([my_shard * row_count, live_states[0]]), generator[0])
    far_share = swapped(share)
    gathered = lax.all_gather(share, ROW, axis=0, tiled=False)
    pieces = both_ways(far_share[:half], "y", "z") + both_ways(far_share[half:], "z", "y")
    ph_order, ph_occupation, pp_occupation, hamiltonian, live_states, _, _ = (
        lax.optimization_barrier(
            (
                ph_order, ph_occupation, pp_occupation, hamiltonian, live_states,
                pieces[4], pieces[12],
            )
        )
    )
    live_count = live_states[0]
    column_alive = positions < live_count
    row_alive = my_shard * row_count + jnp.arange(row_count, dtype=jnp.int32) < live_count
    block_alive = row_alive[:, None] & column_alive[None, :]
    place = jnp.stack(
        [lax.axis_index("y"), lax.axis_index("z"), lax.axis_size("y"), first.astype(jnp.int32)]
    ).astype(jnp.int32)
    early = [piece for k, piece in enumerate(pieces) if k % 4 != 3]
    late = [piece for k, piece in enumerate(pieces) if k % 4 == 3]

    def collect(is_late, parts, aliases):
        return pl.pallas_call(
            functools.partial(collect_kernel, is_late),
            out_shape=shape(gathered.shape, BF),
            in_specs=[SMEM] + [pl.BlockSpec(memory_space=pl.ANY)] * len(parts),
            out_specs=pl.BlockSpec(memory_space=pl.ANY),
            scratch_shapes=[pltpu.SemaphoreType.DMA((2 * len(parts),))],
            input_output_aliases=aliases,
            cost_estimate=pl.CostEstimate(
                flops=0, bytes_accessed=2 * sum(x.size for x in parts), transcendentals=0
            ),
            compiler_params=pltpu.CompilerParams(vmem_limit_bytes=32 << 20),
            name="collect",
        )(place, *parts)

    collected = collect(False, early, {})
    collected = collect(True, [collected] + late, {1: 0})
    gathered = [gathered, collected]

    pp = jnp.where(column_alive, pp_occupation[0], 0)
    ph = jnp.zeros((state_count,), jnp.int32).at[ph_order[0]].set(ph_occupation[0])
    ph = jnp.where(column_alive, ph, 0)
    mine = jnp.stack([pp, ph]).astype(F32)
    other = swapped(mine)
    d0, n0 = jnp.where(first, mine, other)
    d1, n1 = jnp.where(first, other, mine)
    a0 = d0 + r0[0] ** 3 * n0 + r1[1] ** 3 * n1
    a1 = d1 + r1[0] ** 3 * n1 + r0[1] ** 3 * n0
    p = r0[0] ** 2 * r0[1] * n0 + r1[1] ** 2 * r1[0] * n1
    q = r1[0] ** 2 * r1[1] * n1 + r0[1] ** 2 * r0[0] * n0
    zero_set = jnp.stack([a0, p, p, q])
    one_set = jnp.stack([p, q, q, a1])
    own_set = jnp.where(first, zero_set, one_set)
    far_set = jnp.where(first, one_set, zero_set)

    own_ham = jnp.where(block_alive, hamiltonian[0], jnp.zeros_like(hamiltonian[0]))
    keep = lax.dynamic_slice_in_dim(own_ham, hi * half, half, 0)
    gone = lax.dynamic_slice_in_dim(own_ham, (1 - hi) * half, half, 0)
    came = swapped(gone)
    current = jnp.concatenate([jnp.where(first, keep, came), jnp.where(first, came, keep)])

    wide = (tiles + sent_tiles - 1) * LANES
    rest = row_count - LANES
    destinations = 2 * shard_count
    scratch = [
        pltpu.VMEM((2, row_count, wide), BF),
        pltpu.VMEM((row_count, wide), F32),
        pltpu.VMEM((2, state_count, sent_tiles * LANES), BF),
        pltpu.SemaphoreType.DMA((2, shard_count)),
    ]
    more = [pltpu.VMEM((destinations * rest // LANES, LANES, LANES), F32)]
    c_shape = shape((row_count, state_count), BF)
    run_shape = shape((row_count, state_count), F32)
    sent_shape = shape((destinations, half + rest, LANES), BF)
    cost = pl.CostEstimate(
        flops=4 * row_count * state_count * state_count,
        bytes_accessed=4 * state_count * sent_tiles * LANES,
        transcendentals=0,
    )

    def exchanged(columns):
        return lax.all_to_all(columns, ("y", "z", "hi"), split_axis=0, concat_axis=0, tiled=True)

    combined, columns = call(
        functools.partial(first_kernel, half, tiles),
        [c_shape, sent_shape],
        [SMEM] + [VMEM] * 3 + [HBM] * len(gathered),
        "first",
        scratch,
        cost,
        48,
    )(place, current, own_set, far_set, *gathered)
    back = exchanged(columns)
    combined, running, columns = call(
        functools.partial(middle_kernel, half, tiles, -1.0),
        [c_shape, run_shape, sent_shape],
        [SMEM] + [VMEM] * 4 + [HBM] * len(gathered),
        "middle",
        scratch + more,
        cost,
        48,
    )(place, combined, back, own_set, far_set, *gathered)
    back = exchanged(columns)
    which = first.astype(jnp.int32)[None]
    leaving, staying, blocks = call(
        functools.partial(last_kernel, half, tiles, -0.5, -1.0 / TERMS),
        [
            shape((half, state_count), BF),
            shape((half, state_count), F32),
            shape((2, shard_count, half + rest, LANES), BF),
        ],
        [SMEM] + [VMEM] * 5 + [HBM] * len(gathered),
        "last",
        scratch
        + more
        + [pltpu.VMEM((row_count, state_count), F32), pltpu.VMEM((2, state_count, LANES), F32)],
        cost,
        48,
    )(place, combined, back, running, own_set, far_set, *gathered)
    landed = swapped(leaving)
    got = lax.all_to_all(
        blocks.reshape(destinations, half + rest, LANES),
        ("hi", "y", "z"),
        split_axis=0,
        concat_axis=0,
        tiled=True,
    )
    result = call(
        functools.partial(end_kernel, half, -1.0 / TERMS),
        shape((row_count, state_count), F32),
        [SMEM] + [VMEM] * 4,
        "finish",
    )(which, own_ham, staying, landed, got.reshape(2, shard_count, half + rest, LANES))
    return result[None]


def solution(mesh):
    chans, rows = mesh.devices.shape
    side = math.isqrt(rows)
    pairs = Mesh(
        mesh.devices.reshape(2, chans // 2, side, rows // side), ("hi", "lo", "y", "z")
    )
    chan = ("hi", "lo")
    placed = (
        P(chan, ROW, None),
        P(chan, ROW, None),
        P(chan),
        P(chan, None),
        P(chan, None),
        P(chan, None),
        P(),
    )
    return jax.shard_map(
        on_device, mesh=pairs, in_specs=placed, out_specs=P(chan, ROW, None), check_vma=False
    )
```

```python
import functools
import math

import jax
import jax.numpy as jnp
from jax import lax
from jax.experimental import pallas as pl
from jax.experimental.pallas import tpu as pltpu
from jax.sharding import Mesh, PartitionSpec as P

TERMS = 3
ROW = ("y", "z")
LANES = 128
STEP = 32
BF = jnp.bfloat16
F32 = jnp.float32
VMEM = pl.BlockSpec(memory_space=pltpu.VMEM)
SMEM = pl.BlockSpec(memory_space=pltpu.SMEM)
HBM = pl.BlockSpec(memory_space=pltpu.HBM)


def tile_at(index):
    return pl.ds(pl.multiple_of(index * LANES, LANES), LANES)


def pack_kernel(sent_tiles, tiles, scalars, gen_ref, out_ref):
    start, live = scalars[0], scalars[1]
    for group in range(gen_ref.shape[0] // STEP):
        rows = pl.ds(group * STEP, STEP)
        first_row = start + group * STEP
        diagonal = first_row // LANES
        row_at = first_row + lax.broadcasted_iota(jnp.int32, (STEP, LANES), 0)
        for apart in range(sent_tiles):
            tile = lax.rem(diagonal + apart, tiles)
            column_at = tile * LANES + lax.broadcasted_iota(jnp.int32, (STEP, LANES), 1)
            alive = (row_at < live) & (column_at < live)
            value = gen_ref[rows, tile_at(tile)].astype(F32)
            out_ref[rows, apart * LANES : (apart + 1) * LANES] = jnp.where(
                alive, value, 0.0
            ).astype(BF)


def shifted(value, shift):
    shift = shift % LANES
    return pltpu.roll(value, shift, 1) if shift else value


def lane_index():
    return lax.broadcasted_iota(jnp.int32, (1, LANES), 1)


def laid_out(pieces, half, tile):
    low = tile * LANES
    result = None
    for piece in range(low // half, (low + LANES - 1) // half + 1):
        begin = piece * half - low
        value = pieces(piece, begin)
        result = value if result is None else jnp.where(lane_index() >= begin, value, result)
    return result


def mix(x0, x1, own_ref, far_ref, mixed, half, tile, tiles):
    at = slice(tile * LANES, (tile + 1) * LANES)
    places = [at]
    if (tile + tiles + 1) * LANES <= mixed.shape[2]:
        places.append(slice((tile + tiles) * LANES, (tile + tiles + 1) * LANES))
    for which, weights in enumerate((own_ref, far_ref)):
        top = (x0 * weights[0:1, at] + x1 * weights[1:2, at]).astype(BF)
        low = (x0 * weights[2:3, at] + x1 * weights[3:4, at]).astype(BF)
        for place in places:
            mixed[which, :half, place] = top
            mixed[which, half:, place] = low


def product(got, mixed, total, held, sems, tiles):
    pairs = tiles // 2

    def step(pair, carry):
        rows_of = got[0].shape[1]

        def blocks_before(p):
            return (p * 2 * LANES + rows_of - 1) // rows_of

        @pl.loop(blocks_before(pair), blocks_before(pair + 1))
        def _(block):
            own_copy(got, held, sems, block).wait()
            for part in range(2):
                early_copy(got, held, sems, block, part).wait()

        even = pl.multiple_of(pair * 2 * LANES, 2 * LANES)
        odd = pl.multiple_of(even + LANES, LANES)

        def rows(which, start, low, high):
            return held[which, pl.ds(start, LANES), low * LANES : high * LANES]

        def left(apart, count):
            at = pl.ds(pl.multiple_of(even + apart * LANES, LANES), count * LANES)
            return jnp.concatenate([mixed[0, :, at], mixed[1, :, at]], 1)

        def add(apart, count, value):
            at = pl.multiple_of(even + apart * LANES, LANES)
            total[:, pl.ds(at, count * LANES)] += value

        def straight(a, parts):
            w = jnp.concatenate(parts, 0)
            return jnp.dot(a, w, preferred_element_type=F32)

        def turned(a, parts):
            w = jnp.concatenate(parts, 1)
            return lax.dot_general(a, w, (((1,), (1,)), ((), ())), preferred_element_type=F32)

        def two(start, low, high):
            return [rows(w, start, low, high) for w in range(2)]

        span = pairs
        parts = []
        for w in range(2):
            parts += [rows(w, even, 1, span + 1), rows(w, odd, 0, span)]
        add(1, span, straight(left(0, 2), parts))
        parts = [
            jnp.concatenate([rows(w, even, 2, span), rows(w, odd, 1, span - 1)], 0)
            for w in range(2)
        ]
        add(0, 2, -turned(left(2, span - 2), parts))
        near = straight(left(0, 1), two(even, 0, 1))
        add(0, 1, near - turned(left(1, 1), two(even, 1, 2)))
        add(1, 1, -turned(left(span, 1), two(odd, span - 1, span)))
        add(span + 1, 1, straight(left(1, 1), two(odd, span, span + 1)))
        return carry

    lax.fori_loop(0, pairs, step, 0)


NEAR = (0, -1)
REST = (1, 2)
APART = (0, -1, 1, 2)


def collect_kernel(place, *refs):
    *got, out, sems = refs
    half = got[0].shape[0] // 2
    y, z, side = place[0], place[1], place[2]
    copies = []
    buffer = 0
    for part in range(2):
        for near in (NEAR, REST):
            for second in APART[:3]:
                for piece, first in enumerate(near):
                    dy, dz = (first, second) if part == 0 else (second, first)
                    row = lax.rem(y + dy + side, side)
                    column = lax.rem(z + dz + side, side)
                    copies.append(
                        pltpu.make_async_copy(
                            got[buffer].at[piece * half : (piece + 1) * half],
                            out.at[row * side + column, part * half : (part + 1) * half],
                            sems.at[len(copies)],
                        )
                    )
                buffer += 1
    for copy in copies:
        copy.start()
    for copy in copies:
        copy.wait()


def own_copy(got, held, sems, block):
    rows = got[0].shape[1]
    at = pl.multiple_of(block * rows, rows)
    return pltpu.make_async_copy(
        got[0].at[block], held.at[0, pl.ds(at, rows)], sems.at[0, block]
    )


def half_copy(source, held, sems, block, part):
    half = source.shape[0]
    at = pl.multiple_of((2 * block + part) * half, half)
    return pltpu.make_async_copy(source, held.at[1, pl.ds(at, half)], sems.at[1 + part, block])


def early_copy(got, held, sems, block, part):
    half = got[1].shape[1] // 2
    return half_copy(got[1].at[block, part * half : (part + 1) * half], held, sems, block, part)


def begin(got, place, held, sems):
    y, z, side = place[0], place[1], place[2]
    half = got[1].shape[1] // 2
    buffer = 2
    for part in range(2):
        for near in (NEAR, REST):
            for piece, first in enumerate(near):
                dy, dz = (first, APART[3]) if part == 0 else (APART[3], first)
                block = lax.rem(y + dy + side, side) * side + lax.rem(z + dz + side, side)
                source = got[buffer].at[piece * half : (piece + 1) * half]
                half_copy(source, held, sems, block, part).start()
            buffer += 1

    @pl.loop(0, got[0].shape[0])
    def _(block):
        own_copy(got, held, sems, block).start()
        for part, across in enumerate((lax.rem(block, side) - z, block // side - y)):

            @pl.when(lax.rem(across + side, side) != APART[3])
            def _(part=part):
                early_copy(got, held, sems, block, part).start()


def folded(total, tile, tiles):
    at = slice(tile * LANES, (tile + 1) * LANES)
    value = total[:, at]
    if (tile + tiles + 1) * LANES <= total.shape[1]:
        value = value + total[:, (tile + tiles) * LANES : (tile + tiles + 1) * LANES]
    return value.astype(BF)


def pack_columns(c_ref, columns, half):
    count = c_ref.shape[1] // half
    rest = c_ref.shape[0] - LANES
    for tile in range(c_ref.shape[1] // LANES):
        block = c_ref[:LANES, tile * LANES : (tile + 1) * LANES].astype(F32).T.astype(BF)
        step = 16
        for k in range(LANES // step):
            row = tile * LANES + k * step
            columns[row // half, row % half : row % half + step, :] = block[k * step : (k + 1) * step]
    for piece in range(count):
        tile, off = divmod(piece * half, LANES)
        tail = slice(LANES, LANES + rest)
        value = shifted(c_ref[tail, tile * LANES : (tile + 1) * LANES].astype(F32), -off)
        if off + half > LANES:
            more = c_ref[tail, (tile + 1) * LANES : (tile + 2) * LANES].astype(F32)
            value = jnp.where(lane_index() < LANES - off, value, shifted(more, -off))
        columns[piece, half : half + rest, :] = value.astype(BF)


def flipped_tiles(got_ref, turned, half, tile):
    rest = 2 * half - LANES
    group = LANES // rest
    kept = half - rest

    def near(s, begin):
        return shifted(got_ref[s, :half, :].astype(F32), begin)

    def far(s, begin):
        front = shifted(got_ref[s, :half, :].astype(F32), begin - half)
        back = turned[s // group, :half, :]
        back = shifted(back, begin + kept - rest * (s % group))
        return jnp.where(lane_index() >= begin + kept, back, front)

    return laid_out(near, half, tile), laid_out(far, half, tile)


def turn_rest(got_ref, turned, half):
    rest = 2 * half - LANES
    group = LANES // rest
    for k in range(got_ref.shape[0] // group):
        block = jnp.concatenate(
            [got_ref[k * group + m, half : half + rest, :].astype(F32) for m in range(group)], 0
        )
        turned[k] = block.T


def finish_products(c_out, total, tiles):
    for tile in range(tiles):
        c_out[:, tile * LANES : (tile + 1) * LANES] = folded(total, tile, tiles)


def first_kernel(half, tiles, place, x_ref, own_ref, far_ref, *refs):
    *got, c_out, columns, mixed, total, held, sems = refs
    begin(got, place, held, sems)
    for tile in range(tiles):
        at = slice(tile * LANES, (tile + 1) * LANES)
        x0, x1 = x_ref[:half, at].astype(F32), x_ref[half:, at].astype(F32)
        mix(x0, x1, own_ref, far_ref, mixed, half, tile, tiles)
    total[...] = jnp.zeros_like(total)
    product(got, mixed, total, held, sems, tiles)
    finish_products(c_out, total, tiles)
    pack_columns(c_out, columns, half)


def update(half, tiles, scale, c_ref, back_ref, own_ref, far_ref, mixed, turned, keep):
    turn_rest(back_ref, turned, half)
    for tile in range(tiles):
        at = slice(tile * LANES, (tile + 1) * LANES)
        xs = []
        for channel, flipped in enumerate(flipped_tiles(back_ref, turned, half, tile)):
            rows = slice(channel * half, (channel + 1) * half)
            increment = (c_ref[rows, at].astype(F32) + flipped) * scale
            keep(rows, at, increment)
            xs.append(increment.astype(BF).astype(F32))
        mix(xs[0], xs[1], own_ref, far_ref, mixed, half, tile, tiles)


def middle_kernel(half, tiles, scale, place, c_ref, back_ref, own_ref, far_ref, *refs):
    *got, c_out, run_out, columns, mixed, total, held, sems, turned = refs
    begin(got, place, held, sems)

    def keep(rows, at, increment):
        run_out[rows, at] = increment

    update(half, tiles, scale, c_ref, back_ref, own_ref, far_ref, mixed, turned, keep)
    total[...] = jnp.zeros_like(total)
    product(got, mixed, total, held, sems, tiles)
    finish_products(c_out, total, tiles)
    pack_columns(c_out, columns, half)


def last_kernel(
    half, tiles, scale, last_scale, place, c_ref, back_ref, run_ref, own_ref, far_ref, *refs
):
    *got, leave, stay, columns, mixed, total, held, sems, turned, run, turned_all = refs
    begin(got, place, held, sems)

    def keep(rows, at, increment):
        run[rows, at] = run_ref[rows, at] + increment

    update(half, tiles, scale, c_ref, back_ref, own_ref, far_ref, mixed, turned, keep)
    total[...] = jnp.zeros_like(total)
    product(got, mixed, total, held, sems, tiles)
    first = place[3] != 0
    filler = jnp.zeros((LANES - half, LANES), F32)
    for tile in range(tiles):
        at = slice(tile * LANES, (tile + 1) * LANES)
        value = folded(total, tile, tiles).astype(F32)
        for channel in range(2):
            block = jnp.concatenate([value[channel * half : (channel + 1) * half], filler])
            turned_all[channel, at, :] = block.T
        both = run[:, at] + value * last_scale
        leave[:, at] = jnp.where(first, both[half:], both[:half]).astype(BF)
        stay[:, at] = jnp.where(first, both[:half], both[half:])
    tall, spare = 2 * half, LANES - half
    high = columns.shape[2]
    for channel in range(2):
        for row in range(columns.shape[1]):
            base = turned_all[channel, row * tall : row * tall + high]
            tail = turned_all[channel, row * tall + high : (row + 1) * tall]
            side = jnp.concatenate([shifted(tail, half), shifted(tail, half - spare)])
            side = jnp.concatenate([side, jnp.zeros((high - side.shape[0], LANES), F32)])
            columns[channel, row] = jnp.where(lane_index() < half, base, side).astype(BF)


def end_kernel(half, scale, first_ref, ham_ref, stay_ref, land_ref, got_ref, out_ref):
    first = first_ref[0] != 0

    spare = LANES - half
    left_over = 2 * half - got_ref.shape[2]

    def piece(s, begin):
        block = got_ref[s % 2, s // 2].astype(F32)
        front = shifted(block[:left_over], begin - half)
        back = shifted(block[left_over : 2 * left_over], begin - half + spare)
        tail = jnp.where(lane_index() >= begin + spare, back, front)
        return jnp.concatenate([shifted(block, begin), tail])

    for tile in range(ham_ref.shape[1] // LANES):
        at = slice(tile * LANES, (tile + 1) * LANES)
        total = ham_ref[:, at].astype(F32) + laid_out(piece, half, tile) * scale
        stay, land = stay_ref[:, at], land_ref[:, at].astype(F32)
        out_ref[:half, at] = total[:half] + jnp.where(first, stay, land)
        out_ref[half:, at] = total[half:] + jnp.where(first, land, stay)


def call(kernel, out_shape, specs, name, scratch=(), cost=None, megabytes=16):
    single = not isinstance(out_shape, (list, tuple))
    return pl.pallas_call(
        kernel,
        out_shape=out_shape,
        in_specs=specs,
        out_specs=VMEM if single else [VMEM] * len(out_shape),
        scratch_shapes=scratch,
        compiler_params=pltpu.CompilerParams(vmem_limit_bytes=megabytes << 20),
        cost_estimate=cost,
        name=name,
    )


def passed(value, axis, apart):
    size = lax.axis_size(axis)
    return lax.ppermute(value, axis, [(i, (i + apart) % size) for i in range(size)])


def both_ways(value, one, other):
    by_one = {0: value, -1: passed(value, one, 1), 1: passed(value, one, -1)}
    by_one[2] = passed(value, one, 2)
    near = jnp.concatenate([by_one[k] for k in NEAR])
    rest = jnp.concatenate([by_one[k] for k in REST])
    near_up, near_down = passed(near, other, 1), passed(near, other, -1)
    rest_up, rest_down = passed(rest, other, 1), passed(rest, other, -1)
    return [
        near, near_up, near_down, passed(near_up, other, 1),
        rest, rest_up, rest_down, passed(rest_down, other, -1),
    ]


def swapped(value):
    return lax.ppermute(value, "hi", [(0, 1), (1, 0)])


def on_device(
    generator, hamiltonian, live_states, pp_occupation, ph_occupation, ph_order, recoupling
):
    row_count = generator.shape[1]
    state_count = generator.shape[2]
    half = row_count // 2
    shard_count = (lax.axis_size("y") * lax.axis_size("z"))
    tiles = state_count // LANES
    sent_tiles = tiles // 2 + 1
    hi = lax.axis_index("hi")
    lo = lax.axis_index("lo")
    my_shard = lax.axis_index(ROW)
    first = hi == 0
    shape = jax.ShapeDtypeStruct
    r0 = recoupling[lo]
    r1 = recoupling[lo + lax.axis_size("lo")]
    positions = jnp.arange(state_count, dtype=jnp.int32)
    share = call(
        functools.partial(pack_kernel, sent_tiles, tiles),
        shape((row_count, sent_tiles * LANES), BF),
        [SMEM, VMEM],
        "pack",
    )(jnp.stack([my_shard * row_count, live_states[0]]), generator[0])
    gathered = lax.all_gather(share, ROW, axis=0, tiled=False)
    pieces = both_ways(swapped(share[:half]), "y", "z")
    pieces += both_ways(swapped(share[half:]), "z", "y")
    ph_order, ph_occupation, pp_occupation, hamiltonian, live_states, _, _ = (
        lax.optimization_barrier(
            (
                ph_order, ph_occupation, pp_occupation, hamiltonian, live_states,
                pieces[4], pieces[12],
            )
        )
    )
    live_count = live_states[0]
    column_alive = positions < live_count
    row_alive = my_shard * row_count + jnp.arange(row_count, dtype=jnp.int32) < live_count
    block_alive = row_alive[:, None] & column_alive[None, :]
    place = jnp.stack(
        [lax.axis_index("y"), lax.axis_index("z"), lax.axis_size("y"), first.astype(jnp.int32)]
    ).astype(jnp.int32)
    early = [piece for k, piece in enumerate(pieces) if k % 4 != 3]
    late = [piece for k, piece in enumerate(pieces) if k % 4 == 3]

    collected = pl.pallas_call(
        collect_kernel,
        out_shape=shape(gathered.shape, BF),
        in_specs=[SMEM] + [pl.BlockSpec(memory_space=pl.ANY)] * len(early),
        out_specs=pl.BlockSpec(memory_space=pl.ANY),
        scratch_shapes=[pltpu.SemaphoreType.DMA((2 * len(early),))],
        cost_estimate=pl.CostEstimate(
            flops=0, bytes_accessed=2 * sum(x.size for x in early), transcendentals=0
        ),
        compiler_params=pltpu.CompilerParams(vmem_limit_bytes=32 << 20),
        name="collect",
    )(place, *early)
    gathered = [gathered, collected] + late

    pp = jnp.where(column_alive, pp_occupation[0], 0)
    ph = jnp.zeros((state_count,), jnp.int32).at[ph_order[0]].set(ph_occupation[0])
    ph = jnp.where(column_alive, ph, 0)
    mine = jnp.stack([pp, ph]).astype(F32)
    other = swapped(mine)
    d0, n0 = jnp.where(first, mine, other)
    d1, n1 = jnp.where(first, other, mine)
    a0 = d0 + r0[0] ** 3 * n0 + r1[1] ** 3 * n1
    a1 = d1 + r1[0] ** 3 * n1 + r0[1] ** 3 * n0
    p = r0[0] ** 2 * r0[1] * n0 + r1[1] ** 2 * r1[0] * n1
    q = r1[0] ** 2 * r1[1] * n1 + r0[1] ** 2 * r0[0] * n0
    zero_set = jnp.stack([a0, p, p, q])
    one_set = jnp.stack([p, q, q, a1])
    own_set = jnp.where(first, zero_set, one_set)
    far_set = jnp.where(first, one_set, zero_set)

    own_ham = jnp.where(block_alive, hamiltonian[0], jnp.zeros_like(hamiltonian[0]))
    keep = lax.dynamic_slice_in_dim(own_ham, hi * half, half, 0)
    gone = lax.dynamic_slice_in_dim(own_ham, (1 - hi) * half, half, 0)
    came = swapped(gone)
    current = jnp.concatenate([jnp.where(first, keep, came), jnp.where(first, came, keep)])

    wide = (tiles + sent_tiles - 1) * LANES
    rest = row_count - LANES
    destinations = 2 * shard_count
    scratch = [
        pltpu.VMEM((2, row_count, wide), BF),
        pltpu.VMEM((row_count, wide), F32),
        pltpu.VMEM((2, state_count, sent_tiles * LANES), BF),
        pltpu.SemaphoreType.DMA((3, shard_count)),
    ]
    more = [pltpu.VMEM((destinations * rest // LANES, LANES, LANES), F32)]
    c_shape = shape((row_count, state_count), BF)
    run_shape = shape((row_count, state_count), F32)
    sent_shape = shape((destinations, half + rest, LANES), BF)
    cost = pl.CostEstimate(
        flops=4 * row_count * state_count * state_count,
        bytes_accessed=4 * state_count * sent_tiles * LANES,
        transcendentals=0,
    )

    def exchanged(columns):
        return lax.all_to_all(columns, ("y", "z", "hi"), split_axis=0, concat_axis=0, tiled=True)

    combined, columns = call(
        functools.partial(first_kernel, half, tiles),
        [c_shape, sent_shape],
        [SMEM] + [VMEM] * 3 + [HBM] * len(gathered),
        "first",
        scratch,
        cost,
        46,
    )(place, current, own_set, far_set, *gathered)
    back = exchanged(columns)
    combined, running, columns = call(
        functools.partial(middle_kernel, half, tiles, -1.0),
        [c_shape, run_shape, sent_shape],
        [SMEM] + [VMEM] * 4 + [HBM] * len(gathered),
        "middle",
        scratch + more,
        cost,
        46,
    )(place, combined, back, own_set, far_set, *gathered)
    back = exchanged(columns)
    which = first.astype(jnp.int32)[None]
    leaving, staying, blocks = call(
        functools.partial(last_kernel, half, tiles, -0.5, -1.0 / TERMS),
        [
            shape((half, state_count), BF),
            shape((half, state_count), F32),
            shape((2, shard_count, half + rest, LANES), BF),
        ],
        [SMEM] + [VMEM] * 5 + [HBM] * len(gathered),
        "last",
        scratch
        + more
        + [pltpu.VMEM((row_count, state_count), F32), pltpu.VMEM((2, state_count, LANES), F32)],
        cost,
        46,
    )(place, combined, back, running, own_set, far_set, *gathered)
    landed = swapped(leaving)
    got = lax.all_to_all(
        blocks.reshape(destinations, half + rest, LANES),
        ("hi", "y", "z"),
        split_axis=0,
        concat_axis=0,
        tiled=True,
    )
    result = call(
        functools.partial(end_kernel, half, -1.0 / TERMS),
        shape((row_count, state_count), F32),
        [SMEM] + [VMEM] * 4,
        "finish",
    )(which, own_ham, staying, landed, got.reshape(2, shard_count, half + rest, LANES))
    return result[None]


def solution(mesh):
    chans, rows = mesh.devices.shape
    side = math.isqrt(rows)
    pairs = Mesh(
        mesh.devices.reshape(2, chans // 2, side, rows // side), ("hi", "lo", "y", "z")
    )
    chan = ("hi", "lo")
    placed = (
        P(chan, ROW, None),
        P(chan, ROW, None),
        P(chan),
        P(chan, None),
        P(chan, None),
        P(chan, None),
        P(),
    )
    return jax.shard_map(
        on_device, mesh=pairs, in_specs=placed, out_specs=P(chan, ROW, None), check_vma=False
    )
```

```python
import functools
import math

import jax
import jax.numpy as jnp
from jax import lax
from jax.experimental import pallas as pl
from jax.experimental.pallas import tpu as pltpu
from jax.sharding import Mesh, PartitionSpec as P

TERMS = 3
ROW = ("y", "z")
LANES = 128
STEP = 32
BF = jnp.bfloat16
F32 = jnp.float32
VMEM = pl.BlockSpec(memory_space=pltpu.VMEM)
SMEM = pl.BlockSpec(memory_space=pltpu.SMEM)
HBM = pl.BlockSpec(memory_space=pltpu.HBM)


def tile_at(index):
    return pl.ds(pl.multiple_of(index * LANES, LANES), LANES)


def pack_kernel(sent_tiles, tiles, scalars, gen_ref, out_ref):
    start, live = scalars[0], scalars[1]
    for group in range(gen_ref.shape[0] // STEP):
        rows = pl.ds(group * STEP, STEP)
        first_row = start + group * STEP
        diagonal = first_row // LANES
        row_at = first_row + lax.broadcasted_iota(jnp.int32, (STEP, LANES), 0)
        for apart in range(sent_tiles):
            tile = lax.rem(diagonal + apart, tiles)
            column_at = tile * LANES + lax.broadcasted_iota(jnp.int32, (STEP, LANES), 1)
            alive = (row_at < live) & (column_at < live)
            value = gen_ref[rows, tile_at(tile)].astype(F32)
            out_ref[rows, apart * LANES : (apart + 1) * LANES] = jnp.where(
                alive, value, 0.0
            ).astype(BF)


def shifted(value, shift):
    shift = shift % LANES
    return pltpu.roll(value, shift, 1) if shift else value


def lane_index():
    return lax.broadcasted_iota(jnp.int32, (1, LANES), 1)


def laid_out(pieces, half, tile):
    low = tile * LANES
    result = None
    for piece in range(low // half, (low + LANES - 1) // half + 1):
        begin = piece * half - low
        value = pieces(piece, begin)
        result = value if result is None else jnp.where(lane_index() >= begin, value, result)
    return result


def mix(x0, x1, own_ref, far_ref, mixed, half, tile, tiles):
    at = slice(tile * LANES, (tile + 1) * LANES)
    places = [at]
    if (tile + tiles + 1) * LANES <= mixed.shape[2]:
        places.append(slice((tile + tiles) * LANES, (tile + tiles + 1) * LANES))
    for which, weights in enumerate((own_ref, far_ref)):
        top = (x0 * weights[0:1, at] + x1 * weights[1:2, at]).astype(BF)
        low = (x0 * weights[2:3, at] + x1 * weights[3:4, at]).astype(BF)
        for place in places:
            mixed[which, :half, place] = top
            mixed[which, half:, place] = low


def product(got, mixed, total, held, sems, tiles):
    pairs = tiles // 2

    def step(pair, carry):
        rows_of = got[0].shape[1]

        def blocks_before(p):
            return (p * 2 * LANES + rows_of - 1) // rows_of

        @pl.loop(blocks_before(pair), blocks_before(pair + 1))
        def _(block):
            for which in range(2):
                block_copy(got, held, sems, which, block).wait()

        even = pl.multiple_of(pair * 2 * LANES, 2 * LANES)
        odd = pl.multiple_of(even + LANES, LANES)

        def rows(which, start, low, high):
            return held[which, pl.ds(start, LANES), low * LANES : high * LANES]

        def left(apart, count):
            at = pl.ds(pl.multiple_of(even + apart * LANES, LANES), count * LANES)
            return jnp.concatenate([mixed[0, :, at], mixed[1, :, at]], 1)

        def add(apart, count, value):
            at = pl.multiple_of(even + apart * LANES, LANES)
            total[:, pl.ds(at, count * LANES)] += value

        def straight(a, parts):
            w = jnp.concatenate(parts, 0)
            return jnp.dot(a, w, preferred_element_type=F32)

        def turned(a, parts):
            w = jnp.concatenate(parts, 1)
            return lax.dot_general(a, w, (((1,), (1,)), ((), ())), preferred_element_type=F32)

        def two(start, low, high):
            return [rows(w, start, low, high) for w in range(2)]

        span = pairs
        parts = []
        for w in range(2):
            parts += [rows(w, even, 1, span + 1), rows(w, odd, 0, span)]
        add(1, span, straight(left(0, 2), parts))
        parts = [
            jnp.concatenate([rows(w, even, 2, span), rows(w, odd, 1, span - 1)], 0)
            for w in range(2)
        ]
        add(0, 2, -turned(left(2, span - 2), parts))
        near = straight(left(0, 1), two(even, 0, 1))
        add(0, 1, near - turned(left(1, 1), two(even, 1, 2)))
        add(1, 1, -turned(left(span, 1), two(odd, span - 1, span)))
        add(span + 1, 1, straight(left(1, 1), two(odd, span, span + 1)))
        return carry

    lax.fori_loop(0, pairs, step, 0)


NEAR = (0, -1)
REST = (1, 2)
APART = (0, -1, 1, 2)


def collect_kernel(late, place, *refs):
    *got, out, sems = refs
    got = got[1:] if late else got
    half = got[0].shape[0] // 2
    y, z, side = place[0], place[1], place[2]
    copies = []
    buffer = 0
    for part in range(2):
        for near in (NEAR, REST):
            for second in APART[3:] if late else APART[:3]:
                for piece, first in enumerate(near):
                    dy, dz = (first, second) if part == 0 else (second, first)
                    row = lax.rem(y + dy + side, side)
                    column = lax.rem(z + dz + side, side)
                    copies.append(
                        pltpu.make_async_copy(
                            got[buffer].at[piece * half : (piece + 1) * half],
                            out.at[row * side + column, part * half : (part + 1) * half],
                            sems.at[len(copies)],
                        )
                    )
                buffer += 1
    for copy in copies:
        copy.start()
    for copy in copies:
        copy.wait()


def block_copy(got, held, sems, which, block):
    rows = got[which].shape[1]
    at = pl.multiple_of(block * rows, rows)
    return pltpu.make_async_copy(
        got[which].at[block], held.at[which, pl.ds(at, rows)], sems.at[which, block]
    )


def begin(got, held, sems):
    @pl.loop(0, got[0].shape[0])
    def _(block):
        for which in range(2):
            block_copy(got, held, sems, which, block).start()


def folded(total, tile, tiles):
    at = slice(tile * LANES, (tile + 1) * LANES)
    value = total[:, at]
    if (tile + tiles + 1) * LANES <= total.shape[1]:
        value = value + total[:, (tile + tiles) * LANES : (tile + tiles + 1) * LANES]
    return value.astype(BF)


def pack_columns(c_ref, columns, half):
    count = c_ref.shape[1] // half
    rest = c_ref.shape[0] - LANES
    for tile in range(c_ref.shape[1] // LANES):
        block = c_ref[:LANES, tile * LANES : (tile + 1) * LANES].astype(F32).T.astype(BF)
        step = 16
        for k in range(LANES // step):
            row = tile * LANES + k * step
            columns[row // half, row % half : row % half + step, :] = block[k * step : (k + 1) * step]
    for piece in range(count):
        tile, off = divmod(piece * half, LANES)
        tail = slice(LANES, LANES + rest)
        value = shifted(c_ref[tail, tile * LANES : (tile + 1) * LANES].astype(F32), -off)
        if off + half > LANES:
            more = c_ref[tail, (tile + 1) * LANES : (tile + 2) * LANES].astype(F32)
            value = jnp.where(lane_index() < LANES - off, value, shifted(more, -off))
        columns[piece, half : half + rest, :] = value.astype(BF)


def flipped_tiles(got_ref, turned, half, tile):
    rest = 2 * half - LANES
    group = LANES // rest
    kept = half - rest

    def near(s, begin):
        return shifted(got_ref[s, :half, :].astype(F32), begin)

    def far(s, begin):
        front = shifted(got_ref[s, :half, :].astype(F32), begin - half)
        back = turned[s // group, :half, :]
        back = shifted(back, begin + kept - rest * (s % group))
        return jnp.where(lane_index() >= begin + kept, back, front)

    return laid_out(near, half, tile), laid_out(far, half, tile)


def turn_rest(got_ref, turned, half):
    rest = 2 * half - LANES
    group = LANES // rest
    for k in range(got_ref.shape[0] // group):
        block = jnp.concatenate(
            [got_ref[k * group + m, half : half + rest, :].astype(F32) for m in range(group)], 0
        )
        turned[k] = block.T


def finish_products(c_out, total, tiles):
    for tile in range(tiles):
        c_out[:, tile * LANES : (tile + 1) * LANES] = folded(total, tile, tiles)


def start_kernel(half, tiles, x_ref, own_ref, far_ref, mixed):
    for tile in range(tiles):
        at = slice(tile * LANES, (tile + 1) * LANES)
        x0, x1 = x_ref[:half, at].astype(F32), x_ref[half:, at].astype(F32)
        mix(x0, x1, own_ref, far_ref, mixed, half, tile, tiles)


def first_kernel(half, tiles, place, mixed, *refs):
    *got, c_out, columns, total, held, sems = refs
    begin(got, held, sems)
    total[...] = jnp.zeros_like(total)
    product(got, mixed, total, held, sems, tiles)
    finish_products(c_out, total, tiles)
    pack_columns(c_out, columns, half)


def update(half, tiles, scale, c_ref, back_ref, own_ref, far_ref, mixed, turned, keep):
    turn_rest(back_ref, turned, half)
    for tile in range(tiles):
        at = slice(tile * LANES, (tile + 1) * LANES)
        xs = []
        for channel, flipped in enumerate(flipped_tiles(back_ref, turned, half, tile)):
            rows = slice(channel * half, (channel + 1) * half)
            increment = (c_ref[rows, at].astype(F32) + flipped) * scale
            keep(rows, at, increment)
            xs.append(increment.astype(BF).astype(F32))
        mix(xs[0], xs[1], own_ref, far_ref, mixed, half, tile, tiles)


def middle_kernel(half, tiles, scale, place, c_ref, back_ref, own_ref, far_ref, *refs):
    *got, c_out, run_out, columns, mixed, total, held, sems, turned = refs
    begin(got, held, sems)

    def keep(rows, at, increment):
        run_out[rows, at] = increment

    update(half, tiles, scale, c_ref, back_ref, own_ref, far_ref, mixed, turned, keep)
    total[...] = jnp.zeros_like(total)
    product(got, mixed, total, held, sems, tiles)
    finish_products(c_out, total, tiles)
    pack_columns(c_out, columns, half)


def last_kernel(
    half, tiles, scale, last_scale, place, c_ref, back_ref, run_ref, own_ref, far_ref, *refs
):
    *got, leave, stay, columns, mixed, total, held, sems, turned, run, turned_all = refs
    begin(got, held, sems)

    def keep(rows, at, increment):
        run[rows, at] = run_ref[rows, at] + increment

    update(half, tiles, scale, c_ref, back_ref, own_ref, far_ref, mixed, turned, keep)
    total[...] = jnp.zeros_like(total)
    product(got, mixed, total, held, sems, tiles)
    first = place[3] != 0
    filler = jnp.zeros((LANES - half, LANES), F32)
    for tile in range(tiles):
        at = slice(tile * LANES, (tile + 1) * LANES)
        value = folded(total, tile, tiles).astype(F32)
        for channel in range(2):
            block = jnp.concatenate([value[channel * half : (channel + 1) * half], filler])
            turned_all[channel, at, :] = block.T
        both = run[:, at] + value * last_scale
        leave[:, at] = jnp.where(first, both[half:], both[:half]).astype(BF)
        stay[:, at] = jnp.where(first, both[:half], both[half:])
    tall, spare = 2 * half, LANES - half
    high = columns.shape[2]
    for channel in range(2):
        for row in range(columns.shape[1]):
            base = turned_all[channel, row * tall : row * tall + high]
            tail = turned_all[channel, row * tall + high : (row + 1) * tall]
            side = jnp.concatenate([shifted(tail, half), shifted(tail, half - spare)])
            side = jnp.concatenate([side, jnp.zeros((high - side.shape[0], LANES), F32)])
            columns[channel, row] = jnp.where(lane_index() < half, base, side).astype(BF)


def end_kernel(half, scale, first_ref, ham_ref, stay_ref, land_ref, got_ref, out_ref):
    first = first_ref[0] != 0

    spare = LANES - half
    left_over = 2 * half - got_ref.shape[2]

    def piece(s, begin):
        block = got_ref[s % 2, s // 2].astype(F32)
        front = shifted(block[:left_over], begin - half)
        back = shifted(block[left_over : 2 * left_over], begin - half + spare)
        tail = jnp.where(lane_index() >= begin + spare, back, front)
        return jnp.concatenate([shifted(block, begin), tail])

    for tile in range(ham_ref.shape[1] // LANES):
        at = slice(tile * LANES, (tile + 1) * LANES)
        total = ham_ref[:, at].astype(F32) + laid_out(piece, half, tile) * scale
        stay, land = stay_ref[:, at], land_ref[:, at].astype(F32)
        out_ref[:half, at] = total[:half] + jnp.where(first, stay, land)
        out_ref[half:, at] = total[half:] + jnp.where(first, land, stay)


def call(kernel, out_shape, specs, name, scratch=(), cost=None, megabytes=16):
    single = not isinstance(out_shape, (list, tuple))
    return pl.pallas_call(
        kernel,
        out_shape=out_shape,
        in_specs=specs,
        out_specs=VMEM if single else [VMEM] * len(out_shape),
        scratch_shapes=scratch,
        compiler_params=pltpu.CompilerParams(vmem_limit_bytes=megabytes << 20),
        cost_estimate=cost,
        name=name,
    )


def passed(value, axis, apart):
    size = lax.axis_size(axis)
    return lax.ppermute(value, axis, [(i, (i + apart) % size) for i in range(size)])


def both_ways(value, one, other):
    by_one = {0: value, -1: passed(value, one, 1), 1: passed(value, one, -1)}
    by_one[2] = passed(value, one, 2)
    near = jnp.concatenate([by_one[k] for k in NEAR])
    rest = jnp.concatenate([by_one[k] for k in REST])
    near_up, near_down = passed(near, other, 1), passed(near, other, -1)
    rest_up, rest_down = passed(rest, other, 1), passed(rest, other, -1)
    return [
        near, near_up, near_down, passed(near_up, other, 1),
        rest, rest_up, rest_down, passed(rest_down, other, -1),
    ]


def swapped(value):
    return lax.ppermute(value, "hi", [(0, 1), (1, 0)])


def on_device(
    generator, hamiltonian, live_states, pp_occupation, ph_occupation, ph_order, recoupling
):
    row_count = generator.shape[1]
    state_count = generator.shape[2]
    half = row_count // 2
    shard_count = (lax.axis_size("y") * lax.axis_size("z"))
    tiles = state_count // LANES
    sent_tiles = tiles // 2 + 1
    hi = lax.axis_index("hi")
    lo = lax.axis_index("lo")
    my_shard = lax.axis_index(ROW)
    first = hi == 0
    shape = jax.ShapeDtypeStruct
    r0 = recoupling[lo]
    r1 = recoupling[lo + lax.axis_size("lo")]
    positions = jnp.arange(state_count, dtype=jnp.int32)
    share = call(
        functools.partial(pack_kernel, sent_tiles, tiles),
        shape((row_count, sent_tiles * LANES), BF),
        [SMEM, VMEM],
        "pack",
    )(jnp.stack([my_shard * row_count, live_states[0]]), generator[0])
    far_share = swapped(share)
    gathered = lax.all_gather(share, ROW, axis=0, tiled=False)
    pieces = both_ways(far_share[:half], "y", "z") + both_ways(far_share[half:], "z", "y")
    ph_order, ph_occupation, pp_occupation, hamiltonian, live_states, _, _ = (
        lax.optimization_barrier(
            (
                ph_order, ph_occupation, pp_occupation, hamiltonian, live_states,
                pieces[4], pieces[12],
            )
        )
    )
    live_count = live_states[0]
    column_alive = positions < live_count
    row_alive = my_shard * row_count + jnp.arange(row_count, dtype=jnp.int32) < live_count
    block_alive = row_alive[:, None] & column_alive[None, :]
    place = jnp.stack(
        [lax.axis_index("y"), lax.axis_index("z"), lax.axis_size("y"), first.astype(jnp.int32)]
    ).astype(jnp.int32)
    early = [piece for k, piece in enumerate(pieces) if k % 4 != 3]
    late = [piece for k, piece in enumerate(pieces) if k % 4 == 3]

    def collect(is_late, parts, aliases):
        return pl.pallas_call(
            functools.partial(collect_kernel, is_late),
            out_shape=shape(gathered.shape, BF),
            in_specs=[SMEM, pl.BlockSpec(memory_space=pl.ANY)]
            + [VMEM if is_late else pl.BlockSpec(memory_space=pl.ANY)] * (len(parts) - 1),
            out_specs=pl.BlockSpec(memory_space=pl.ANY),
            scratch_shapes=[pltpu.SemaphoreType.DMA((2 * len(parts),))],
            input_output_aliases=aliases,
            cost_estimate=pl.CostEstimate(
                flops=0, bytes_accessed=2 * sum(x.size for x in parts), transcendentals=0
            ),
            compiler_params=pltpu.CompilerParams(vmem_limit_bytes=(50 if is_late else 32) << 20),
            name="collect",
        )(place, *parts)

    collected = collect(False, early, {})
    collected = collect(True, [collected] + late, {1: 0})
    gathered = [gathered, collected]

    pp = jnp.where(column_alive, pp_occupation[0], 0)
    ph = jnp.zeros((state_count,), jnp.int32).at[ph_order[0]].set(ph_occupation[0])
    ph = jnp.where(column_alive, ph, 0)
    mine = jnp.stack([pp, ph]).astype(F32)
    other = swapped(mine)
    d0, n0 = jnp.where(first, mine, other)
    d1, n1 = jnp.where(first, other, mine)
    a0 = d0 + r0[0] ** 3 * n0 + r1[1] ** 3 * n1
    a1 = d1 + r1[0] ** 3 * n1 + r0[1] ** 3 * n0
    p = r0[0] ** 2 * r0[1] * n0 + r1[1] ** 2 * r1[0] * n1
    q = r1[0] ** 2 * r1[1] * n1 + r0[1] ** 2 * r0[0] * n0
    zero_set = jnp.stack([a0, p, p, q])
    one_set = jnp.stack([p, q, q, a1])
    own_set = jnp.where(first, zero_set, one_set)
    far_set = jnp.where(first, one_set, zero_set)

    own_ham = jnp.where(block_alive, hamiltonian[0], jnp.zeros_like(hamiltonian[0]))
    keep = lax.dynamic_slice_in_dim(own_ham, hi * half, half, 0)
    gone = lax.dynamic_slice_in_dim(own_ham, (1 - hi) * half, half, 0)
    came = swapped(gone)
    current = jnp.concatenate([jnp.where(first, keep, came), jnp.where(first, came, keep)])

    wide = (tiles + sent_tiles - 1) * LANES
    rest = row_count - LANES
    destinations = 2 * shard_count
    scratch = [
        pltpu.VMEM((2, row_count, wide), BF),
        pltpu.VMEM((row_count, wide), F32),
        pltpu.VMEM((2, state_count, sent_tiles * LANES), BF),
        pltpu.SemaphoreType.DMA((2, shard_count)),
    ]
    more = [pltpu.VMEM((destinations * rest // LANES, LANES, LANES), F32)]
    c_shape = shape((row_count, state_count), BF)
    run_shape = shape((row_count, state_count), F32)
    sent_shape = shape((destinations, half + rest, LANES), BF)
    cost = pl.CostEstimate(
        flops=4 * row_count * state_count * state_count,
        bytes_accessed=4 * state_count * sent_tiles * LANES,
        transcendentals=0,
    )

    def exchanged(columns):
        return lax.all_to_all(columns, ("y", "z", "hi"), split_axis=0, concat_axis=0, tiled=True)

    mixed = call(
        functools.partial(start_kernel, half, tiles),
        shape((2, row_count, wide), BF),
        [VMEM] * 3,
        "start",
    )(current, own_set, far_set)
    combined, columns = call(
        functools.partial(first_kernel, half, tiles),
        [c_shape, sent_shape],
        [SMEM, VMEM] + [HBM] * len(gathered),
        "first",
        scratch[1:],
        cost,
        48,
    )(place, mixed, *gathered)
    back = exchanged(columns)
    combined, running, columns = call(
        functools.partial(middle_kernel, half, tiles, -1.0),
        [c_shape, run_shape, sent_shape],
        [SMEM] + [VMEM] * 4 + [HBM] * len(gathered),
        "middle",
        scratch + more,
        cost,
        48,
    )(place, combined, back, own_set, far_set, *gathered)
    back = exchanged(columns)
    which = first.astype(jnp.int32)[None]
    leaving, staying, blocks = call(
        functools.partial(last_kernel, half, tiles, -0.5, -1.0 / TERMS),
        [
            shape((half, state_count), BF),
            shape((half, state_count), F32),
            shape((2, shard_count, half + rest, LANES), BF),
        ],
        [SMEM] + [VMEM] * 5 + [HBM] * len(gathered),
        "last",
        scratch
        + more
        + [pltpu.VMEM((row_count, state_count), F32), pltpu.VMEM((2, state_count, LANES), F32)],
        cost,
        48,
    )(place, combined, back, running, own_set, far_set, *gathered)
    landed = swapped(leaving)
    got = lax.all_to_all(
        blocks.reshape(destinations, half + rest, LANES),
        ("hi", "y", "z"),
        split_axis=0,
        concat_axis=0,
        tiled=True,
    )
    result = call(
        functools.partial(end_kernel, half, -1.0 / TERMS),
        shape((row_count, state_count), F32),
        [SMEM] + [VMEM] * 4,
        "finish",
    )(which, own_ham, staying, landed, got.reshape(2, shard_count, half + rest, LANES))
    return result[None]


def solution(mesh):
    chans, rows = mesh.devices.shape
    side = math.isqrt(rows)
    pairs = Mesh(
        mesh.devices.reshape(2, chans // 2, side, rows // side), ("hi", "lo", "y", "z")
    )
    chan = ("hi", "lo")
    placed = (
        P(chan, ROW, None),
        P(chan, ROW, None),
        P(chan),
        P(chan, None),
        P(chan, None),
        P(chan, None),
        P(),
    )
    return jax.shard_map(
        on_device, mesh=pairs, in_specs=placed, out_specs=P(chan, ROW, None), check_vma=False
    )
```

```python
import functools
import math

import jax
import jax.numpy as jnp
from jax import lax
from jax.experimental import pallas as pl
from jax.experimental.pallas import tpu as pltpu
from jax.sharding import Mesh, PartitionSpec as P

TERMS = 3
ROW = ("y", "z")
LANES = 128
STEP = 32
BF = jnp.bfloat16
F32 = jnp.float32
VMEM = pl.BlockSpec(memory_space=pltpu.VMEM)
SMEM = pl.BlockSpec(memory_space=pltpu.SMEM)
HBM = pl.BlockSpec(memory_space=pltpu.HBM)


def tile_at(index):
    return pl.ds(pl.multiple_of(index * LANES, LANES), LANES)


def pack_kernel(sent_tiles, tiles, scalars, gen_ref, out_ref):
    start, live = scalars[0], scalars[1]
    for group in range(gen_ref.shape[0] // STEP):
        rows = pl.ds(group * STEP, STEP)
        first_row = start + group * STEP
        diagonal = first_row // LANES
        row_at = first_row + lax.broadcasted_iota(jnp.int32, (STEP, LANES), 0)
        for apart in range(sent_tiles):
            tile = lax.rem(diagonal + apart, tiles)
            column_at = tile * LANES + lax.broadcasted_iota(jnp.int32, (STEP, LANES), 1)
            alive = (row_at < live) & (column_at < live)
            value = gen_ref[rows, tile_at(tile)].astype(F32)
            out_ref[rows, apart * LANES : (apart + 1) * LANES] = jnp.where(
                alive, value, 0.0
            ).astype(BF)


def shifted(value, shift):
    shift = shift % LANES
    return pltpu.roll(value, shift, 1) if shift else value


def lane_index():
    return lax.broadcasted_iota(jnp.int32, (1, LANES), 1)


def laid_out(pieces, half, tile):
    low = tile * LANES
    result = None
    for piece in range(low // half, (low + LANES - 1) // half + 1):
        begin = piece * half - low
        value = pieces(piece, begin)
        result = value if result is None else jnp.where(lane_index() >= begin, value, result)
    return result


def mix(x0, x1, own_ref, far_ref, mixed, half, tile, tiles):
    at = slice(tile * LANES, (tile + 1) * LANES)
    places = [at]
    if (tile + tiles + 1) * LANES <= mixed.shape[2]:
        places.append(slice((tile + tiles) * LANES, (tile + tiles + 1) * LANES))
    for which, weights in enumerate((own_ref, far_ref)):
        top = (x0 * weights[0:1, at] + x1 * weights[1:2, at]).astype(BF)
        low = (x0 * weights[2:3, at] + x1 * weights[3:4, at]).astype(BF)
        for place in places:
            mixed[which, :half, place] = top
            mixed[which, half:, place] = low


def product(got, mixed, total, held, sems, tiles):
    pairs = tiles // 2

    def step(pair, carry):
        rows_of = got[0].shape[1]

        def blocks_before(p):
            return (p * 2 * LANES + rows_of - 1) // rows_of

        @pl.loop(blocks_before(pair), blocks_before(pair + 1))
        def _(block):
            for which in range(2):
                block_copy(got, held, sems, which, block).wait()

        even = pl.multiple_of(pair * 2 * LANES, 2 * LANES)
        odd = pl.multiple_of(even + LANES, LANES)

        def rows(which, start, low, high):
            return held[which, pl.ds(start, LANES), low * LANES : high * LANES]

        def left(apart, count):
            at = pl.ds(pl.multiple_of(even + apart * LANES, LANES), count * LANES)
            return jnp.concatenate([mixed[0, :, at], mixed[1, :, at]], 1)

        def add(apart, count, value):
            at = pl.multiple_of(even + apart * LANES, LANES)
            total[:, pl.ds(at, count * LANES)] += value

        def straight(a, parts):
            w = jnp.concatenate(parts, 0)
            return jnp.dot(a, w, preferred_element_type=F32)

        def turned(a, parts):
            w = jnp.concatenate(parts, 1)
            return lax.dot_general(a, w, (((1,), (1,)), ((), ())), preferred_element_type=F32)

        def two(start, low, high):
            return [rows(w, start, low, high) for w in range(2)]

        span = pairs
        parts = []
        for w in range(2):
            parts += [rows(w, even, 1, span + 1), rows(w, odd, 0, span)]
        add(1, span, straight(left(0, 2), parts))
        parts = [
            jnp.concatenate([rows(w, even, 2, span), rows(w, odd, 1, span - 1)], 0)
            for w in range(2)
        ]
        add(0, 2, -turned(left(2, span - 2), parts))
        near = straight(left(0, 1), two(even, 0, 1))
        add(0, 1, near - turned(left(1, 1), two(even, 1, 2)))
        add(1, 1, -turned(left(span, 1), two(odd, span - 1, span)))
        add(span + 1, 1, straight(left(1, 1), two(odd, span, span + 1)))
        return carry

    lax.fori_loop(0, pairs, step, 0)


NEAR = (0, -1)
REST = (1, 2)
APART = (0, -1, 1, 2)


def collect_kernel(late, place, *refs):
    *got, out, sems = refs
    got = got[1:] if late else got
    half = got[0].shape[0] // 2
    y, z, side = place[0], place[1], place[2]
    copies = []
    buffer = 0
    for part in range(2):
        for near in (NEAR, REST):
            for second in APART[3:] if late else APART[:3]:
                for piece, first in enumerate(near):
                    dy, dz = (first, second) if part == 0 else (second, first)
                    row = lax.rem(y + dy + side, side)
                    column = lax.rem(z + dz + side, side)
                    copies.append(
                        pltpu.make_async_copy(
                            got[buffer].at[piece * half : (piece + 1) * half],
                            out.at[row * side + column, part * half : (part + 1) * half],
                            sems.at[len(copies)],
                        )
                    )
                buffer += 1
    for copy in copies:
        copy.start()
    for copy in copies:
        copy.wait()


def block_copy(got, held, sems, which, block):
    rows = got[which].shape[1]
    at = pl.multiple_of(block * rows, rows)
    return pltpu.make_async_copy(
        got[which].at[block], held.at[which, pl.ds(at, rows)], sems.at[which, block]
    )


def begin(got, held, sems):
    @pl.loop(0, got[0].shape[0])
    def _(block):
        for which in range(2):
            block_copy(got, held, sems, which, block).start()


def folded(total, tile, tiles):
    at = slice(tile * LANES, (tile + 1) * LANES)
    value = total[:, at]
    if (tile + tiles + 1) * LANES <= total.shape[1]:
        value = value + total[:, (tile + tiles) * LANES : (tile + tiles + 1) * LANES]
    return value.astype(BF)


def pack_columns(c_ref, columns, half):
    count = c_ref.shape[1] // half
    rest = c_ref.shape[0] - LANES
    for tile in range(c_ref.shape[1] // LANES):
        block = c_ref[:LANES, tile * LANES : (tile + 1) * LANES].astype(F32).T.astype(BF)
        step = 16
        for k in range(LANES // step):
            row = tile * LANES + k * step
            columns[row // half, row % half : row % half + step, :] = block[k * step : (k + 1) * step]
    for piece in range(count):
        tile, off = divmod(piece * half, LANES)
        tail = slice(LANES, LANES + rest)
        value = shifted(c_ref[tail, tile * LANES : (tile + 1) * LANES].astype(F32), -off)
        if off + half > LANES:
            more = c_ref[tail, (tile + 1) * LANES : (tile + 2) * LANES].astype(F32)
            value = jnp.where(lane_index() < LANES - off, value, shifted(more, -off))
        columns[piece, half : half + rest, :] = value.astype(BF)


def flipped_tiles(got_ref, turned, half, tile):
    rest = 2 * half - LANES
    group = LANES // rest
    kept = half - rest

    def near(s, begin):
        return shifted(got_ref[s, :half, :].astype(F32), begin)

    def far(s, begin):
        front = shifted(got_ref[s, :half, :].astype(F32), begin - half)
        back = turned[s // group, :half, :]
        back = shifted(back, begin + kept - rest * (s % group))
        return jnp.where(lane_index() >= begin + kept, back, front)

    return laid_out(near, half, tile), laid_out(far, half, tile)


def turn_rest(got_ref, turned, half):
    rest = 2 * half - LANES
    group = LANES // rest
    for k in range(got_ref.shape[0] // group):
        block = jnp.concatenate(
            [got_ref[k * group + m, half : half + rest, :].astype(F32) for m in range(group)], 0
        )
        turned[k] = block.T


def finish_products(c_out, total, tiles):
    for tile in range(tiles):
        c_out[:, tile * LANES : (tile + 1) * LANES] = folded(total, tile, tiles)


def first_kernel(half, tiles, place, x_ref, own_ref, far_ref, *refs):
    *got, c_out, columns, mixed, total, held, sems = refs
    begin(got, held, sems)
    for tile in range(tiles):
        at = slice(tile * LANES, (tile + 1) * LANES)
        x0, x1 = x_ref[:half, at].astype(F32), x_ref[half:, at].astype(F32)
        mix(x0, x1, own_ref, far_ref, mixed, half, tile, tiles)
    total[...] = jnp.zeros_like(total)
    product(got, mixed, total, held, sems, tiles)
    finish_products(c_out, total, tiles)
    pack_columns(c_out, columns, half)


def update(half, tiles, scale, c_ref, back_ref, own_ref, far_ref, mixed, turned, keep):
    turn_rest(back_ref, turned, half)
    for tile in range(tiles):
        at = slice(tile * LANES, (tile + 1) * LANES)
        xs = []
        for channel, flipped in enumerate(flipped_tiles(back_ref, turned, half, tile)):
            rows = slice(channel * half, (channel + 1) * half)
            increment = (c_ref[rows, at].astype(F32) + flipped) * scale
            keep(rows, at, increment)
            xs.append(increment.astype(BF).astype(F32))
        mix(xs[0], xs[1], own_ref, far_ref, mixed, half, tile, tiles)


def middle_kernel(half, tiles, scale, place, c_ref, back_ref, own_ref, far_ref, *refs):
    *got, c_out, run_out, columns, mixed, total, held, sems, turned = refs
    begin(got, held, sems)

    def keep(rows, at, increment):
        run_out[rows, at] = increment

    update(half, tiles, scale, c_ref, back_ref, own_ref, far_ref, mixed, turned, keep)
    total[...] = jnp.zeros_like(total)
    product(got, mixed, total, held, sems, tiles)
    finish_products(c_out, total, tiles)
    pack_columns(c_out, columns, half)


def last_kernel(
    half, tiles, scale, last_scale, place, c_ref, back_ref, run_ref, own_ref, far_ref, *refs
):
    *got, leave, stay, columns, mixed, total, held, sems, turned, run, turned_all = refs
    begin(got, held, sems)

    def keep(rows, at, increment):
        run[rows, at] = run_ref[rows, at] + increment

    update(half, tiles, scale, c_ref, back_ref, own_ref, far_ref, mixed, turned, keep)
    total[...] = jnp.zeros_like(total)
    product(got, mixed, total, held, sems, tiles)
    first = place[3] != 0
    filler = jnp.zeros((LANES - half, LANES), F32)
    for tile in range(tiles):
        at = slice(tile * LANES, (tile + 1) * LANES)
        value = folded(total, tile, tiles).astype(F32)
        for channel in range(2):
            block = jnp.concatenate([value[channel * half : (channel + 1) * half], filler])
            turned_all[channel, at, :] = block.T
        both = run[:, at] + value * last_scale
        leave[:, at] = jnp.where(first, both[half:], both[:half]).astype(BF)
        stay[:, at] = jnp.where(first, both[:half], both[half:])
    tall, spare = 2 * half, LANES - half
    high = columns.shape[2]
    for channel in range(2):
        for row in range(columns.shape[1]):
            base = turned_all[channel, row * tall : row * tall + high]
            tail = turned_all[channel, row * tall + high : (row + 1) * tall]
            side = jnp.concatenate([shifted(tail, half), shifted(tail, half - spare)])
            side = jnp.concatenate([side, jnp.zeros((high - side.shape[0], LANES), F32)])
            columns[channel, row] = jnp.where(lane_index() < half, base, side).astype(BF)


def end_kernel(half, scale, first_ref, ham_ref, stay_ref, land_ref, got_ref, out_ref):
    first = first_ref[0] != 0

    spare = LANES - half
    left_over = 2 * half - got_ref.shape[2]

    def piece(s, begin):
        block = got_ref[s % 2, s // 2].astype(F32)
        front = shifted(block[:left_over], begin - half)
        back = shifted(block[left_over : 2 * left_over], begin - half + spare)
        tail = jnp.where(lane_index() >= begin + spare, back, front)
        return jnp.concatenate([shifted(block, begin), tail])

    for tile in range(ham_ref.shape[1] // LANES):
        at = slice(tile * LANES, (tile + 1) * LANES)
        total = ham_ref[:, at].astype(F32) + laid_out(piece, half, tile) * scale
        stay, land = stay_ref[:, at], land_ref[:, at].astype(F32)
        out_ref[:half, at] = total[:half] + jnp.where(first, stay, land)
        out_ref[half:, at] = total[half:] + jnp.where(first, land, stay)


def call(kernel, out_shape, specs, name, scratch=(), cost=None, megabytes=16):
    single = not isinstance(out_shape, (list, tuple))
    return pl.pallas_call(
        kernel,
        out_shape=out_shape,
        in_specs=specs,
        out_specs=VMEM if single else [VMEM] * len(out_shape),
        scratch_shapes=scratch,
        compiler_params=pltpu.CompilerParams(vmem_limit_bytes=megabytes << 20),
        cost_estimate=cost,
        name=name,
    )


def passed(value, axis, apart):
    size = lax.axis_size(axis)
    return lax.ppermute(value, axis, [(i, (i + apart) % size) for i in range(size)])


def both_ways(value, one, other):
    by_one = {0: value, -1: passed(value, one, 1), 1: passed(value, one, -1)}
    by_one[2] = passed(value, one, 2)
    near = jnp.concatenate([by_one[k] for k in NEAR])
    rest = jnp.concatenate([by_one[k] for k in REST])
    near_up, near_down = passed(near, other, 1), passed(near, other, -1)
    rest_up, rest_down = passed(rest, other, 1), passed(rest, other, -1)
    return [
        near, near_up, near_down, passed(near_up, other, 1),
        rest, rest_up, rest_down, passed(rest_down, other, -1),
    ]


def swapped(value):
    return lax.ppermute(value, "hi", [(0, 1), (1, 0)])


def on_device(
    generator, hamiltonian, live_states, pp_occupation, ph_occupation, ph_order, recoupling
):
    row_count = generator.shape[1]
    state_count = generator.shape[2]
    half = row_count // 2
    shard_count = (lax.axis_size("y") * lax.axis_size("z"))
    tiles = state_count // LANES
    sent_tiles = tiles // 2 + 1
    hi = lax.axis_index("hi")
    lo = lax.axis_index("lo")
    my_shard = lax.axis_index(ROW)
    first = hi == 0
    shape = jax.ShapeDtypeStruct
    r0 = recoupling[lo]
    r1 = recoupling[lo + lax.axis_size("lo")]
    positions = jnp.arange(state_count, dtype=jnp.int32)
    share = call(
        functools.partial(pack_kernel, sent_tiles, tiles),
        shape((row_count, sent_tiles * LANES), BF),
        [SMEM, VMEM],
        "pack",
    )(jnp.stack([my_shard * row_count, live_states[0]]), generator[0])
    far_share = swapped(share)
    gathered = lax.all_gather(share, ROW, axis=0, tiled=False)
    pieces = both_ways(far_share[:half], "y", "z") + both_ways(far_share[half:], "z", "y")
    ph_order, ph_occupation, pp_occupation, hamiltonian, live_states, _, _ = (
        lax.optimization_barrier(
            (
                ph_order, ph_occupation, pp_occupation, hamiltonian, live_states,
                pieces[4], pieces[12],
            )
        )
    )
    live_count = live_states[0]
    column_alive = positions < live_count
    row_alive = my_shard * row_count + jnp.arange(row_count, dtype=jnp.int32) < live_count
    block_alive = row_alive[:, None] & column_alive[None, :]
    place = jnp.stack(
        [lax.axis_index("y"), lax.axis_index("z"), lax.axis_size("y"), first.astype(jnp.int32)]
    ).astype(jnp.int32)
    early = [piece for k, piece in enumerate(pieces) if k % 4 != 3]
    late = [piece for k, piece in enumerate(pieces) if k % 4 == 3]

    def collect(is_late, parts, aliases):
        return pl.pallas_call(
            functools.partial(collect_kernel, is_late),
            out_shape=shape(gathered.shape, BF),
            in_specs=[SMEM, pl.BlockSpec(memory_space=pl.ANY)]
            + [VMEM if is_late else pl.BlockSpec(memory_space=pl.ANY)] * (len(parts) - 1),
            out_specs=pl.BlockSpec(memory_space=pl.ANY),
            scratch_shapes=[pltpu.SemaphoreType.DMA((2 * len(parts),))],
            input_output_aliases=aliases,
            cost_estimate=pl.CostEstimate(
                flops=0, bytes_accessed=2 * sum(x.size for x in parts), transcendentals=0
            ),
            compiler_params=pltpu.CompilerParams(vmem_limit_bytes=(50 if is_late else 32) << 20),
            name="collect",
        )(place, *parts)

    collected = collect(False, early, {})
    collected = collect(True, [collected] + late, {1: 0})
    gathered = [gathered, collected]

    pp = jnp.where(column_alive, pp_occupation[0], 0)
    ph = jnp.zeros((state_count,), jnp.int32).at[ph_order[0]].set(ph_occupation[0])
    ph = jnp.where(column_alive, ph, 0)
    mine = jnp.stack([pp, ph]).astype(F32)
    other = swapped(mine)
    d0, n0 = jnp.where(first, mine, other)
    d1, n1 = jnp.where(first, other, mine)
    a0 = d0 + r0[0] ** 3 * n0 + r1[1] ** 3 * n1
    a1 = d1 + r1[0] ** 3 * n1 + r0[1] ** 3 * n0
    p = r0[0] ** 2 * r0[1] * n0 + r1[1] ** 2 * r1[0] * n1
    q = r1[0] ** 2 * r1[1] * n1 + r0[1] ** 2 * r0[0] * n0
    zero_set = jnp.stack([a0, p, p, q])
    one_set = jnp.stack([p, q, q, a1])
    own_set = jnp.where(first, zero_set, one_set)
    far_set = jnp.where(first, one_set, zero_set)

    own_ham = jnp.where(block_alive, hamiltonian[0], jnp.zeros_like(hamiltonian[0]))
    keep = lax.dynamic_slice_in_dim(own_ham, hi * half, half, 0)
    gone = lax.dynamic_slice_in_dim(own_ham, (1 - hi) * half, half, 0)
    came = swapped(gone)
    current = jnp.concatenate([jnp.where(first, keep, came), jnp.where(first, came, keep)])

    wide = (tiles + sent_tiles - 1) * LANES
    rest = row_count - LANES
    destinations = 2 * shard_count
    scratch = [
        pltpu.VMEM((2, row_count, wide), BF),
        pltpu.VMEM((row_count, wide), F32),
        pltpu.VMEM((2, state_count, sent_tiles * LANES), BF),
        pltpu.SemaphoreType.DMA((2, shard_count)),
    ]
    more = [pltpu.VMEM((destinations * rest // LANES, LANES, LANES), F32)]
    c_shape = shape((row_count, state_count), BF)
    run_shape = shape((row_count, state_count), F32)
    sent_shape = shape((destinations, half + rest, LANES), BF)
    cost = pl.CostEstimate(
        flops=4 * row_count * state_count * state_count,
        bytes_accessed=4 * state_count * sent_tiles * LANES,
        transcendentals=0,
    )

    def exchanged(columns):
        return lax.all_to_all(columns, ("y", "z", "hi"), split_axis=0, concat_axis=0, tiled=True)

    combined, columns = call(
        functools.partial(first_kernel, half, tiles),
        [c_shape, sent_shape],
        [SMEM] + [VMEM] * 3 + [HBM] * len(gathered),
        "first",
        scratch,
        cost,
        48,
    )(place, current, own_set, far_set, *gathered)
    back = exchanged(columns)
    combined, running, columns = call(
        functools.partial(middle_kernel, half, tiles, -1.0),
        [c_shape, run_shape, sent_shape],
        [SMEM] + [VMEM] * 4 + [HBM] * len(gathered),
        "middle",
        scratch + more,
        cost,
        48,
    )(place, combined, back, own_set, far_set, *gathered)
    back = exchanged(columns)
    which = first.astype(jnp.int32)[None]
    leaving, staying, blocks = call(
        functools.partial(last_kernel, half, tiles, -0.5, -1.0 / TERMS),
        [
            shape((half, state_count), BF),
            shape((half, state_count), F32),
            shape((2, shard_count, half + rest, LANES), BF),
        ],
        [SMEM] + [VMEM] * 5 + [HBM] * len(gathered),
        "last",
        scratch
        + more
        + [pltpu.VMEM((row_count, state_count), F32), pltpu.VMEM((2, state_count, LANES), F32)],
        cost,
        48,
    )(place, combined, back, running, own_set, far_set, *gathered)
    landed = swapped(leaving)
    got = lax.all_to_all(
        blocks.reshape(destinations, half + rest, LANES),
        ("hi", "y", "z"),
        split_axis=0,
        concat_axis=0,
        tiled=True,
    )
    result = call(
        functools.partial(end_kernel, half, -1.0 / TERMS),
        shape((row_count, state_count), F32),
        [SMEM] + [VMEM] * 4,
        "finish",
    )(which, own_ham, staying, landed, got.reshape(2, shard_count, half + rest, LANES))
    return result[None]


def solution(mesh):
    chans, rows = mesh.devices.shape
    side = math.isqrt(rows)
    pairs = Mesh(
        mesh.devices.reshape(2, chans // 2, side, rows // side), ("hi", "lo", "y", "z")
    )
    chan = ("hi", "lo")
    placed = (
        P(chan, ROW, None),
        P(chan, ROW, None),
        P(chan),
        P(chan, None),
        P(chan, None),
        P(chan, None),
        P(),
    )
    return jax.shard_map(
        on_device, mesh=pairs, in_specs=placed, out_specs=P(chan, ROW, None), check_vma=False
    )
```

```python
import functools
import math

import jax
import jax.numpy as jnp
from jax import lax
from jax.experimental import pallas as pl
from jax.experimental.pallas import tpu as pltpu
from jax.sharding import Mesh, PartitionSpec as P

TERMS = 3
ROW = ("y", "z")
LANES = 128
STEP = 32
BF = jnp.bfloat16
F32 = jnp.float32
VMEM = pl.BlockSpec(memory_space=pltpu.VMEM)
SMEM = pl.BlockSpec(memory_space=pltpu.SMEM)
HBM = pl.BlockSpec(memory_space=pltpu.HBM)


def tile_at(index):
    return pl.ds(pl.multiple_of(index * LANES, LANES), LANES)


def pack_kernel(sent_tiles, tiles, scalars, gen_ref, out_ref):
    start, live = scalars[0], scalars[1]
    for group in range(gen_ref.shape[0] // STEP):
        rows = pl.ds(group * STEP, STEP)
        first_row = start + group * STEP
        diagonal = first_row // LANES
        row_at = first_row + lax.broadcasted_iota(jnp.int32, (STEP, LANES), 0)
        for apart in range(sent_tiles):
            tile = lax.rem(diagonal + apart, tiles)
            column_at = tile * LANES + lax.broadcasted_iota(jnp.int32, (STEP, LANES), 1)
            alive = (row_at < live) & (column_at < live)
            value = gen_ref[rows, tile_at(tile)].astype(F32)
            out_ref[rows, apart * LANES : (apart + 1) * LANES] = jnp.where(
                alive, value, 0.0
            ).astype(BF)


def shifted(value, shift):
    shift = shift % LANES
    return pltpu.roll(value, shift, 1) if shift else value


def lane_index():
    return lax.broadcasted_iota(jnp.int32, (1, LANES), 1)


def laid_out(pieces, half, tile):
    low = tile * LANES
    result = None
    for piece in range(low // half, (low + LANES - 1) // half + 1):
        begin = piece * half - low
        value = pieces(piece, begin)
        result = value if result is None else jnp.where(lane_index() >= begin, value, result)
    return result


def mix(x0, x1, own_ref, far_ref, mixed, half, tile, tiles):
    at = slice(tile * LANES, (tile + 1) * LANES)
    places = [at]
    if (tile + tiles + 1) * LANES <= mixed.shape[2]:
        places.append(slice((tile + tiles) * LANES, (tile + tiles + 1) * LANES))
    for which, weights in enumerate((own_ref, far_ref)):
        top = (x0 * weights[0:1, at] + x1 * weights[1:2, at]).astype(BF)
        low = (x0 * weights[2:3, at] + x1 * weights[3:4, at]).astype(BF)
        for place in places:
            mixed[which, :half, place] = top
            mixed[which, half:, place] = low


def product(got, mixed, total, held, sems, tiles):
    pairs = tiles // 2

    def step(pair, carry):
        rows_of = got[0].shape[1]

        def blocks_before(p):
            return (p * 2 * LANES + rows_of - 1) // rows_of

        @pl.loop(blocks_before(pair), blocks_before(pair + 1))
        def _(block):
            for which in range(2):
                block_copy(got, held, sems, which, block).wait()

        even = pl.multiple_of(pair * 2 * LANES, 2 * LANES)
        odd = pl.multiple_of(even + LANES, LANES)

        def rows(which, start, low, high):
            return held[which, pl.ds(start, LANES), low * LANES : high * LANES]

        def left(apart, count):
            at = pl.ds(pl.multiple_of(even + apart * LANES, LANES), count * LANES)
            return jnp.concatenate([mixed[0, :, at], mixed[1, :, at]], 1)

        def add(apart, count, value):
            at = pl.multiple_of(even + apart * LANES, LANES)
            total[:, pl.ds(at, count * LANES)] += value

        def straight(a, parts):
            w = jnp.concatenate(parts, 0)
            return jnp.dot(a, w, preferred_element_type=F32)

        def turned(a, parts):
            w = jnp.concatenate(parts, 1)
            return lax.dot_general(a, w, (((1,), (1,)), ((), ())), preferred_element_type=F32)

        def two(start, low, high):
            return [rows(w, start, low, high) for w in range(2)]

        span = pairs
        parts = []
        for w in range(2):
            parts += [rows(w, even, 1, span + 1), rows(w, odd, 0, span)]
        add(1, span, straight(left(0, 2), parts))
        parts = [
            jnp.concatenate([rows(w, even, 2, span), rows(w, odd, 1, span - 1)], 0)
            for w in range(2)
        ]
        add(0, 2, -turned(left(2, span - 2), parts))
        near = straight(left(0, 1), two(even, 0, 1))
        add(0, 1, near - turned(left(1, 1), two(even, 1, 2)))
        add(1, 1, -turned(left(span, 1), two(odd, span - 1, span)))
        add(span + 1, 1, straight(left(1, 1), two(odd, span, span + 1)))
        return carry

    lax.fori_loop(0, pairs, step, 0)


NEAR = (0, -1)
REST = (1, 2)
APART = (0, -1, 1, 2)


def collect_kernel(late, place, *refs):
    *got, out, sems = refs
    got = got[1:] if late else got
    half = got[0].shape[0] // 2
    y, z, side = place[0], place[1], place[2]
    copies = []
    buffer = 0
    for part in range(2):
        for near in (NEAR, REST):
            for second in APART[3:] if late else APART[:3]:
                for piece, first in enumerate(near):
                    dy, dz = (first, second) if part == 0 else (second, first)
                    row = lax.rem(y + dy + side, side)
                    column = lax.rem(z + dz + side, side)
                    copies.append(
                        pltpu.make_async_copy(
                            got[buffer].at[piece * half : (piece + 1) * half],
                            out.at[row * side + column, part * half : (part + 1) * half],
                            sems.at[len(copies)],
                        )
                    )
                buffer += 1
    for copy in copies:
        copy.start()
    for copy in copies:
        copy.wait()


def block_copy(got, held, sems, which, block):
    rows = got[which].shape[1]
    at = pl.multiple_of(block * rows, rows)
    return pltpu.make_async_copy(
        got[which].at[block], held.at[which, pl.ds(at, rows)], sems.at[which, block]
    )


def begin(got, held, sems):
    @pl.loop(0, got[0].shape[0])
    def _(block):
        for which in range(2):
            block_copy(got, held, sems, which, block).start()


def folded(total, tile, tiles):
    at = slice(tile * LANES, (tile + 1) * LANES)
    value = total[:, at]
    if (tile + tiles + 1) * LANES <= total.shape[1]:
        value = value + total[:, (tile + tiles) * LANES : (tile + tiles + 1) * LANES]
    return value.astype(BF)


def pack_columns(c_ref, columns, half):
    count = c_ref.shape[1] // half
    rest = c_ref.shape[0] - LANES
    for tile in range(c_ref.shape[1] // LANES):
        block = c_ref[:LANES, tile * LANES : (tile + 1) * LANES].astype(F32).T.astype(BF)
        step = 16
        for k in range(LANES // step):
            row = tile * LANES + k * step
            columns[row // half, row % half : row % half + step, :] = block[k * step : (k + 1) * step]
    for piece in range(count):
        tile, off = divmod(piece * half, LANES)
        tail = slice(LANES, LANES + rest)
        value = shifted(c_ref[tail, tile * LANES : (tile + 1) * LANES].astype(F32), -off)
        if off + half > LANES:
            more = c_ref[tail, (tile + 1) * LANES : (tile + 2) * LANES].astype(F32)
            value = jnp.where(lane_index() < LANES - off, value, shifted(more, -off))
        columns[piece, half : half + rest, :] = value.astype(BF)


def flipped_tiles(got_ref, turned, half, tile):
    rest = 2 * half - LANES
    group = LANES // rest
    kept = half - rest

    def near(s, begin):
        return shifted(got_ref[s, :half, :].astype(F32), begin)

    def far(s, begin):
        front = shifted(got_ref[s, :half, :].astype(F32), begin - half)
        back = turned[s // group, :half, :]
        back = shifted(back, begin + kept - rest * (s % group))
        return jnp.where(lane_index() >= begin + kept, back, front)

    return laid_out(near, half, tile), laid_out(far, half, tile)


def turn_rest(got_ref, turned, half):
    rest = 2 * half - LANES
    group = LANES // rest
    for k in range(got_ref.shape[0] // group):
        block = jnp.concatenate(
            [got_ref[k * group + m, half : half + rest, :].astype(F32) for m in range(group)], 0
        )
        turned[k] = block.T


def finish_products(c_out, total, tiles):
    for tile in range(tiles):
        c_out[:, tile * LANES : (tile + 1) * LANES] = folded(total, tile, tiles)


def first_kernel(half, tiles, place, x_ref, own_ref, far_ref, *refs):
    *got, c_out, columns, mixed, total, held, sems = refs
    begin(got, held, sems)
    for tile in range(tiles):
        at = slice(tile * LANES, (tile + 1) * LANES)
        x0, x1 = x_ref[:half, at].astype(F32), x_ref[half:, at].astype(F32)
        mix(x0, x1, own_ref, far_ref, mixed, half, tile, tiles)
    total[...] = jnp.zeros_like(total)
    product(got, mixed, total, held, sems, tiles)
    finish_products(c_out, total, tiles)
    pack_columns(c_out, columns, half)


def update(half, tiles, scale, c_ref, back_ref, own_ref, far_ref, mixed, turned, keep):
    turn_rest(back_ref, turned, half)
    for tile in range(tiles):
        at = slice(tile * LANES, (tile + 1) * LANES)
        xs = []
        for channel, flipped in enumerate(flipped_tiles(back_ref, turned, half, tile)):
            rows = slice(channel * half, (channel + 1) * half)
            increment = (c_ref[rows, at].astype(F32) + flipped) * scale
            keep(rows, at, increment)
            xs.append(increment.astype(BF).astype(F32))
        mix(xs[0], xs[1], own_ref, far_ref, mixed, half, tile, tiles)


def middle_kernel(half, tiles, scale, place, c_ref, back_ref, own_ref, far_ref, *refs):
    *got, c_out, run_out, columns, mixed, total, held, sems, turned = refs
    begin(got, held, sems)

    def keep(rows, at, increment):
        run_out[rows, at] = increment

    update(half, tiles, scale, c_ref, back_ref, own_ref, far_ref, mixed, turned, keep)
    total[...] = jnp.zeros_like(total)
    product(got, mixed, total, held, sems, tiles)
    finish_products(c_out, total, tiles)
    pack_columns(c_out, columns, half)


def last_kernel(
    half, tiles, scale, last_scale, place, c_ref, back_ref, run_ref, own_ref, far_ref, *refs
):
    *got, leave, stay, columns, mixed, total, held, sems, turned, run, turned_all = refs
    begin(got, held, sems)

    def keep(rows, at, increment):
        run[rows, at] = run_ref[rows, at] + increment

    update(half, tiles, scale, c_ref, back_ref, own_ref, far_ref, mixed, turned, keep)
    total[...] = jnp.zeros_like(total)
    product(got, mixed, total, held, sems, tiles)
    first = place[3] != 0
    filler = jnp.zeros((LANES - half, LANES), F32)
    for tile in range(tiles):
        at = slice(tile * LANES, (tile + 1) * LANES)
        value = folded(total, tile, tiles).astype(F32)
        for channel in range(2):
            block = jnp.concatenate([value[channel * half : (channel + 1) * half], filler])
            turned_all[channel, at, :] = block.T
        both = run[:, at] + value * last_scale
        leave[:, at] = jnp.where(first, both[half:], both[:half]).astype(BF)
        stay[:, at] = jnp.where(first, both[:half], both[half:])
    tall, spare = 2 * half, LANES - half
    high = columns.shape[2]
    for channel in range(2):
        for row in range(columns.shape[1]):
            base = turned_all[channel, row * tall : row * tall + high]
            tail = turned_all[channel, row * tall + high : (row + 1) * tall]
            side = jnp.concatenate([shifted(tail, half), shifted(tail, half - spare)])
            side = jnp.concatenate([side, jnp.zeros((high - side.shape[0], LANES), F32)])
            columns[channel, row] = jnp.where(lane_index() < half, base, side).astype(BF)


def end_kernel(half, scale, first_ref, ham_ref, stay_ref, land_ref, got_ref, out_ref):
    first = first_ref[0] != 0

    spare = LANES - half
    left_over = 2 * half - got_ref.shape[2]

    def piece(s, begin):
        block = got_ref[s % 2, s // 2].astype(F32)
        front = shifted(block[:left_over], begin - half)
        back = shifted(block[left_over : 2 * left_over], begin - half + spare)
        tail = jnp.where(lane_index() >= begin + spare, back, front)
        return jnp.concatenate([shifted(block, begin), tail])

    for tile in range(ham_ref.shape[1] // LANES):
        at = slice(tile * LANES, (tile + 1) * LANES)
        total = ham_ref[:, at].astype(F32) + laid_out(piece, half, tile) * scale
        stay, land = stay_ref[:, at], land_ref[:, at].astype(F32)
        out_ref[:half, at] = total[:half] + jnp.where(first, stay, land)
        out_ref[half:, at] = total[half:] + jnp.where(first, land, stay)


def call(kernel, out_shape, specs, name, scratch=(), cost=None, megabytes=16):
    single = not isinstance(out_shape, (list, tuple))
    return pl.pallas_call(
        kernel,
        out_shape=out_shape,
        in_specs=specs,
        out_specs=VMEM if single else [VMEM] * len(out_shape),
        scratch_shapes=scratch,
        compiler_params=pltpu.CompilerParams(vmem_limit_bytes=megabytes << 20),
        cost_estimate=cost,
        name=name,
    )


def passed(value, axis, apart):
    size = lax.axis_size(axis)
    return lax.ppermute(value, axis, [(i, (i + apart) % size) for i in range(size)])


def both_ways(value, one, other):
    by_one = {0: value, -1: passed(value, one, 1), 1: passed(value, one, -1)}
    by_one[2] = passed(value, one, 2)
    near = jnp.concatenate([by_one[k] for k in NEAR])
    rest = jnp.concatenate([by_one[k] for k in REST])
    near_up, near_down = passed(near, other, 1), passed(near, other, -1)
    rest_up, rest_down = passed(rest, other, 1), passed(rest, other, -1)
    return [
        near, near_up, near_down, passed(near_up, other, 1),
        rest, rest_up, rest_down, passed(rest_down, other, -1),
    ]


def swapped(value):
    return lax.ppermute(value, "hi", [(0, 1), (1, 0)])


def on_device(
    generator, hamiltonian, live_states, pp_occupation, ph_occupation, ph_order, recoupling
):
    row_count = generator.shape[1]
    state_count = generator.shape[2]
    half = row_count // 2
    shard_count = (lax.axis_size("y") * lax.axis_size("z"))
    tiles = state_count // LANES
    sent_tiles = tiles // 2 + 1
    hi = lax.axis_index("hi")
    lo = lax.axis_index("lo")
    my_shard = lax.axis_index(ROW)
    first = hi == 0
    shape = jax.ShapeDtypeStruct
    r0 = recoupling[lo]
    r1 = recoupling[lo + lax.axis_size("lo")]
    positions = jnp.arange(state_count, dtype=jnp.int32)
    share = call(
        functools.partial(pack_kernel, sent_tiles, tiles),
        shape((row_count, sent_tiles * LANES), BF),
        [SMEM, VMEM],
        "pack",
    )(jnp.stack([my_shard * row_count, live_states[0]]), generator[0])
    far_share = swapped(share)
    gathered = lax.all_gather(share, ROW, axis=0, tiled=False)
    pieces = both_ways(far_share[:half], "y", "z") + both_ways(far_share[half:], "z", "y")
    ph_order, ph_occupation, pp_occupation, hamiltonian, live_states, _, _ = (
        lax.optimization_barrier(
            (
                ph_order, ph_occupation, pp_occupation, hamiltonian, live_states,
                pieces[4], pieces[12],
            )
        )
    )
    live_count = live_states[0]
    column_alive = positions < live_count
    row_alive = my_shard * row_count + jnp.arange(row_count, dtype=jnp.int32) < live_count
    block_alive = row_alive[:, None] & column_alive[None, :]
    place = jnp.stack(
        [lax.axis_index("y"), lax.axis_index("z"), lax.axis_size("y"), first.astype(jnp.int32)]
    ).astype(jnp.int32)
    early = [piece for k, piece in enumerate(pieces) if k % 4 != 3]
    late = [piece for k, piece in enumerate(pieces) if k % 4 == 3]

    def collect(is_late, parts, aliases):
        return pl.pallas_call(
            functools.partial(collect_kernel, is_late),
            out_shape=shape(gathered.shape, BF),
            in_specs=[SMEM, pl.BlockSpec(memory_space=pl.ANY)]
            + [VMEM if is_late else pl.BlockSpec(memory_space=pl.ANY)] * (len(parts) - 1),
            out_specs=pl.BlockSpec(memory_space=pl.ANY),
            scratch_shapes=[pltpu.SemaphoreType.DMA((2 * len(parts),))],
            input_output_aliases=aliases,
            cost_estimate=pl.CostEstimate(
                flops=0, bytes_accessed=2 * sum(x.size for x in parts), transcendentals=0
            ),
            compiler_params=pltpu.CompilerParams(vmem_limit_bytes=(50 if is_late else 32) << 20),
            name="collect",
        )(place, *parts)

    collected = collect(False, early, {})
    collected = collect(True, [collected] + late, {1: 0})
    gathered = [gathered, collected]

    pp = jnp.where(column_alive, pp_occupation[0], 0)
    ph = jnp.zeros((state_count,), jnp.int32).at[ph_order[0]].set(ph_occupation[0])
    ph = jnp.where(column_alive, ph, 0)
    mine = jnp.stack([pp, ph]).astype(F32)
    other = swapped(mine)
    d0, n0 = jnp.where(first, mine, other)
    d1, n1 = jnp.where(first, other, mine)
    a0 = d0 + r0[0] ** 3 * n0 + r1[1] ** 3 * n1
    a1 = d1 + r1[0] ** 3 * n1 + r0[1] ** 3 * n0
    p = r0[0] ** 2 * r0[1] * n0 + r1[1] ** 2 * r1[0] * n1
    q = r1[0] ** 2 * r1[1] * n1 + r0[1] ** 2 * r0[0] * n0
    zero_set = jnp.stack([a0, p, p, q])
    one_set = jnp.stack([p, q, q, a1])
    own_set = jnp.where(first, zero_set, one_set)
    far_set = jnp.where(first, one_set, zero_set)

    own_ham = jnp.where(block_alive, hamiltonian[0], jnp.zeros_like(hamiltonian[0]))
    keep = lax.dynamic_slice_in_dim(own_ham, hi * half, half, 0)
    gone = lax.dynamic_slice_in_dim(own_ham, (1 - hi) * half, half, 0)
    came = swapped(gone)
    current = jnp.concatenate([jnp.where(first, keep, came), jnp.where(first, came, keep)])

    wide = (tiles + sent_tiles - 1) * LANES
    rest = row_count - LANES
    destinations = 2 * shard_count
    scratch = [
        pltpu.VMEM((2, row_count, wide), BF),
        pltpu.VMEM((row_count, wide), F32),
        pltpu.VMEM((2, state_count, sent_tiles * LANES), BF),
        pltpu.SemaphoreType.DMA((2, shard_count)),
    ]
    more = [pltpu.VMEM((destinations * rest // LANES, LANES, LANES), F32)]
    c_shape = shape((row_count, state_count), BF)
    run_shape = shape((row_count, state_count), F32)
    sent_shape = shape((destinations, half + rest, LANES), BF)
    cost = pl.CostEstimate(
        flops=4 * row_count * state_count * state_count,
        bytes_accessed=4 * state_count * sent_tiles * LANES,
        transcendentals=0,
    )

    def exchanged(columns):
        return lax.all_to_all(columns, ("y", "z", "hi"), split_axis=0, concat_axis=0, tiled=True)

    combined, columns = call(
        functools.partial(first_kernel, half, tiles),
        [c_shape, sent_shape],
        [SMEM] + [VMEM] * 3 + [HBM] * len(gathered),
        "first",
        scratch,
        cost,
        48,
    )(place, current, own_set, far_set, *gathered)
    back = exchanged(columns)
    combined, running, columns = call(
        functools.partial(middle_kernel, half, tiles, -1.0),
        [c_shape, run_shape, sent_shape],
        [SMEM] + [VMEM] * 4 + [HBM] * len(gathered),
        "middle",
        scratch + more,
        cost,
        48,
    )(place, combined, back, own_set, far_set, *gathered)
    back = exchanged(columns)
    which = first.astype(jnp.int32)[None]
    leaving, staying, blocks = call(
        functools.partial(last_kernel, half, tiles, -0.5, -1.0 / TERMS),
        [
            shape((half, state_count), BF),
            shape((half, state_count), F32),
            shape((2, shard_count, half + rest, LANES), BF),
        ],
        [SMEM] + [VMEM] * 5 + [HBM] * len(gathered),
        "last",
        scratch
        + more
        + [pltpu.VMEM((row_count, state_count), F32), pltpu.VMEM((2, state_count, LANES), F32)],
        cost,
        52,
    )(place, combined, back, running, own_set, far_set, *gathered)
    landed = swapped(leaving)
    got = lax.all_to_all(
        blocks.reshape(destinations, half + rest, LANES),
        ("hi", "y", "z"),
        split_axis=0,
        concat_axis=0,
        tiled=True,
    )
    result = call(
        functools.partial(end_kernel, half, -1.0 / TERMS),
        shape((row_count, state_count), F32),
        [SMEM] + [VMEM] * 4,
        "finish",
    )(which, own_ham, staying, landed, got.reshape(2, shard_count, half + rest, LANES))
    return result[None]


def solution(mesh):
    chans, rows = mesh.devices.shape
    side = math.isqrt(rows)
    pairs = Mesh(
        mesh.devices.reshape(2, chans // 2, side, rows // side), ("hi", "lo", "y", "z")
    )
    chan = ("hi", "lo")
    placed = (
        P(chan, ROW, None),
        P(chan, ROW, None),
        P(chan),
        P(chan, None),
        P(chan, None),
        P(chan, None),
        P(),
    )
    return jax.shard_map(
        on_device, mesh=pairs, in_specs=placed, out_specs=P(chan, ROW, None), check_vma=False
    )
```
